32 devices in a mesh: seq: 2 (over y), blk: 16 (over z, x, core).
Axes of the slice: x: 2, y: 2, z: 4, core: 2. Of those that a mesh axis runs over, the one named last changes fastest.
Arguments:
- residual: bfloat16 [16, 256, 1024], P('blk', 'seq'), may hold values from -6 to 6
- segments: int32 [4096], replicated, may hold values from 0 to 15, never falling along the last dimension, each value on 1 to 512 neighbouring positions
- routes: int32 [16, 256, 8], P('blk', 'seq'), may hold values from 0 to 15, all different within a row; in each aligned block of 128 rows (0 to 127, 128 to 255, ..., all dimensions but the last counted through in order) at most 96 rows name the same one
- w_query: bfloat16 [1024, 1024], P(('seq', 'blk')), may hold values from -0.1875 to 0.1875
- w_key: bfloat16 [1024, 512], P(('seq', 'blk')), may hold values from -0.1875 to 0.1875
- w_value: bfloat16 [1024, 512], P(('seq', 'blk')), may hold values from -0.1875 to 0.1875
- w_out: bfloat16 [1024, 1024], P(None, ('seq', 'blk')), may hold values from -0.75 to 0.75
- w_router: bfloat16 [1024, 16], P(('seq', 'blk')), may hold values from -0.09375 to 0.09375
- attn_gain: bfloat16 [1024], P(('seq', 'blk')), may hold values from 0.5 to 1.5
- moe_gain: bfloat16 [1024], P(('seq', 'blk')), may hold values from 0.5 to 1.5
- w_gate: bfloat16 [16, 1024, 512], P('blk', 'seq'), may hold values from -0.1875 to 0.1875
- w_up: bfloat16 [16, 1024, 512], P('blk', 'seq'), may hold values from -0.1875 to 0.1875
- w_down: bfloat16 [16, 512, 1024], P('blk', 'seq'), may hold values from -1 to 1
- cotangent: bfloat16 [16, 256, 1024], P('blk', 'seq'), may hold values from -6 to 6
Outputs:
- block_out: bfloat16 [16, 256, 1024], P('blk', 'seq')
- grad_input: float32 [16, 256, 1024], P('blk', 'seq')
- grad_query: float32 [1024, 1024], P(('seq', 'blk'))
- grad_key: float32 [1024, 512], P(('seq', 'blk'))
- grad_value: float32 [1024, 512], P(('seq', 'blk'))
- grad_out: float32 [1024, 1024], P(None, ('seq', 'blk'))
- grad_router: float32 [1024, 16], P(('seq', 'blk'))
- grad_attn_gain: float32 [1024], P(('seq', 'blk'))
- grad_moe_gain: float32 [1024], P(('seq', 'blk'))
- grad_gate: float32 [16, 1024, 512], P('blk', 'seq')
- grad_up: float32 [16, 1024, 512], P('blk', 'seq')
- grad_down: float32 [16, 512, 1024], P('blk', 'seq')
The draws below stay inside these ranges and needn't reach their ends.
Inputs may be any that keep to these rules, and one draw needn't show every extreme that they name: `routes`: among the 128 consecutive tokens of one device no expert is named by more than 96 tokens, a bound that some block reaches. `segments`: document numbers never fall along the sequence; each document has 1 to 512 tokens and one has exactly 512.
All inputs are finite; a program needn't handle non-finite values.
Results may differ from the reference program's by a relative error of at most 0.02.
Values may be sent and summed in bfloat16 or wider, within the bound.
No kernel may reach another device: no remote copies, remote signals or barrier semaphores. Data moves between devices by JAX's collectives and lax.ppermute only.
A program may use at most 128 MiB of HBM per device.

```python
import math
import jax
import jax.numpy as jnp
import numpy as np
from jax import lax

D = 1024
HEADS = 16
KV_HEADS = 8
HEAD_DIM = 64
FF = 512
TOP = 8
TOK_DEV = 128
EXPERTS = 16
BLOCK_ROWS = 256
TOKENS = 4096
CAP = 96
DOCS = 16
DOC_MOST = 512
N_SEQ = 2
N_BLK = 16


def block_levels(rng, shape, shards, low, high):
    loudness = 1.0
    for dim, shards_of in shards:
        steps = jax.random.uniform(jax.random.fold_in(jax.random.fold_in(rng, 6), dim), (shards_of,), jnp.float32, low / len(shards), high / len(shards))
        loudness = loudness * jnp.repeat(jnp.exp(steps), shape[dim] // shards_of).reshape((-1,) + (1,) * (len(shape) - 1 - dim))
    return loudness


def length_profile(amount, total, most, lean):
    weights = [(1 << 20) // math.isqrt(grade ** lean) + 1 for grade in range(2, amount + 1)]
    spare, given = total - most - (amount - 1), [1] * (amount - 1)
    while spare > 0:
        candidates = [i for i in range(amount - 1) if given[i] < most]
        whole, remaining = sum([weights[i] for i in candidates]), spare
        for i in candidates:
            addition = min(most - given[i], max(1, remaining * weights[i] // whole), spare)
            given[i] = given[i] + addition
            spare = spare - addition
    return np.array([most] + given)


def uneven(rng, number_of, total, reach, lean):
    if number_of == 2:
        one = jax.random.randint(rng, (), max(1, total - reach), min(reach, total - 1) + 1)
        return jnp.stack([one, total - one])
    sizes = jnp.asarray(length_profile(number_of, total, reach, lean), jnp.int32)
    twos = (number_of - 1) // 2
    donor, sink = sizes[1:1 + 2 * twos:2], sizes[2:2 + 2 * twos:2]
    margin = jnp.minimum(donor - 1, reach - sink)
    moved = jax.random.randint(jax.random.fold_in(rng, 1), (twos,), 0, 1 << 20) % (margin + 1)
    sizes = sizes.at[1:1 + 2 * twos:2].set(donor - moved).at[2:2 + 2 * twos:2].set(sink + moved)
    return sizes[jax.random.permutation(jax.random.fold_in(rng, 2), number_of)]


def routed_block(key, own, number, rows, number_of, top, reach, slope):
    order = jax.random.permutation(key, number_of)
    packed, common = load_shares(number_of, rows * top, reach, slope, True), load_shares(number_of, rows * top, reach, slope, False)
    places = jnp.arange(number_of)

    def named(tallies, offset_by):
        used = int((tallies > 0).sum())
        fixed = max(1, used // 4)
        shifted = fixed + (places - fixed + offset_by * (used - fixed)) % max(1, number_of - fixed)
        return jnp.zeros((number_of,), jnp.int32).at[order[jnp.where(places < fixed, places, shifted)]].set(jnp.asarray(tallies, jnp.int32))

    tallies = jnp.where(number % 4 == 0, named(packed, number // 4), named(common, number - number // 4 - 1))
    mixed = jax.random.permutation(jax.random.fold_in(own, 3), number_of)
    donor, receiver = mixed[0:number_of // 2 * 2:2], mixed[1:number_of // 2 * 2:2]
    slack = jnp.minimum(tallies[donor] - 1, reach - tallies[receiver]) // 2
    slack = jnp.where((donor == order[0]) | (receiver == order[0]) | (tallies[receiver] == 0), 0, jnp.maximum(slack, 0))
    shifted = jax.random.randint(jax.random.fold_in(own, 4), (number_of // 2,), 0, 1 << 20) % (slack + 1)
    tallies = tallies.at[donor].add(-shifted).at[receiver].add(shifted)
    items = jnp.searchsorted(jnp.cumsum(tallies), jnp.arange(rows * top), side="right").astype(jnp.int32)
    listing = items.reshape(top, rows).T
    listing = listing[jax.random.permutation(jax.random.fold_in(own, 1), rows)]
    offset_by = jax.random.randint(jax.random.fold_in(own, 2), (rows, 1), 0, top)
    return jnp.take_along_axis(listing, (jnp.arange(top)[None, :] + offset_by) % top, axis=1)


def load_shares(amount, total, limit, lean, full):
    weights = [(1 << 20) // math.isqrt(standing ** lean) + 1 for standing in range(1, amount + 1)]
    largest = limit if full else min(limit, max(-(-total // amount), total * weights[0] // sum(weights)))
    least = 1 if total - largest >= amount - 1 else 0
    counts, spare = [largest] + [least] * (amount - 1), total - largest - least * (amount - 1)
    while spare > 0:
        free = [i for i in range(1, amount) if counts[i] < largest] or [i for i in range(1, amount) if counts[i] < limit]
        pool, left = sum([weights[i] for i in free]), spare
        for i in free:
            more = min(limit - counts[i], max(1, left * weights[i] // pool), spare)
            counts[i] = counts[i] + more
            spare = spare - more
    return np.array(counts)


def centred(own_key, extent, scale, bound, shards=(), held_as=jnp.bfloat16):
    drawn = jax.random.normal(own_key, extent, jnp.float32) * scale
    if len(shards) > 0:
        drawn = block_levels(own_key, extent, shards, -0.22, 0.18) * drawn
    return jnp.clip(drawn, min=-bound, max=bound).astype(held_as)


def setup_inputs(seed: int = 0) -> dict:
    seeds = jax.random.split(jax.random.key(seed), 15)
    residual = centred(seeds[0], (N_BLK, BLOCK_ROWS, D), 1.0, 6.0, ((0, 16), (1, 2)))
    segments = jnp.searchsorted(jnp.cumsum(uneven(seeds[1], DOCS, TOKENS, DOC_MOST, 2)), jnp.arange(TOKENS), side="right").astype(jnp.int32)
    routes_keys = jax.random.split(jax.random.fold_in(seeds[2], 1), N_BLK * BLOCK_ROWS // TOK_DEV)
    routes_turns = jax.random.permutation(jax.random.fold_in(seeds[2], 3), N_BLK * BLOCK_ROWS // TOK_DEV)
    routes = jax.vmap(lambda own, number: routed_block(jax.random.fold_in(seeds[2], 2), own, number, TOK_DEV, EXPERTS, TOP, CAP, 1))(routes_keys, routes_turns).reshape((N_BLK, BLOCK_ROWS, TOP))
    w_query = centred(seeds[3], (D, HEADS * HEAD_DIM), D ** -0.5, 0.1875, ((0, 32),))
    w_key = centred(seeds[4], (D, KV_HEADS * HEAD_DIM), D ** -0.5, 0.1875, ((0, 32),))
    w_value = centred(seeds[5], (D, KV_HEADS * HEAD_DIM), D ** -0.5, 0.1875, ((0, 32),))
    w_out = centred(seeds[6], (HEADS * HEAD_DIM, D), 64 ** -0.5, 0.75, ((1, 32),))
    w_router = centred(seeds[7], (D, EXPERTS), (4 * D) ** -0.5, 0.09375, ((0, 32),))
    attn_gain = jnp.clip(1.0 + 0.1 * jax.random.normal(seeds[8], (D,), jnp.float32), 0.5, 1.5).astype(jnp.bfloat16)
    moe_gain = jnp.clip(1.0 + 0.1 * jax.random.normal(seeds[9], (D,), jnp.float32), 0.5, 1.5).astype(jnp.bfloat16)
    w_gate = centred(seeds[10], (EXPERTS, D, FF), D ** -0.5, 0.1875, ((0, 16), (1, 2)))
    w_up = centred(seeds[11], (EXPERTS, D, FF), D ** -0.5, 0.1875, ((0, 16), (1, 2)))
    w_down = centred(seeds[12], (EXPERTS, FF, D), (FF // 16) ** -0.5, 1.0, ((0, 16), (1, 2)))
    cotangent = centred(seeds[13], (N_BLK, BLOCK_ROWS, D), 1.0, 6.0, ((0, 16), (1, 2)))
    return dict(residual=residual, segments=segments, routes=routes, w_query=w_query, w_key=w_key, w_value=w_value, w_out=w_out, w_router=w_router, attn_gain=attn_gain, moe_gain=moe_gain, w_gate=w_gate, w_up=w_up, w_down=w_down, cotangent=cotangent)


@jax.custom_vjp
def low(v):
    return lax.optimization_barrier(v.astype(jnp.bfloat16)).astype(jnp.float32)

@jax.custom_vjp
def low_back(v):
    return v

def low_keep(v):
    return (low(v), None)

def low_pass(kept, grad):
    return (grad,)

def back_keep(v):
    return (v, None)

def back_low(kept, grad):
    return (low(grad),)
low.defvjp(low_keep, low_pass)
low_back.defvjp(back_keep, back_low)
highest = lax.Precision.HIGHEST
epsilon = 1e-06
neg_large = -1e+30
query_block = 256

def rms_norm(values, gain):
    return values * lax.rsqrt(lax.optimization_barrier(jnp.mean(values * values, axis=-1, keepdims=True)) + epsilon) * gain

def rope_tables(positions, width):
    half_dim = width // 2
    inverse = jnp.exp(jnp.arange(half_dim, dtype=jnp.float32) * (-2.0 * math.log(10000.0) / width))
    angles = positions.astype(jnp.float32)[:, None] * inverse[None, :]
    return (jnp.cos(angles), jnp.sin(angles))

def rotate(vector, cos_part, sin_part):
    half_dim = vector.shape[-1] // 2
    first_half = vector[..., :half_dim]
    second = vector[..., half_dim:]
    cos_b = cos_part[:, None, :]
    sin_b = sin_part[:, None, :]
    return jnp.concatenate([first_half * cos_b - second * sin_b, second * cos_b + first_half * sin_b], axis=-1)

def attention(queries, key_rows, value_rows, segments):
    group_size = HEADS // KV_HEADS
    window = DOC_MOST + query_block
    score_scale = HEAD_DIM ** (-0.5)
    block_count = TOKENS // query_block
    starts = jnp.arange(block_count, dtype=jnp.int32) * query_block
    blocks = queries.reshape(block_count, query_block, KV_HEADS, group_size, HEAD_DIM)
    offsets = jnp.arange(query_block, dtype=jnp.int32)
    key_offsets = jnp.arange(window, dtype=jnp.int32)

    def attend_block(block_args):
        query_part, start = block_args
        key_start = jnp.maximum(start + query_block - window, 0).astype(jnp.int32)
        key_part = lax.dynamic_slice_in_dim(key_rows, key_start, window, 0)
        value_part = lax.dynamic_slice_in_dim(value_rows, key_start, window, 0)
        query_seg = lax.dynamic_slice_in_dim(segments, start.astype(jnp.int32), query_block, 0)
        key_seg = lax.dynamic_slice_in_dim(segments, key_start, window, 0)
        visible = ((key_start + key_offsets)[None, :] <= (start + offsets)[:, None]) & (key_seg[None, :] == query_seg[:, None])
        visible = visible[:, None, None, :]
        scores = low_back(jnp.einsum('qhgd,khd->qhgk', query_part, key_part, precision=highest) * score_scale)
        masked = jnp.where(visible, scores, neg_large)
        row_max = lax.optimization_barrier(jnp.max(masked, axis=-1, keepdims=True))
        log_total = row_max + jnp.log(lax.optimization_barrier(jnp.sum(jnp.exp(masked - row_max), axis=-1, keepdims=True)))
        weights = low(jnp.where(visible, jnp.exp(masked - log_total), 0.0))
        return jnp.einsum('qhgk,khd->qhgd', weights, value_part, precision=highest)
    mixed = lax.map(jax.checkpoint(attend_block), (blocks, starts))
    return mixed.reshape(TOKENS, HEADS * HEAD_DIM)

def reference(residual, segments, routes, w_query, w_key, w_value, w_out, w_router, attn_gain, moe_gain, w_gate, w_up, w_down, cotangent):
    group_size = HEADS // KV_HEADS
    block_total = N_SEQ * N_BLK
    flat_routes = routes.reshape(block_total, TOK_DEV, TOP)
    positions = jnp.arange(TOKENS, dtype=jnp.int32)
    cos_part, sin_part = rope_tables(positions, HEAD_DIM)

    def forward(stream, query_w, key_w, value_w, out_w, router_w, gain_one, gain_two, gate_w, up_w, down_w):
        normed = low(rms_norm(stream, gain_one))
        q_pre = low_back(jnp.dot(normed, query_w, precision=highest)).reshape(TOKENS, HEADS, HEAD_DIM)
        k_pre = low_back(jnp.dot(normed, key_w, precision=highest)).reshape(TOKENS, KV_HEADS, HEAD_DIM)
        value_rows = low_back(low(jnp.dot(normed, value_w, precision=highest))).reshape(TOKENS, KV_HEADS, HEAD_DIM)
        queries = low_back(low(rotate(q_pre, cos_part, sin_part))).reshape(TOKENS, KV_HEADS, group_size, HEAD_DIM)
        key_rows = low_back(low(rotate(k_pre, cos_part, sin_part)))
        mixed = low_back(low(attention(queries, key_rows, value_rows, segments)))
        middle = stream + low_back(jnp.dot(mixed, out_w, precision=highest))
        second_in = low(rms_norm(middle, gain_two))

        def expert_block(block_args):
            normed_rows, route_rows = block_args
            chosen = (route_rows[:, :, None] == jnp.arange(EXPERTS, dtype=jnp.int32)[None, None, :]).astype(jnp.float32)
            member = lax.optimization_barrier(jnp.sum(chosen, axis=1))
            slot_rank = jnp.cumsum(member, axis=0) - member
            slot_hit = member.T[:, None, :] * (slot_rank.T[:, None, :] == jnp.arange(CAP, dtype=jnp.float32)[None, :, None]).astype(jnp.float32)
            logits = jnp.dot(normed_rows, router_w, precision=highest)
            picked = jnp.einsum('tke,te->tk', chosen, logits, precision=highest)
            gate_prob = jax.nn.softmax(picked, axis=-1)
            gate_table = jnp.einsum('tk,tke->te', gate_prob, chosen, precision=highest)
            inputs = low_back(jnp.einsum('ect,td->ecd', slot_hit, normed_rows, precision=highest))
            gate_pre = low_back(jnp.einsum('ecd,edf->ecf', inputs, gate_w, precision=highest))
            up_pre = low_back(jnp.einsum('ecd,edf->ecf', inputs, up_w, precision=highest))
            hidden = low(jax.nn.silu(gate_pre) * up_pre)
            result = low_back(low(jnp.einsum('ecf,efd->ecd', hidden, down_w, precision=highest)))
            per_expert = jnp.einsum('ect,ecd->ted', slot_hit, result, precision=highest)
            return lax.optimization_barrier(jnp.sum(gate_table[:, :, None] * per_expert, axis=1))
        moe_out = lax.map(jax.checkpoint(expert_block), (second_in.reshape(block_total, TOK_DEV, D), flat_routes))
        return middle + moe_out.reshape(TOKENS, D)
    floats = (residual.reshape(TOKENS, D).astype(jnp.float32), w_query.astype(jnp.float32), w_key.astype(jnp.float32), w_value.astype(jnp.float32), w_out.astype(jnp.float32), w_router.astype(jnp.float32), attn_gain.astype(jnp.float32), moe_gain.astype(jnp.float32), w_gate.astype(jnp.float32), w_up.astype(jnp.float32), w_down.astype(jnp.float32))
    final, pullback = jax.vjp(forward, *floats)
    grads = pullback(cotangent.reshape(TOKENS, D).astype(jnp.float32))
    return (final.astype(jnp.bfloat16).reshape(N_BLK, BLOCK_ROWS, D), grads[0].reshape(N_BLK, BLOCK_ROWS, D), grads[1], grads[2], grads[3], grads[4], grads[5], grads[6], grads[7], grads[8], grads[9], grads[10])
```

```python
import functools
import math

import jax
import jax.numpy as jnp
from jax import lax
from jax.experimental import pallas as pl
from jax.experimental.pallas import tpu as pltpu
from jax.sharding import PartitionSpec as P

HEADS = 16
KV_HEADS = 8
HEAD_DIM = 64
LANES = 128

f32 = jnp.float32
bf16 = jnp.bfloat16
epsilon = 1e-06
neg_large = -1e30


def swap_with(value, axis, mask):
    if mask == 0:
        return value
    count = lax.axis_size(axis)
    return lax.ppermute(value, axis, [(i, i ^ mask) for i in range(count)])


def shifted(value, axis, steps):
    count = lax.axis_size(axis)
    leading, last = (max(0, -steps), min(count, count - steps))
    return lax.ppermute(value, axis, [(i, i + steps) for i in range(leading, last)])


def gather_seq(value):
    count = lax.axis_size("seq")
    me = lax.axis_index("seq")
    whole = jnp.zeros((count,) + value.shape, value.dtype)
    for k in range(count):
        piece = swap_with(value, "seq", k)
        whole = lax.dynamic_update_index_in_dim(whole, piece, me ^ k, 0)
    return whole


def exchange_seq(parts):
    count = lax.axis_size("seq")
    me = lax.axis_index("seq")
    return [
        swap_with(lax.dynamic_index_in_dim(parts, me ^ k, 0, keepdims=False), "seq", k)
        for k in range(count)
    ]


def in_seq_order(pieces):
    me = lax.axis_index("seq")
    whole = jnp.zeros((len(pieces),) + pieces[0].shape, pieces[0].dtype)
    for k, piece in enumerate(pieces):
        whole = lax.dynamic_update_index_in_dim(whole, piece, me ^ k, 0)
    return whole


def gather_blk(value):
    groups = lax.axis_size("blk") // 4
    chunks = []
    for k in range(groups):
        far = swap_with(value, "blk", 4 * k)
        pair = jnp.stack([far, swap_with(far, "blk", 2)])
        chunks.append((pair, swap_with(pair, "blk", 1)))
    return chunks


def reduce_chunk(k, keep, send):
    total = (keep.astype(f32) + swap_with(send, "blk", 1).astype(f32)).astype(keep.dtype)
    near = (total[0].astype(f32) + swap_with(total[1], "blk", 2).astype(f32)).astype(keep.dtype)
    return swap_with(near, "blk", 4 * k)


def reduce_blk(terms):
    groups = lax.axis_size("blk") // 4
    total = None
    for k in reversed(range(groups)):
        piece = reduce_chunk(k, terms[4 * k : 4 * k + 2], terms[4 * k + 2 : 4 * k + 4]).astype(f32)
        total = piece if total is None else total + piece
    return total


def call(body, out_shape, **options):
    return pl.pallas_call(
        body,
        out_shape=out_shape,
        compiler_params=pltpu.CompilerParams(vmem_limit_bytes=40 * 1024 * 1024),
        **options,
    )


def shape_of(dims, dtype):
    return jax.ShapeDtypeStruct(dims, dtype)


def lane_ids(shape):
    return lax.broadcasted_iota(jnp.int32, shape, len(shape) - 1)


def half_swap(tile):
    lanes = lane_ids(tile.shape)
    return jnp.where(lanes % 64 < 32, pltpu.roll(tile, 96, 1), pltpu.roll(tile, 32, 1))


def nt(a, b):
    return lax.dot_general(a, b, (((1,), (1,)), ((), ())), preferred_element_type=f32)


def tn(a, b):
    return lax.dot_general(a, b, (((0,), (0,)), ((), ())), preferred_element_type=f32)


def nn(a, b):
    return jnp.dot(a, b, preferred_element_type=f32)


def project_body(q_cols, kv_cols, gain_lane, x_ref, w_ref, cq, sq, ck, sk, q_ref, kv_ref, normed_ref):
    x = x_ref[...].astype(f32)
    inverse = lax.rsqrt(jnp.mean(x * x, axis=-1, keepdims=True) + epsilon)
    cols = q_cols + kv_cols
    pick = (lane_ids((8, LANES)) == gain_lane).astype(bf16)
    gain = nt(pick, w_ref[:, cols : cols + LANES])[0:1, :]
    normed = (x * inverse * gain).astype(bf16)
    normed_ref[...] = normed
    for first in range(0, cols, LANES):
        tile = nn(normed, w_ref[:, first : first + LANES])
        if first < q_cols:
            tile = tile * cq[...] + half_swap(tile) * sq[...]
            q_ref[:, first : first + LANES] = tile.astype(bf16)
        else:
            tile = tile * ck[...] + half_swap(tile) * sk[...]
            kv_ref[:, first - q_cols : first - q_cols + LANES] = tile.astype(bf16)


def visible_keys(rows, keys, behind, first_row, seg_q, seg_k):
    key_ids = lax.broadcasted_iota(jnp.int32, (rows, keys), 1) - behind
    row_ids = lax.broadcasted_iota(jnp.int32, (rows, keys), 0) + first_row
    return (key_ids <= row_ids) & (seg_q == seg_k)


def attend_body(behind, scale, q_ref, kv_ref, seg_q, seg_k, out_ref, lse_ref):
    rows, keys = q_ref.shape[0], kv_ref.shape[0]
    visible = visible_keys(rows, keys, behind, pl.program_id(1) * rows, seg_q[...], seg_k[...])
    q = q_ref[...]
    kv = kv_ref[...]
    low = lane_ids(q.shape) < 64
    outs, lses = [], []
    for half in range(2):
        turned = (pltpu.roll(q.astype(f32), 64, 1) if half else q.astype(f32))
        head = jnp.where(low, turned, 0.0).astype(bf16)
        scores = jnp.where(visible, nt(head, kv) * scale, neg_large)
        most = jnp.max(scores, axis=-1, keepdims=True)
        weights = jnp.exp(scores - most)
        total = jnp.sum(weights, axis=-1, keepdims=True)
        outs.append(nn(weights.astype(bf16), kv) / total)
        lses.append(most + jnp.log(total))
    out_ref[...] = jnp.where(low, pltpu.roll(outs[0], 64, 1), outs[1]).astype(bf16)
    lse_ref[...] = jnp.where(low, lses[0], lses[1])


def attend_back_body(
    behind, scale, q_ref, kv_ref, mixed_ref, grad_ref, lse_ref, seg_q, seg_k, cq, sq, dq_ref, dkv_ref
):
    rows, keys = q_ref.shape[0], kv_ref.shape[0]
    visible = visible_keys(rows, keys, behind, pl.program_id(1) * rows, seg_q[...], seg_k[...])
    q = q_ref[...].astype(f32)
    kv = kv_ref[...]
    grad = grad_ref[...].astype(f32)
    low = lane_ids(q.shape) < 64
    product = grad * mixed_ref[...].astype(f32)
    lse = lse_ref[...]
    dqs = []
    dkv = jnp.zeros((keys, LANES), f32)
    for half in range(2):
        head = jnp.where(low, pltpu.roll(q, 64, 1) if half else q, 0.0).astype(bf16)
        grad_head = jnp.where(low, 0.0, grad if half else pltpu.roll(grad, 64, 1)).astype(bf16)
        mine = (low == (half == 0))
        delta = jnp.sum(jnp.where(mine, product, 0.0), axis=-1, keepdims=True)
        lse_head = lse[:, 64 * half : 64 * half + 1]
        probs = jnp.where(visible, jnp.exp(nt(head, kv) * scale - lse_head), 0.0)
        grad_scores = (probs * (nt(grad_head, kv) - delta)).astype(bf16)
        dqs.append(nn(grad_scores, kv) * scale)
        dkv = dkv + tn(grad_scores, head) * scale + tn(probs.astype(bf16), grad_head)
    dq = jnp.where(low, dqs[0], pltpu.roll(dqs[1], 64, 1)).astype(bf16).astype(f32)
    dq_ref[...] = (dq * cq[...] - half_swap(dq) * sq[...]).astype(bf16)

    @pl.when(pl.program_id(1) == 0)
    def _():
        dkv_ref[...] = dkv

    @pl.when(pl.program_id(1) > 0)
    def _():
        dkv_ref[...] += dkv


def turn_back_body(count, *refs):
    own, others, (ck, sk, out_ref) = refs[0], refs[1 : 1 + count], refs[1 + count :]
    for first in range(0, own.shape[1], LANES):
        span = slice(first, first + LANES)
        total = own[:, span]
        for other in others:
            total = total + other[:, span].astype(f32)
        total = total.astype(bf16).astype(f32)
        out_ref[:, span] = (total * ck[...] - half_swap(total) * sk[...]).astype(bf16)


def middle_body(count, experts, *refs):
    parts = refs[:count]
    res, gain, router, member, middle_ref, wide_ref, prob_ref = refs[count:]
    width = res.shape[1]
    middle = res[...].astype(f32)
    for part in parts:
        middle = middle + part[...].astype(f32)
    middle_ref[...] = middle
    inverse = lax.rsqrt(jnp.mean(middle * middle, axis=-1, keepdims=True) + epsilon)
    normed = (middle * inverse * gain[...]).astype(bf16)
    wide_ref[:, :width] = normed
    inside = member[...] > 0
    logits = jnp.where(inside, nn(normed, router[...]), neg_large)
    raised = jnp.where(inside, jnp.exp(logits - jnp.max(logits, axis=-1, keepdims=True)), 0.0)
    prob = raised / jnp.sum(raised, axis=-1, keepdims=True)
    prob_ref[...] = prob
    high = prob.astype(bf16).astype(f32)
    rest = (prob - high).astype(bf16).astype(f32)
    wide_ref[:, width:] = (high + pltpu.roll(rest, experts, 1)).astype(bf16)


def expert_body(experts, me_ref, *refs):
    (near, far, c0, c1, c2, c3, w_gate, w_up, w_down), outs = refs[:9], refs[9:]
    x_ref, y_keep, y_send, gi_keep, gi_send, hid_ref, ggp_ref, gup_ref, geo_ref = outs
    rows, width = c0.shape[1], c0.shape[2]
    me = me_ref[0]
    spots = ((near, 0), (near, 1), (far, 0), (far, 1))
    probs = []
    for i, (ref, xr) in enumerate(spots):
        x_ref[i * rows : (i + 1) * rows, :] = ref[xr, :, :width]
        extra = ref[xr, :, width:].astype(f32)
        lanes = lane_ids(extra.shape)
        mine = (lanes == me) | (lanes == me + experts)
        probs.append(jnp.sum(jnp.where(mine, extra, 0.0), axis=-1, keepdims=True))
    x = x_ref[...]
    gate = nn(x, w_gate[...])
    up = nn(x, w_up[...])
    sigmoid = 1.0 / (1.0 + jnp.exp(-gate))
    active = gate * sigmoid
    hidden = (active * up).astype(bf16)
    hid_ref[...] = hidden
    result = nn(hidden, w_down[...]).astype(bf16)
    marks = []
    for i, cot in enumerate((c0, c1, c2, c3)):
        part = result[i * rows : (i + 1) * rows, :].astype(f32)
        final = cot[0].astype(f32)
        out = y_send if i >= 2 else y_keep
        out[i % 2] = (probs[i] * part).astype(bf16)
        geo_ref[i * rows : (i + 1) * rows, :] = (probs[i] * final).astype(bf16)
        marks.append(jnp.sum(part * final, axis=-1, keepdims=True))
    grad_hidden = nt(geo_ref[...], w_down[...])
    ggp = (grad_hidden * up * sigmoid * (1.0 + gate * (1.0 - sigmoid))).astype(bf16)
    gup = (grad_hidden * active).astype(bf16)
    ggp_ref[...] = ggp
    gup_ref[...] = gup
    grad_in = (nt(ggp, w_gate[...]) + nt(gup, w_up[...])).astype(bf16)
    for i in range(4):
        out = gi_send if i >= 2 else gi_keep
        out[i % 2, :, :width] = grad_in[i * rows : (i + 1) * rows, :]
        high = marks[i].astype(bf16).astype(f32)
        lanes = lane_ids((rows, LANES))
        extra = jnp.where(lanes == me, high, 0.0) + jnp.where(lanes == me + experts, marks[i] - high, 0.0)
        out[i % 2, :, width:] = extra.astype(bf16)


def middle_back_body(count, experts, *refs):
    parts = refs[:count]
    middle_ref, prob_ref, cot, gain, router, grad_ref, branch_ref, pack_ref = refs[count:]
    width = cot.shape[1]
    total = parts[0][...].astype(f32)
    for part in parts[1:]:
        total = total + part[...].astype(f32)
    extra = total[:, width:]
    marks = extra + pltpu.roll(extra, LANES - experts, 1)
    prob = prob_ref[...]
    weighted = jnp.where(prob > 0, prob * marks, 0.0)
    spread = jnp.sum(weighted, axis=-1, keepdims=True)
    grad_logits = weighted - prob * spread
    high = grad_logits.astype(bf16)
    rest = (grad_logits - high.astype(f32)).astype(bf16)
    grad_normed = total[:, :width] + nt(high, router[...]) + nt(rest, router[...])
    middle = middle_ref[...]
    inverse = lax.rsqrt(jnp.mean(middle * middle, axis=-1, keepdims=True) + epsilon)
    unit = middle * inverse
    scaled = grad_normed * gain[...]
    grad = cot[...].astype(f32) + inverse * (
        scaled - unit * jnp.mean(scaled * unit, axis=-1, keepdims=True)
    )
    grad_ref[...] = grad
    branch_ref[...] = grad.astype(bf16)
    normed = (unit * gain[...]).astype(bf16)
    pack = tn(high, normed) + tn(rest, normed)
    gain_row = jnp.sum(grad_normed * unit, axis=0, keepdims=True)
    at_gain = lax.broadcasted_iota(jnp.int32, pack.shape, 0) == experts
    pack_ref[...] = jnp.where(at_gain, gain_row, pack).astype(bf16)


def input_back_body(count, *refs):
    parts = refs[:count]
    res, grad_middle, gain, out_ref = refs[count:]
    grad_normed = parts[0][...].astype(f32)
    for part in parts[1:]:
        grad_normed = grad_normed + part[...].astype(f32)
    x = res[...].astype(f32)
    inverse = lax.rsqrt(jnp.mean(x * x, axis=-1, keepdims=True) + epsilon)
    unit = x * inverse
    scaled = grad_normed * gain[...]
    out_ref[...] = grad_middle[...] + inverse * (
        scaled - unit * jnp.mean(scaled * unit, axis=-1, keepdims=True)
    )


def rope_tables(positions):
    half_dim = HEAD_DIM // 2
    inverse = jnp.exp(jnp.arange(half_dim, dtype=f32) * (-2.0 * math.log(10000.0) / HEAD_DIM))
    angles = positions.astype(f32)[:, None] * inverse[None, :]
    cos, sin = jnp.cos(angles), jnp.sin(angles)
    one, zero = jnp.ones_like(cos), jnp.zeros_like(sin)
    join = functools.partial(jnp.concatenate, axis=1)
    return (
        join([cos, cos, cos, cos]),
        join([-sin, sin, -sin, sin]),
        join([cos, cos, one, one]),
        join([-sin, sin, zero, zero]),
    )


def per_device(
    residual, segments, routes, w_query, w_key, w_value, w_out, w_router, attn_gain, moe_gain,
    w_gate, w_up, w_down, cotangent,
):
    seqs, blks = lax.axis_size("seq"), lax.axis_size("blk")
    seq_me, blk_me = lax.axis_index("seq"), lax.axis_index("blk")
    toks, width = residual.shape[1], residual.shape[2]
    rows = toks * seqs
    experts = blks
    own_rows = w_query.shape[0]
    kv_local = KV_HEADS // seqs
    q_cols, kv_cols = HEADS // seqs * HEAD_DIM, kv_local * 2 * HEAD_DIM
    scale = HEAD_DIM ** (-0.5)
    tokens = segments.shape[0]
    doc_most = tokens // 8
    hops = min(blks - 1, -(-(doc_most - 1) // rows))
    behind = hops * rows
    keys = behind + rows
    groups = blks // 4
    res = residual[0]
    cot = cotangent[0]

    extra = jnp.concatenate([w_router, attn_gain[:, None], moe_gain[:, None]], axis=1)
    extra = jnp.pad(extra, ((0, 0), (0, LANES - extra.shape[1])))
    by_seq = lambda w: w.reshape(own_rows, seqs, -1).swapaxes(0, 1)
    split_heads = lambda w: by_seq(w).reshape(seqs, own_rows, kv_local, HEAD_DIM)
    kv_parts = jnp.stack([split_heads(w_key), split_heads(w_value)], axis=3)
    out_parts = w_out.reshape(seqs, q_cols, own_rows).swapaxes(1, 2)
    weight_parts = jnp.concatenate(
        [
            by_seq(w_query),
            kv_parts.reshape(seqs, own_rows, kv_cols),
            jnp.broadcast_to(extra, (seqs,) + extra.shape),
            out_parts,
        ],
        axis=2,
    )
    weight_own = in_seq_order(exchange_seq(weight_parts)).reshape(seqs * own_rows, -1)
    res_all = gather_seq(res).reshape(rows, width)
    weight_rel = jnp.concatenate(
        [piece.reshape(2 * seqs * own_rows, -1) for pair in gather_blk(weight_own) for piece in pair],
        axis=0,
    )
    gate_all = gather_seq(w_gate[0]).reshape(width, -1)
    up_all = gather_seq(w_up[0]).reshape(width, -1)
    down_all = gather_seq(w_down[0]).reshape(-1, width)
    cot_all = lax.all_gather(cot, "blk", axis=0)

    spot = jnp.arange(width, dtype=jnp.int32)
    place, inner = spot // (seqs * own_rows), spot % (seqs * own_rows)
    device = blk_me ^ (4 * (place // 4) + 2 * (place % 2) + (place // 2) % 2)
    source = (inner // own_rows * blks + device) * own_rows + inner % own_rows
    order = (spot[:, None] == source[None, :]).astype(bf16)

    positions = blk_me * rows + jnp.arange(rows, dtype=jnp.int32)
    cos_q, sin_q, cos_k, sin_k = rope_tables(positions)
    x_rel = nn(res_all, order).astype(bf16)
    q_all, kv_own, normed_rel = call(
        functools.partial(project_body, q_cols, kv_cols, experts),
        (shape_of((rows, q_cols), bf16), shape_of((rows, kv_cols), bf16), shape_of((rows, width), bf16)),
    )(x_rel, weight_rel, cos_q, sin_q, cos_k, sin_k)
    weight_abs = nn(order, weight_rel).astype(bf16)
    cols = q_cols + kv_cols
    qkv_abs = weight_abs[:, :cols]
    router_abs = weight_abs[:, cols : cols + LANES]
    out_abs = weight_abs[:, cols + LANES :]
    gains = router_abs[:, experts : experts + 2].astype(f32).T
    gain_one, gain_two = gains[0:1], gains[1:2]

    kv_keys = jnp.concatenate([shifted(kv_own, "blk", n) for n in range(hops, 0, -1)] + [kv_own], axis=0)
    seg_padded = jnp.concatenate([jnp.full((behind,), -1, jnp.int32), segments])
    seg_k = lax.dynamic_slice_in_dim(seg_padded, blk_me * rows, keys)[None, :]
    seg_q = lax.dynamic_slice_in_dim(segments, blk_me * rows, rows)[:, None]
    step = min(rows, 256)
    grid = (kv_local, rows // step)
    row_block = pl.BlockSpec((step, LANES), lambda g, i: (i, g))
    key_block = pl.BlockSpec((keys, LANES), lambda g, i: (0, g))
    seg_q_block = pl.BlockSpec((step, 1), lambda g, i: (i, 0))
    seg_k_block = pl.BlockSpec((1, keys), lambda g, i: (0, 0))
    table_block = pl.BlockSpec((step, LANES), lambda g, i: (i, 0))
    mixed, lse = call(
        functools.partial(attend_body, behind, scale),
        (shape_of((rows, q_cols), bf16), shape_of((rows, q_cols), f32)),
        grid=grid,
        in_specs=[row_block, key_block, seg_q_block, seg_k_block],
        out_specs=(row_block, row_block),
    )(q_all, kv_keys, seg_q, seg_k)

    def sum_over_seq(partial):
        parts = partial.reshape(seqs, -1, partial.shape[-1])
        own = lax.dynamic_index_in_dim(parts, seq_me, 0, keepdims=False)
        others = exchange_seq(parts.astype(bf16))[1:]
        return [own] + others

    branch_parts = sum_over_seq(nt(mixed, out_abs))
    lanes = jnp.arange(LANES, dtype=jnp.int32)
    member = jnp.sum((routes[0][:, :, None] == lanes[None, None, :]).astype(f32), axis=1)
    middle, wide, prob = call(
        functools.partial(middle_body, seqs, experts),
        (shape_of((toks, width), f32), shape_of((toks, width + LANES), bf16), shape_of((toks, LANES), f32)),
    )(*branch_parts, res, gain_two, router_abs, member)

    hidden_cols = gate_all.shape[1]
    me = jnp.reshape(blk_me, (1,)).astype(jnp.int32)
    whole = lambda dims: pl.BlockSpec(dims, lambda i, me_ref: (0,) * len(dims))
    chunk_rows = 4 * toks
    keep_y, keep_gi = (2, toks, width), (2, toks, width + LANES)
    out_dims = [
        ((chunk_rows, width), bf16), (keep_y, bf16), (keep_y, bf16), (keep_gi, bf16), (keep_gi, bf16),
        ((chunk_rows, hidden_cols), bf16), ((chunk_rows, hidden_cols), bf16),
        ((chunk_rows, hidden_cols), bf16), ((chunk_rows, width), bf16),
    ]
    results = []
    for k, (near, far) in enumerate(gather_blk(wide)):
        cot_spec = lambda j: pl.BlockSpec((1, toks, width), lambda i, me_ref: (me_ref[0] ^ j, 0, 0))
        results.append(
            call(
                functools.partial(expert_body, experts),
                tuple(shape_of(d, t) for d, t in out_dims),
                grid_spec=pltpu.PrefetchScalarGridSpec(
                    num_scalar_prefetch=1,
                    grid=(1,),
                    in_specs=[whole(keep_gi), whole(keep_gi)]
                    + [cot_spec(4 * k + j) for j in (0, 2, 1, 3)]
                    + [whole(gate_all.shape), whole(up_all.shape), whole(down_all.shape)],
                    out_specs=[whole(d) for d, _ in out_dims],
                ),
            )(me, near, far, cot_all, cot_all, cot_all, cot_all, gate_all, up_all, down_all)
        )
    grad_parts = [reduce_chunk(k, results[k][3], results[k][4]) for k in range(groups)]
    join = lambda i: jnp.concatenate([r[i] for r in results], axis=0)
    x_all, hid_all, ggp_all, gup_all, geo_all = join(0), join(5), join(6), join(7), join(8)
    tdot = lambda a, b: lax.dot_general(a, b, (((0,), (0,)), ((), ())), preferred_element_type=f32)
    grad_gate, grad_up, grad_down = tdot(x_all, ggp_all), tdot(x_all, gup_all), tdot(hid_all, geo_all)

    grad_middle, grad_branch, pack = call(
        functools.partial(middle_back_body, groups, experts),
        (shape_of((toks, width), f32), shape_of((toks, width), bf16), shape_of((LANES, width), bf16)),
    )(*grad_parts, middle, prob, cot, gain_two, router_abs)

    branch_all = gather_seq(grad_branch).reshape(rows, width)
    grad_mixed = nn(branch_all, out_abs).astype(bf16)
    gq_pre, grad_kv = call(
        functools.partial(attend_back_body, behind, scale),
        (shape_of((rows, q_cols), bf16), shape_of((keys, kv_cols), f32)),
        grid=grid,
        in_specs=[row_block, key_block, row_block, row_block, row_block, seg_q_block, seg_k_block,
                  table_block, table_block],
        out_specs=(row_block, key_block),
    )(q_all, kv_keys, mixed, grad_mixed, lse, seg_q, seg_k, cos_q, sin_q)
    returned = [
        shifted(grad_kv[(hops - n) * rows : (hops - n + 1) * rows].astype(bf16), "blk", -n)
        for n in range(1, hops + 1)
    ]
    gkv_pre = call(
        functools.partial(turn_back_body, hops), shape_of((rows, kv_cols), bf16)
    )(grad_kv[behind:], *returned, cos_k, sin_k)

    def reduce_rows(grad):
        terms = grad.astype(bf16).reshape(blks, seqs, own_rows, -1)
        return in_seq_order(exchange_seq(reduce_blk(terms).astype(bf16)))

    q_rows = reduce_rows(tdot(normed_rel, gq_pre))
    kv_rows = reduce_rows(tdot(normed_rel, gkv_pre))
    normed_parts = sum_over_seq(nt(gq_pre, qkv_abs[:, :q_cols]) + nt(gkv_pre, qkv_abs[:, q_cols:]))
    grad_input = call(
        functools.partial(input_back_body, seqs), shape_of((toks, width), f32)
    )(*normed_parts, res, grad_middle, gain_one)

    branch_rel = nn(branch_all, order).astype(bf16)
    pack_rel = tdot(order, pack.T).astype(bf16)
    out_rows = reduce_rows(jnp.concatenate([tdot(branch_rel, mixed).astype(bf16), pack_rel], axis=1))
    shard_query = q_rows.astype(f32).swapaxes(0, 1).reshape(own_rows, -1)
    kv_rows = kv_rows.astype(f32).reshape(seqs, own_rows, kv_local, 2, HEAD_DIM).transpose(3, 1, 0, 2, 4)
    shard_key = kv_rows[0].reshape(own_rows, -1)
    shard_value = kv_rows[1].reshape(own_rows, -1)
    shard_out = out_rows[:, :, :q_cols].astype(f32).transpose(0, 2, 1).reshape(-1, own_rows)
    packed = jnp.sum(out_rows[:, :, q_cols:].astype(f32), axis=0)
    shard_router = packed[:, :experts]
    shard_gain_two = packed[:, experts]
    weigh = lambda w, g: jnp.sum(w.astype(f32) * g, axis=1)
    shard_gain_one = (
        weigh(w_query, shard_query) + weigh(w_key, shard_key) + weigh(w_value, shard_value)
    ) / attn_gain.astype(f32)

    def reduce_seq(grad):
        total = None
        for piece in sum_over_seq(grad):
            total = piece if total is None else total + piece.astype(f32)
        return total[None]

    shard_gate, shard_up, shard_down = reduce_seq(grad_gate), reduce_seq(grad_up), reduce_seq(grad_down)

    y_total = middle
    for k in range(groups):
        y_total = y_total + reduce_chunk(k, results[k][1], results[k][2]).astype(f32)
    block_out = y_total.astype(bf16)[None]
    return (
        block_out, grad_input[None], shard_query, shard_key, shard_value, shard_out, shard_router,
        shard_gain_one, shard_gain_two, shard_gate, shard_up, shard_down,
    )


def solution(mesh):
    both = ("seq", "blk")
    tokens, rows, cols, line = P("blk", "seq", None), P(both, None), P(None, both), P(both)
    return jax.shard_map(
        per_device,
        mesh=mesh,
        in_specs=(
            tokens, P(), tokens, rows, rows, rows, cols, rows, line, line, tokens, tokens, tokens, tokens,
        ),
        out_specs=(
            tokens, tokens, rows, rows, rows, cols, rows, line, line, tokens, tokens, tokens,
        ),
        check_vma=False,
    )
```

```python
import functools
import math

import jax
import jax.numpy as jnp
import numpy as np
from jax import lax
from jax.experimental import pallas as pl
from jax.experimental.pallas import tpu as pltpu
from jax.sharding import PartitionSpec as P

HEADS = 16
KV_HEADS = 8
HEAD_DIM = 64
LANES = 128

f32 = jnp.float32
bf16 = jnp.bfloat16
epsilon = 1e-06
neg_large = -1e30


def swap_with(value, axis, mask):
    if mask == 0:
        return value
    count = lax.axis_size(axis)
    return lax.ppermute(value, axis, [(i, i ^ mask) for i in range(count)])


def shifted(value, axis, steps):
    count = lax.axis_size(axis)
    leading, last = (max(0, -steps), min(count, count - steps))
    return lax.ppermute(value, axis, [(i, i + steps) for i in range(leading, last)])


def gather_seq(value):
    count = lax.axis_size("seq")
    me = lax.axis_index("seq")
    whole = jnp.zeros((count,) + value.shape, value.dtype)
    for k in range(count):
        piece = swap_with(value, "seq", k)
        whole = lax.dynamic_update_index_in_dim(whole, piece, me ^ k, 0)
    return whole


def after(value, *others):
    return lax.optimization_barrier((value,) + others)[0]


def gather_masks(groups):
    near = [0, 2, 4, 6]
    far = [4 * k + x for k in range(2, groups) for x in (0, 2)]
    return [m + c for half in (near, far) for c in (0, 1) for m in half]


def gather_rows(value):
    groups = lax.axis_size("blk") // 4
    near_z = swap_with(value, "blk", 4)
    far, last = [], value
    for k in range(2, groups):
        last = swap_with(after(value, last), "blk", 4 * k)
        far += [last, swap_with(last, "blk", 2)]
    near = jnp.concatenate(
        [value, swap_with(value, "blk", 2), near_z, swap_with(near_z, "blk", 2)], axis=0
    )
    far = jnp.concatenate(far, axis=0)
    return jnp.concatenate([near, swap_with(near, "blk", 1), far, swap_with(far, "blk", 1)], axis=0)


def added(a, b):
    return (a.astype(f32) + b.astype(f32)).astype(a.dtype)


def scatter_core(keep, send):
    return added(keep, swap_with(send, "blk", 1))


def scatter_across(total):
    groups = lax.axis_size("blk") // 4
    parts = total.reshape(groups, 2, total.shape[0] // groups // 2, -1)
    return added(parts[:, 0], swap_with(parts[:, 1], "blk", 2))


def scatter_far(parts):
    return [swap_with(parts[k], "blk", 4 * k) for k in range(parts.shape[0] - 1, 0, -1)] + [parts[0]]


def call(body, out_shape, limit=16, flops=0, **options):
    many = isinstance(out_shape, (tuple, list))
    if "grid" not in options:
        space = pl.BlockSpec(memory_space=pltpu.VMEM)
        options.setdefault("out_specs", tuple(space for _ in out_shape) if many else space)
    sized = sum(math.prod(o.shape) * o.dtype.itemsize for o in (out_shape if many else [out_shape]))
    return pl.pallas_call(
        body,
        out_shape=out_shape,
        compiler_params=pltpu.CompilerParams(vmem_limit_bytes=limit * 1024 * 1024),
        cost_estimate=pl.CostEstimate(flops=flops, bytes_accessed=2 * sized, transcendentals=0),
        **options,
    )


def in_hbm(value):
    return pltpu.with_memory_space_constraint(value, pltpu.HBM)


def shape_of(dims, dtype):
    return jax.ShapeDtypeStruct(dims, dtype)


def lane_ids(shape):
    return lax.broadcasted_iota(jnp.int32, shape, len(shape) - 1)


def half_swap(tile):
    lanes = lane_ids(tile.shape)
    return jnp.where(lanes % 64 < 32, pltpu.roll(tile, 96, 1), pltpu.roll(tile, 32, 1))


def nt(a, b):
    return lax.dot_general(a, b, (((1,), (1,)), ((), ())), preferred_element_type=f32)


def tn(a, b):
    return lax.dot_general(a, b, (((0,), (0,)), ((), ())), preferred_element_type=f32)


def nn(a, b):
    return jnp.dot(a, b, preferred_element_type=f32)


def turned(tile, cos, sin, back=False):
    moved = half_swap(tile) * sin
    return tile * cos + (-moved if back else moved)


def key_tables(cos, sin):
    low = lane_ids(cos.shape) < HEAD_DIM
    return jnp.where(low, cos, 1.0), jnp.where(low, sin, 0.0)


def pack_body(seqs, dims, me_ref, *refs):
    q_cols, kv_cols, experts = dims
    sources, outs = refs[:7], refs[7 : 7 + seqs]
    held, sems = refs[7 + seqs : 14 + seqs], refs[14 + seqs]
    copies = [pltpu.make_async_copy(a, b, sems.at[i]) for i, (a, b) in enumerate(zip(sources, held))]
    for copy in copies:
        copy.start()
    for copy in copies:
        copy.wait()
    wq, wk, wv, wo, wr, gain_a, gain_m = held
    own_rows = wq.shape[0]
    lines = [wr[...].astype(f32), gain_a[...].astype(f32), gain_m[...].astype(f32)]
    lines.append(jnp.zeros((LANES - experts - 2, own_rows), f32))
    extra = jnp.concatenate(lines, axis=0).T.astype(bf16)
    half = kv_cols // 2
    for s in range(seqs):
        for k in range(seqs):

            @pl.when(me_ref[0] == s ^ k)
            def _(s=s, k=k):
                out = outs[k]
                out[:, :q_cols] = wq[:, s * q_cols : (s + 1) * q_cols]
                for g in range(half // HEAD_DIM):
                    span = slice(s * half + g * HEAD_DIM, s * half + (g + 1) * HEAD_DIM)
                    at = q_cols + 2 * g * HEAD_DIM
                    out[:, at : at + LANES] = jnp.concatenate([wk[:, span], wv[:, span]], axis=1)
                at = q_cols + kv_cols
                out[:, at : at + LANES] = extra
                out[:, at + LANES :] = wo[:, s * q_cols : (s + 1) * q_cols]


def restore_body(seqs, masks, experts, seq_ref, blk_ref, weight, qkv_ref, router_ref, gain_ref):
    cols = qkv_ref.shape[1]
    blks = len(masks)
    unit = weight.shape[0] // blks
    own_rows = unit // seqs
    for i, mask in enumerate(masks):
        for k in range(seqs):
            at = ((seq_ref[0] ^ k) * blks + (blk_ref[0] ^ mask)) * own_rows
            to = pl.ds(pl.multiple_of(at, own_rows), own_rows)
            span = slice(i * unit + k * own_rows, i * unit + (k + 1) * own_rows)
            qkv_ref[to, :] = weight[span, :cols]
            router_ref[to, :] = weight[span, cols:]
    pick = lax.broadcasted_iota(jnp.int32, (8, LANES), 0) + experts == lane_ids((8, LANES))
    gain_ref[...] = nt(pick.astype(bf16), router_ref[...])


def restore_out_body(seqs, blks, seq_ref, blk_ref, own, other, out_ref, sem):
    q_cols = out_ref.shape[1]
    own_rows = out_ref.shape[0] // blks // seqs
    copies = []
    for i in range(blks // 2):
        for c, weight in enumerate((own, other)):
            for k in range(seqs):
                blk = 2 * i + ((blk_ref[0] & 1) ^ c)
                at = ((seq_ref[0] ^ k) * blks + blk) * own_rows
                to = pl.ds(pl.multiple_of(at, own_rows), own_rows)
                part = weight.at[i, :, k * q_cols : (k + 1) * q_cols]
                copies.append(pltpu.make_async_copy(part, out_ref.at[to, :], sem.at[len(copies)]))
    for copy in copies:
        copy.start()
    for copy in copies:
        copy.wait()


def project_body(q_cols, kv_cols, gain_lane, x_ref, w_ref, cos, sin, q_ref, kv_ref, normed_ref):
    x = x_ref[...].astype(f32)
    inverse = lax.rsqrt(jnp.mean(x * x, axis=-1, keepdims=True) + epsilon)
    cols = q_cols + kv_cols
    pick = (lane_ids((8, LANES)) == gain_lane).astype(bf16)
    gain = nt(pick, w_ref[:, cols : cols + LANES])[0:1, :]
    normed = (x * inverse * gain).astype(bf16)
    normed_ref[...] = normed
    cos_q, sin_q = cos[...], sin[...]
    cos_k, sin_k = key_tables(cos_q, sin_q)
    wide = 2 * LANES if q_cols % (2 * LANES) == 0 and kv_cols % (2 * LANES) == 0 else LANES
    for first in range(0, cols, wide):
        both = nn(normed, w_ref[:, first : first + wide])
        for at in range(first, first + wide, LANES):
            tile = both[:, at - first : at - first + LANES]
            if at < q_cols:
                q_ref[:, at : at + LANES] = turned(tile, cos_q, sin_q).astype(bf16)
            else:
                kv_ref[:, at - q_cols : at - q_cols + LANES] = turned(tile, cos_k, sin_k).astype(bf16)


def visible_keys(meta_q, meta_k):
    mine = meta_q[...].T
    theirs = meta_k[...]
    return (theirs[1:2, :] <= mine[:, 1:2]) & (theirs[0:1, :] == mine[:, 0:1])


def attend_body(scale, q_ref, kv_ref, meta_q, meta_k, out_ref, lse_ref):
    visible = visible_keys(meta_q, meta_k)
    q = q_ref[...].astype(f32)
    kv = kv_ref[...]
    low = lane_ids(q.shape) < HEAD_DIM
    outs, lses = [], []
    for half in range(2):
        head = jnp.where(low, pltpu.roll(q, HEAD_DIM, 1) if half else q, 0.0).astype(bf16)
        scores = jnp.where(visible, nt(head, kv) * scale, neg_large)
        most = jnp.max(scores, axis=-1, keepdims=True)
        weights = jnp.exp(scores - most)
        total = jnp.sum(weights, axis=-1, keepdims=True)
        outs.append(nn(weights.astype(bf16), kv) / total)
        lses.append(most + jnp.log(total))
    out_ref[...] = jnp.where(low, pltpu.roll(outs[0], HEAD_DIM, 1), outs[1]).astype(bf16)
    lse_ref[...] = jnp.where(low, lses[0], lses[1])


def attend_back_body(
    scale, q_ref, kv_ref, mixed_ref, grad_ref, lse_ref, meta_q, meta_k, cos, sin, dq_ref, *outs
):
    outs, dkv_ref = outs[:-1], outs[-1]
    visible = visible_keys(meta_q, meta_k)
    q = q_ref[...].astype(f32)
    kv = kv_ref[...]
    grad = grad_ref[...].astype(f32)
    low = lane_ids(q.shape) < HEAD_DIM
    product = grad * mixed_ref[...].astype(f32)
    lse = lse_ref[...]
    dqs = []
    dkv = None
    for half in range(2):
        head = jnp.where(low, pltpu.roll(q, HEAD_DIM, 1) if half else q, 0.0).astype(bf16)
        grad_head = jnp.where(low, 0.0, grad if half else pltpu.roll(grad, HEAD_DIM, 1)).astype(bf16)
        delta = jnp.sum(jnp.where(low == (half == 0), product, 0.0), axis=-1, keepdims=True)
        lse_head = lse[:, HEAD_DIM * half : HEAD_DIM * half + 1]
        probs = jnp.where(visible, jnp.exp(nt(head, kv) * scale - lse_head), 0.0)
        grad_scores = (probs * (nt(grad_head, kv) - delta)).astype(bf16)
        dqs.append(nn(grad_scores, kv) * scale)
        term = tn(grad_scores, head) * scale + tn(probs.astype(bf16), grad_head)
        dkv = term if dkv is None else dkv + term
    dq = jnp.where(low, dqs[0], pltpu.roll(dqs[1], HEAD_DIM, 1)).astype(bf16).astype(f32)
    dq_ref[...] = turned(dq, cos[...], sin[...], back=True).astype(bf16)

    @pl.when(pl.program_id(1) == 0)
    def _():
        dkv_ref[...] = dkv

    @pl.when(pl.program_id(1) > 0)
    def _():
        dkv_ref[...] += dkv

    @pl.when(pl.program_id(1) == pl.num_programs(1) - 1)
    def _():
        at = 0
        for out in outs:
            out[...] = dkv_ref[at : at + out.shape[0], :].astype(out.dtype)
            at += out.shape[0]


def row_spans(width):
    near, far = 4, width // 2 - 4
    return ((0, near, 0, 0), (near, near, 1, 0), (2 * near, far, 0, near), (2 * near + far, far, 1, near))


def query_terms_body(blks, normed, gq, branch, mixed, pack, *outs):
    q_cols = gq.shape[1]
    unit = normed.shape[1] // blks
    for at, count, which, to in row_spans(blks):
        span, place = slice(at * unit, (at + count) * unit), slice(to * unit, (to + count) * unit)
        out = outs[which]
        out[place, :q_cols] = tn(normed[:, span], gq[...]).astype(bf16)
        out[place, q_cols : 2 * q_cols] = tn(branch[:, span], mixed[...]).astype(bf16)
        out[place, 2 * q_cols :] = pack[span, :]


def key_terms_body(blks, normed, gkv, *outs):
    unit = normed.shape[1] // blks
    for at, count, which, to in row_spans(blks):
        span, place = slice(at * unit, (at + count) * unit), slice(to * unit, (to + count) * unit)
        outs[which][place, :] = tn(normed[:, span], gkv[...]).astype(bf16)


def turn_back_body(count, seqs, *refs):
    own, others = refs[0], refs[1 : 1 + count]
    cos, sin, gq, weight = refs[1 + count : 5 + count]
    outs = refs[5 + count :]
    gkv_ref, parts = outs[0], outs[1:]
    cos_k, sin_k = key_tables(cos[...], sin[...])
    q_cols = gq.shape[1]
    for first in range(0, own.shape[1], LANES):
        span = slice(first, first + LANES)
        total = own[:, span]
        for other in others:
            total = total + other[:, span].astype(f32)
        gkv_ref[:, span] = turned(total.astype(bf16).astype(f32), cos_k, sin_k, back=True).astype(bf16)
    toks = parts[0].shape[0]
    for k in reversed(range(seqs)):
        span = slice(k * toks, (k + 1) * toks)
        grad = nt(gq[span, :], weight[:, :q_cols]) + nt(gkv_ref[span, :], weight[:, q_cols:])
        parts[k][...] = grad.astype(parts[k].dtype)


def to_row(column):
    count = column.shape[0]
    same = lax.broadcasted_iota(jnp.int32, (count, count), 0) == lane_ids((count, count))
    return jnp.sum(jnp.where(same, column, 0.0), axis=0, keepdims=True)


def finish_body(seqs, experts, me_ref, *refs):
    q_pieces, kv_pieces = refs[:seqs], refs[seqs : 2 * seqs]
    wq, wk, wv, gain = refs[2 * seqs : 2 * seqs + 4]
    query_ref, key_ref, value_ref, out_ref, router_ref, gain_one_ref, gain_two_ref = refs[2 * seqs + 4 :]
    q_cols = query_ref.shape[1] // seqs
    half = key_ref.shape[1] // seqs
    packed = None
    for k in range(seqs):
        part = q_pieces[k][:, 2 * q_cols :].astype(f32)
        packed = part if packed is None else packed + part
        for s in range(seqs):

            @pl.when(me_ref[0] == s ^ k)
            def _(s=s, k=k):
                span = slice(s * q_cols, (s + 1) * q_cols)
                query_ref[:, span] = q_pieces[k][:, :q_cols].astype(f32)
                out_ref[:, span] = q_pieces[k][:, q_cols : 2 * q_cols].astype(f32)
                for g in range(half // HEAD_DIM):
                    both = kv_pieces[k][:, 2 * g * HEAD_DIM : 2 * (g + 1) * HEAD_DIM].astype(f32)
                    span = slice(s * half + g * HEAD_DIM, s * half + (g + 1) * HEAD_DIM)
                    key_ref[:, span] = both[:, :HEAD_DIM]
                    value_ref[:, span] = both[:, HEAD_DIM:]

    router_ref[...] = packed.T[:experts, :]
    gain_two_ref[...] = to_row(packed[:, experts : experts + 1])
    weigh = lambda w, g: jnp.sum(w[...].astype(f32) * g[...], axis=1, keepdims=True)
    total = weigh(wq, query_ref) + weigh(wk, key_ref) + weigh(wv, value_ref)
    gain_one_ref[...] = to_row(total) / gain[...].astype(f32)


def middle_body(count, experts, *refs):
    parts = refs[:count]
    res, gains, router, routes, middle_ref, wide_ref, prob_ref = refs[count:]
    width = res.shape[1]
    middle = res[...].astype(f32)
    for part in parts:
        middle = middle + part[...].astype(f32)
    middle_ref[...] = middle
    inverse = lax.rsqrt(jnp.mean(middle * middle, axis=-1, keepdims=True) + epsilon)
    normed = (middle * inverse * gains[1:2, :]).astype(bf16)
    wide_ref[:, :width] = normed
    named = routes[...].astype(f32).T
    lanes = lane_ids((named.shape[0], LANES)).astype(f32)
    inside = lanes == named[:, 0:1]
    for i in range(1, named.shape[1]):
        inside = inside | (lanes == named[:, i : i + 1])
    logits = jnp.where(inside, nn(normed, router[...]), neg_large)
    raised = jnp.where(inside, jnp.exp(logits - jnp.max(logits, axis=-1, keepdims=True)), 0.0)
    prob = raised / jnp.sum(raised, axis=-1, keepdims=True)
    prob_ref[...] = prob
    high = prob.astype(bf16).astype(f32)
    rest = (prob - high).astype(bf16).astype(f32)
    wide_ref[:, width:] = (high + pltpu.roll(rest, experts, 1)).astype(bf16)


def expert_body(experts, k, seqs, me_ref, seq_ref, *refs):
    pieces, cot_all, packs = refs[:2], refs[2], refs[3 : 3 + 2 * seqs]
    outs, scratch = refs[-18:-11], refs[-11:]
    y_all, x_all, hid_all, ggp_all, gup_all, geo_all, gi_ref = outs
    wide, cot_ref, y_ref, x_ref, hid_ref, ggp_ref, gup_ref, geo_ref, wgu, wd, sems = scratch
    rows, width = cot_ref.shape[1], cot_ref.shape[2]
    high, low, cols = width // seqs, wd.shape[1] // seqs, wgu.shape[2] // 2
    me = me_ref[0]
    loads = [pltpu.make_async_copy(p, wide.at[i], sems.at[0, i]) for i, p in enumerate(pieces)]
    gates, downs = [], []
    for e in range(2):
        for j in range(seqs):
            at = pl.ds(pl.multiple_of((seq_ref[0] ^ j) * high, high), high)
            to = pl.ds(pl.multiple_of((seq_ref[0] ^ j) * low, low), low)
            pack = packs[e * seqs + j]
            gates.append(pltpu.make_async_copy(pack.at[:high, :], wgu.at[e, at, :], sems.at[1 + e, j]))
            downs.append(pltpu.make_async_copy(pack.at[high:, :], wd.at[e, to, :], sems.at[3 + e, j]))
    cots = [
        pltpu.make_async_copy(cot_all.at[(me ^ (4 * k + 2 * i)) // 2, :rows, :], cot_ref.at[i], sems.at[5, i])
        for i in range(2)
    ]
    for copies in (loads, gates[:seqs], downs[:seqs], cots, gates[seqs:], downs[seqs:]):
        for copy in copies:
            copy.start()
    for copy in loads:
        copy.wait()
    probs = [[], []]
    for i in range(2):
        x_ref[i * rows : (i + 1) * rows, :] = wide[i, :, :width]
        extra = wide[i, :, width:].astype(f32)
        lanes = lane_ids(extra.shape)
        for e in range(2):
            mine = (lanes == (me ^ e)) | (lanes == (me ^ e) + experts)
            probs[e].append(jnp.sum(jnp.where(mine, extra, 0.0), axis=-1, keepdims=True))
    x = x_ref[...]
    place = pl.ds(2 * k * rows, 2 * rows)
    stores = []

    def store(a, b, sem):
        stores.append(pltpu.make_async_copy(a, b, sem))
        stores[-1].start()

    store(x_ref, x_all.at[place, :], sems.at[8, 2])
    out, grad_in, marks, kept = None, None, [], []
    for e in range(2):
        prob = jnp.concatenate(probs[e], axis=0)
        for copy in gates[e * seqs : (e + 1) * seqs]:
            copy.wait()
        gate = nn(x, wgu[e, :, :cols])
        up = nn(x, wgu[e, :, cols:])
        sigmoid = 1.0 / (1.0 + jnp.exp(-gate))
        active = gate * sigmoid
        hidden = (active * up).astype(bf16)
        hid_ref[e] = hidden
        store(hid_ref.at[e], hid_all.at[e, place, :], sems.at[6 + e, 0])
        for copy in downs[e * seqs : (e + 1) * seqs]:
            copy.wait()
        result = nn(hidden, wd[e]).astype(bf16).astype(f32)
        if e == 0:
            for copy in cots:
                copy.wait()
        final = jnp.concatenate([cot_ref[0], cot_ref[1]], axis=0).astype(f32)
        out = prob * result if out is None else out + prob * result
        marks.append(jnp.sum(result * final, axis=-1, keepdims=True))
        geo_ref[e] = (prob * final).astype(bf16)
        store(geo_ref.at[e], geo_all.at[e, place, :], sems.at[6 + e, 3])
        kept.append((gate, up, sigmoid, active))
    y_ref[...] = out.astype(bf16)
    for i in range(2):
        store(y_ref.at[i * rows : (i + 1) * rows, :], y_all.at[(me ^ (4 * k + 2 * i)) // 2], sems.at[8, i])
    for e in range(2):
        gate, up, sigmoid, active = kept[e]
        grad_hidden = nt(geo_ref[e], wd[e])
        ggp = (grad_hidden * up * sigmoid * (1.0 + gate * (1.0 - sigmoid))).astype(bf16)
        gup = (grad_hidden * active).astype(bf16)
        ggp_ref[e] = ggp
        gup_ref[e] = gup
        store(ggp_ref.at[e], ggp_all.at[e, place, :], sems.at[6 + e, 1])
        store(gup_ref.at[e], gup_all.at[e, place, :], sems.at[6 + e, 2])
        grad = nt(ggp, wgu[e, :, :cols]) + nt(gup, wgu[e, :, cols:])
        grad_in = grad if grad_in is None else grad_in + grad
    lanes = lane_ids((2 * rows, LANES))
    extra = jnp.zeros((2 * rows, LANES), f32)
    for e in range(2):
        mark = marks[e].astype(bf16).astype(f32)
        extra = extra + jnp.where(lanes == (me ^ e), mark, 0.0)
        extra = extra + jnp.where(lanes == (me ^ e) + experts, marks[e] - mark, 0.0)
    for i in range(2):
        span = slice(i * rows, (i + 1) * rows)
        gi_ref[i, :, :width] = grad_in[span, :].astype(bf16)
        gi_ref[i, :, width:] = extra[span, :].astype(bf16)
    for copy in stores:
        copy.wait()


def expert_grads_body(e, seqs, me_ref, *refs):
    sources, (x, ggp, gup, hid, geo, sems) = refs[:5], refs[-6:]
    outs = refs[5:-6]
    copies = [
        pltpu.make_async_copy(a if i == 0 else a.at[e], b, sems.at[i])
        for i, (a, b) in enumerate(zip(sources, (x, ggp, gup, hid, geo)))
    ]
    for copy in copies:
        copy.start()
    for copy in copies:
        copy.wait()
    high, cols, low = x.shape[1] // seqs, hid.shape[1], hid.shape[1] // seqs
    places = (
        (slice(0, high), slice(0, cols)),
        (slice(0, high), slice(cols, 2 * cols)),
        (slice(high, high + low), slice(0, 2 * cols)),
    )
    for s in range(seqs):
        at, to = slice(s * high, (s + 1) * high), slice(s * low, (s + 1) * low)
        k = me_ref[0] ^ s
        for i, (rows, lanes) in enumerate(places):
            if i < 2:
                part = tn(x[:, at], (ggp, gup)[i][...])
            else:
                part = tn(hid[:, to], geo[...])
            if e == 1:
                outs[0][k, rows, lanes] = part.astype(bf16)
            else:
                part = part + outs[0][k, rows, lanes].astype(f32)

                @pl.when(k == 0)
                def _(part=part, i=i):
                    outs[1 + i][...] = part

                @pl.when(k != 0)
                def _(part=part, rows=rows, lanes=lanes):
                    outs[4][k - 1, rows, lanes] = part.astype(bf16)


def middle_back_body(count, experts, *refs):
    parts = refs[:count]
    middle_ref, prob_ref, cot, gains, router, grad_ref, branch_ref, pack_ref = refs[count:]
    width = cot.shape[1]
    gain = gains[1:2, :]
    total = parts[0][...].astype(f32)
    for part in parts[1:]:
        total = total + part[...].astype(f32)
    extra = total[:, width:]
    marks = extra + pltpu.roll(extra, LANES - experts, 1)
    prob = prob_ref[...]
    weighted = jnp.where(prob > 0, prob * marks, 0.0)
    spread = jnp.sum(weighted, axis=-1, keepdims=True)
    grad_logits = weighted - prob * spread
    high = grad_logits.astype(bf16)
    rest = (grad_logits - high.astype(f32)).astype(bf16)
    grad_normed = total[:, :width] + nt(high, router[...]) + nt(rest, router[...])
    middle = middle_ref[...]
    inverse = lax.rsqrt(jnp.mean(middle * middle, axis=-1, keepdims=True) + epsilon)
    unit = middle * inverse
    scaled = grad_normed * gain
    grad = cot[...].astype(f32) + inverse * (
        scaled - unit * jnp.mean(scaled * unit, axis=-1, keepdims=True)
    )
    grad_ref[...] = grad
    branch_ref[...] = grad.astype(bf16)
    normed = (unit * gain).astype(bf16)
    pack = tn(high, normed) + tn(rest, normed)
    gain_row = jnp.sum(grad_normed * unit, axis=0, keepdims=True)
    at_gain = lax.broadcasted_iota(jnp.int32, pack.shape, 0) == experts
    pack_ref[...] = jnp.where(at_gain, gain_row, pack).astype(bf16)


def input_back_body(count, *refs):
    parts = refs[:count]
    res, grad_middle, gains, out_ref = refs[count:]
    grad_normed = parts[0][...].astype(f32)
    for part in parts[1:]:
        grad_normed = grad_normed + part[...].astype(f32)
    x = res[...].astype(f32)
    inverse = lax.rsqrt(jnp.mean(x * x, axis=-1, keepdims=True) + epsilon)
    unit = x * inverse
    scaled = grad_normed * gains[0:1, :]
    out_ref[...] = grad_middle[...] + inverse * (
        scaled - unit * jnp.mean(scaled * unit, axis=-1, keepdims=True)
    )


def per_device(
    residual, segments, routes, w_query, w_key, w_value, w_out, w_router, attn_gain, moe_gain,
    w_gate, w_up, w_down, cotangent,
):
    seqs, blks = lax.axis_size("seq"), lax.axis_size("blk")
    seq_me, blk_me = lax.axis_index("seq"), lax.axis_index("blk")
    toks, width = residual.shape[1], residual.shape[2]
    rows = toks * seqs
    experts = blks
    own_rows = w_query.shape[0]
    kv_local = KV_HEADS // seqs
    q_cols, kv_cols = HEADS // seqs * HEAD_DIM, kv_local * 2 * HEAD_DIM
    cols = q_cols + kv_cols
    scale = HEAD_DIM ** (-0.5)
    tokens = segments.shape[0]
    doc_most = tokens // 8
    hops = min(blks - 1, -(-(doc_most - 1) // rows))
    behind = hops * rows
    keys = behind + rows
    groups = blks // 4
    masks = gather_masks(groups)
    res = residual[0]
    cot = cotangent[0]
    vmem = pl.BlockSpec(memory_space=pltpu.VMEM)
    smem = pl.BlockSpec(memory_space=pltpu.SMEM)
    seq_scalar = jnp.reshape(seq_me, (1,)).astype(jnp.int32)
    blk_scalar = jnp.reshape(blk_me, (1,)).astype(jnp.int32)
    hbm = pl.BlockSpec(memory_space=pltpu.HBM)
    gain_row = attn_gain[None, :]

    weight_dims = (own_rows, cols + LANES + q_cols)
    sources = (w_query, w_key, w_value, w_out.T, w_router.T, gain_row, moe_gain[None, :])
    weight_parts = call(
        functools.partial(pack_body, seqs, (q_cols, kv_cols, experts)),
        tuple(shape_of(weight_dims, bf16) for _ in range(seqs)),
        in_specs=[smem] + [hbm] * 7,
        scratch_shapes=[pltpu.VMEM(a.shape, a.dtype) for a in sources] + [pltpu.SemaphoreType.DMA((7,))],
    )(seq_scalar, *[in_hbm(a) for a in sources])
    weight_both = jnp.concatenate([swap_with(p, "seq", k) for k, p in enumerate(weight_parts)], axis=0)
    weight_own = weight_both[:, : cols + LANES]
    late_res = after(res, weight_both)
    res_parts = [res] + [swap_with(late_res, "seq", k) for k in range(1, seqs)]
    weight_rel = gather_rows(weight_own)
    same_core = [[2 * i + c for i in range(blks // 2)] for c in range(2)]
    joint = seqs * own_rows * q_cols // width
    out_own = weight_both[:, cols + LANES :].reshape(seqs, own_rows, q_cols)
    out_own = jnp.concatenate([out_own[k] for k in range(seqs)], axis=1).reshape(joint, width)
    both_all = lax.all_gather(
        jnp.concatenate([cot, out_own], axis=0), "blk", axis=0, axis_index_groups=same_core
    )
    gate, up, down, *_ = lax.optimization_barrier((w_gate[0], w_up[0], w_down[0], *res_parts))
    expert_pack = jnp.concatenate([jnp.concatenate([gate, up], axis=1), down], axis=0)
    packs = [swap_with(expert_pack, "seq", k) for k in range(seqs)]
    seq_me, blk_me = after(seq_me, weight_own), after(blk_me, weight_own)

    spot = np.arange(width)
    place, inner = spot // (seqs * own_rows), spot % (seqs * own_rows)
    mask_row = jnp.asarray(np.asarray(masks)[place], jnp.int32)
    seq_row = jnp.asarray(inner // own_rows, jnp.int32)
    source = ((seq_me ^ seq_row) * blks + (blk_me ^ mask_row)) * own_rows + (inner % own_rows)
    order = (lax.broadcasted_iota(jnp.int32, (width, width), 0) == source[None, :]).astype(bf16)

    turn = lambda i: (seq_me ^ (i // toks % seqs)) * toks + i % toks
    half_dim = HEAD_DIM // 2
    lanes = lane_ids((rows, LANES))
    inverse = jnp.exp((lanes % half_dim).astype(f32) * (-2.0 * math.log(10000.0) / HEAD_DIM))
    position = blk_me * rows + turn(lax.broadcasted_iota(jnp.int32, (rows, LANES), 0))
    angles = position.astype(f32) * inverse
    cos, sin = jnp.cos(angles), jnp.where(lanes % HEAD_DIM < half_dim, -1.0, 1.0) * jnp.sin(angles)
    key_ids = jnp.arange(keys, dtype=jnp.int32)
    key_places = key_ids // rows * rows - behind + turn(key_ids % rows)
    seg_padded = jnp.concatenate([jnp.full((behind,), -1, jnp.int32), segments])
    seg_near = lax.dynamic_slice_in_dim(seg_padded, blk_me * rows, keys).reshape(hops + 1, seqs, toks)
    seg_keys = jnp.stack(
        [lax.dynamic_index_in_dim(seg_near, seq_me ^ k, 1, keepdims=False) for k in range(seqs)], axis=1
    ).reshape(keys)
    meta = jnp.concatenate(
        [seg_keys.astype(f32)[None], key_places.astype(f32)[None], jnp.zeros((6, keys), f32)], axis=0
    )

    x_rel = jnp.concatenate([nn(part, order).astype(bf16) for part in res_parts], axis=0)
    q_all, kv_own, normed_rel = call(
        functools.partial(project_body, q_cols, kv_cols, experts),
        (shape_of((rows, q_cols), bf16), shape_of((rows, kv_cols), bf16), shape_of((rows, width), bf16)),
    )(x_rel, weight_rel, cos, sin)
    if own_rows % 16 == 0:
        qkv_abs, router_abs, gains = call(
            functools.partial(restore_body, seqs, masks, experts),
            (shape_of((width, cols), bf16), shape_of((width, LANES), bf16), shape_of((8, width), f32)),
            in_specs=[smem, smem, vmem],
        )(seq_scalar, blk_scalar, weight_rel)
    else:
        weight_abs = nn(order, weight_rel).astype(bf16)
        qkv_abs, router_abs = weight_abs[:, :cols], weight_abs[:, cols:]
        gains = jnp.pad(router_abs[:, experts : experts + 2].astype(f32).T, ((0, 6), (0, 0)))

    kv_keys = jnp.concatenate([shifted(kv_own, "blk", n) for n in range(hops, 0, -1)] + [kv_own], axis=0)
    step = min(rows, 256)
    grid = (kv_local, rows // step)
    row_block = pl.BlockSpec((step, LANES), lambda g, i: (i, g))
    key_block = pl.BlockSpec((keys, LANES), lambda g, i: (0, g))
    meta_q_block = pl.BlockSpec((8, step), lambda g, i: (0, behind // step + i))
    meta_k_block = pl.BlockSpec((8, keys), lambda g, i: (0, 0))
    table_block = pl.BlockSpec((step, LANES), lambda g, i: (i, 0))
    attend_limit = 8 + step * keys * 40 // 1024 // 1024
    mixed, lse = call(
        functools.partial(attend_body, scale),
        (shape_of((rows, q_cols), bf16), shape_of((rows, q_cols), f32)),
        limit=attend_limit,
        grid=grid,
        in_specs=[row_block, key_block, meta_q_block, meta_k_block],
        out_specs=(row_block, row_block),
    )(q_all, kv_keys, meta, meta)

    packs += [swap_with(after(p, mixed), "blk", 1) for p in packs]

    out_same = after(both_all[:, toks:], mixed)
    out_pair = [out_same, swap_with(out_same, "blk", 1)]
    if own_rows % 16 == 0:
        out_abs = call(
            functools.partial(restore_out_body, seqs, blks),
            shape_of((width, q_cols), bf16),
            in_specs=[smem, smem, hbm, hbm],
            scratch_shapes=[pltpu.SemaphoreType.DMA((blks * seqs,))],
        )(seq_scalar, blk_scalar, *[in_hbm(a) for a in out_pair])
    else:
        odd = blk_me % 2 == 1
        pair = jnp.stack([jnp.where(odd, out_pair[1 - c], out_pair[c]) for c in range(2)], axis=1)
        out_parts = pair.reshape(blks, own_rows, seqs, q_cols).swapaxes(1, 2)
        out_abs = jnp.stack(
            [lax.dynamic_index_in_dim(out_parts, seq_me ^ k, 1, keepdims=False) for k in range(seqs)]
        ).reshape(width, q_cols)

    branch = nt(mixed, out_abs)
    branch_parts = [branch[:toks]] + [
        swap_with(branch[k * toks : (k + 1) * toks].astype(bf16), "seq", k) for k in range(1, seqs)
    ]
    middle, wide, prob = call(
        functools.partial(middle_body, seqs, experts),
        (shape_of((toks, width), f32), shape_of((toks, width + LANES), bf16), shape_of((toks, LANES), f32)),
    )(*branch_parts, res, gains, router_abs, routes[0].T)

    hidden_cols = w_gate.shape[2]
    held = 2 * toks * groups
    buffers = [
        (2 * groups, toks, width), (held, width), (2, held, hidden_cols),
        (2, held, hidden_cols), (2, held, hidden_cols), (2, held, width),
    ]

    def run_experts(k, pieces, before):
        operands = [*pieces, both_all, *packs, *before]
        fixed = len(operands) - len(before) + 2
        return call(
            functools.partial(expert_body, experts, k, seqs),
            tuple(pltpu.HBM(d, bf16) for d in buffers) + (shape_of((2, toks, width + LANES), bf16),),
            limit=32,
            flops=48 * toks * width * hidden_cols,
            in_specs=[smem, smem] + [hbm] * len(operands),
            out_specs=(hbm,) * len(buffers) + (vmem,),
            input_output_aliases={fixed + i: i for i in range(len(before))},
            scratch_shapes=[
                pltpu.VMEM((2, toks, width + LANES), bf16),
                pltpu.VMEM((2, toks, width), bf16),
                pltpu.VMEM((2 * toks, width), bf16),
                pltpu.VMEM((2 * toks, width), bf16),
                pltpu.VMEM((2, 2 * toks, hidden_cols), bf16),
                pltpu.VMEM((2, 2 * toks, hidden_cols), bf16),
                pltpu.VMEM((2, 2 * toks, hidden_cols), bf16),
                pltpu.VMEM((2, 2 * toks, width), bf16),
                pltpu.VMEM((2, width, 2 * hidden_cols), bf16),
                pltpu.VMEM((2, hidden_cols, width), bf16),
                pltpu.SemaphoreType.DMA((9, max(4, seqs))),
            ],
        )(blk_scalar, seq_scalar, *[in_hbm(a) for a in operands])

    turns = [1] + list(range(groups - 1, 1, -1)) + [0]
    far = {0: wide}
    last = wide
    for k in turns[:-1]:
        far[k] = swap_with(after(wide, last), "blk", 4 * k)
        last = far[k] if k > 1 else last
    across = {k: swap_with(far[k], "blk", 2) for k in far}
    grads, nears, before = {}, {}, []
    for i, k in enumerate(turns):
        holds = [prob]
        if i > 0:
            holds.append(grads[turns[i - 1]])
        if i > 1:
            n = turns[i - 2]
            nears[n] = added(grads[n][0], swap_with(grads[n][1], "blk", 2))
            holds.append(nears[n])
        *before, grads[k] = run_experts(k, [after(far[k], *holds), across[k]], before)
    for n in turns[-2:]:
        nears[n] = added(grads[n][0], swap_with(grads[n][1], "blk", 2))
    grad_parts = [swap_with(nears[k], "blk", 4 * k) for k in turns]
    y_all, x_all, hid_all, ggp_all, gup_all, geo_all = before
    tdot = lambda a, b: lax.dot_general(a, b, (((0,), (0,)), ((), ())), preferred_element_type=f32)

    grad_middle, grad_branch, pack = call(
        functools.partial(middle_back_body, groups, experts),
        (shape_of((toks, width), f32), shape_of((toks, width), bf16), shape_of((LANES, width), bf16)),
    )(*grad_parts, middle, prob, cot, gains, router_abs)

    high, low = width // seqs, hidden_cols // seqs

    def expert_grads(e, outs, *others):
        operands = [in_hbm(a) for a in (x_all, ggp_all, gup_all, hid_all, geo_all)]
        return call(
            functools.partial(expert_grads_body, e, seqs),
            outs,
            limit=20 + 14 * held // 2048,
            flops=6 * held * width * hidden_cols,
            in_specs=[smem] + [hbm] * 5 + [vmem] * len(others),
            scratch_shapes=[
                pltpu.VMEM((held, width), bf16), pltpu.VMEM((held, hidden_cols), bf16),
                pltpu.VMEM((held, hidden_cols), bf16), pltpu.VMEM((held, hidden_cols), bf16),
                pltpu.VMEM((held, width), bf16), pltpu.SemaphoreType.DMA((5,)),
            ],
        )(seq_scalar, *operands, *others)

    partner_terms = expert_grads(1, shape_of((seqs, high + low, width), bf16))
    branch_others = [swap_with(grad_branch, "seq", k) for k in range(1, seqs)]
    branch_all = after(jnp.concatenate([grad_branch] + branch_others, axis=0), partner_terms)
    grad_mixed = nn(branch_all, out_abs).astype(bf16)
    block_spec = pl.BlockSpec((rows, LANES), lambda g, i: (0, g))
    gq_pre, *grad_kv = call(
        functools.partial(attend_back_body, scale),
        (shape_of((rows, q_cols), bf16),)
        + (shape_of((rows, kv_cols), bf16),) * hops
        + (shape_of((rows, kv_cols), f32),),
        limit=attend_limit,
        grid=grid,
        in_specs=[row_block, key_block, row_block, row_block, row_block, meta_q_block, meta_k_block,
                  table_block, table_block],
        out_specs=(row_block,) + (block_spec,) * (hops + 1),
        scratch_shapes=[pltpu.VMEM((keys, LANES), f32)],
    )(q_all, kv_keys, mixed, grad_mixed, lse, meta, meta, cos, sin)
    returned = [shifted(grad_kv[hops - n], "blk", -n) for n in range(1, hops + 1)]
    *shards, grad_sends = expert_grads(
        0,
        (shape_of((high, hidden_cols), f32), shape_of((high, hidden_cols), f32), shape_of((low, width), f32),
         shape_of((max(1, seqs - 1), high + low, width), bf16)),
        after(swap_with(partner_terms, "blk", 1), gq_pre),
    )
    branch_rel = nn(branch_all, order).astype(bf16)
    pack_rel = tdot(order, pack.T).astype(bf16)
    unit = seqs * own_rows
    q_terms = call(
        functools.partial(query_terms_body, blks),
        (shape_of((width // 2, 2 * q_cols + LANES), bf16),) * 2,
    )(normed_rel, gq_pre, branch_rel, mixed, pack_rel)

    def for_this_row(terms):
        total = sum(t.astype(f32) for t in terms).astype(bf16)
        return [swap_with(total[k * own_rows : (k + 1) * own_rows], "seq", k) for k in range(seqs)]

    q_total = scatter_core(*q_terms)
    q_stage = scatter_across(q_total)
    own_kv = after(grad_kv[-1], q_total, grad_sends)

    gkv_pre, *normed_parts = call(
        functools.partial(turn_back_body, hops, seqs),
        (shape_of((rows, kv_cols), bf16),)
        + tuple(shape_of((toks, width), bf16 if k else f32) for k in range(seqs)),
    )(own_kv, *returned, cos, sin, gq_pre, qkv_abs)
    kv_terms = call(
        functools.partial(key_terms_body, blks), (shape_of((width // 2, kv_cols), bf16),) * 2
    )(normed_rel, gkv_pre)
    q_pieces = for_this_row(scatter_far(q_stage))
    kv_pieces = for_this_row(scatter_far(scatter_across(scatter_core(*kv_terms))))
    shard_query, shard_key, shard_value, shard_out, shard_router, shard_gain_one, shard_gain_two = call(
        functools.partial(finish_body, seqs, experts),
        (shape_of(w_query.shape, f32), shape_of(w_key.shape, f32), shape_of(w_value.shape, f32),
         shape_of(w_out.shape[::-1], f32), shape_of(w_router.shape[::-1], f32),
         shape_of((1, own_rows), f32), shape_of((1, own_rows), f32)),
        in_specs=[smem] + [vmem] * (2 * seqs + 4),
    )(seq_scalar, *q_pieces, *kv_pieces, w_query, w_key, w_value, gain_row)
    normed_others = [swap_with(p, "seq", k) for k, p in enumerate(normed_parts) if k]
    grads_from = [swap_with(after(grad_sends[k - 1], *normed_others), "seq", k) for k in range(1, seqs)]
    grad_input = call(
        functools.partial(input_back_body, seqs), shape_of((toks, width), f32)
    )(normed_parts[0], *normed_others, res, grad_middle, gains)

    high_cols = slice(0, hidden_cols), slice(hidden_cols, 2 * hidden_cols)
    for k in range(1, seqs):
        other = grads_from[k - 1].astype(f32)
        parts = other[:high, high_cols[0]], other[:high, high_cols[1]], other[high:]
        shards = [a + b for a, b in zip(shards, parts)]
    shard_gate, shard_up, shard_down = (s[None] for s in shards)

    y_sum = lax.psum_scatter(
        after(y_all, nears[turns[-1]]).reshape(-1, width), "blk", scatter_dimension=0, tiled=True,
        axis_index_groups=same_core,
    )
    y_sum = after(y_sum, shard_key, grad_input)
    block_out = (middle + y_sum.astype(f32)).astype(bf16)[None]
    return (
        block_out, grad_input[None], shard_query, shard_key, shard_value, shard_out.T, shard_router.T,
        shard_gain_one[0], shard_gain_two[0], shard_gate, shard_up, shard_down,
    )


def solution(mesh):
    both = ("seq", "blk")
    tokens, rows, cols, line = P("blk", "seq", None), P(both, None), P(None, both), P(both)
    return jax.shard_map(
        per_device,
        mesh=mesh,
        in_specs=(
            tokens, P(), tokens, rows, rows, rows, cols, rows, line, line, tokens, tokens, tokens, tokens,
        ),
        out_specs=(
            tokens, tokens, rows, rows, rows, cols, rows, line, line, tokens, tokens, tokens,
        ),
        check_vma=False,
    )
```

```python
import functools
import math

import jax
import jax.numpy as jnp
import numpy as np
from jax import lax
from jax.experimental import pallas as pl
from jax.experimental.pallas import tpu as pltpu
from jax.sharding import PartitionSpec as P

HEADS = 16
KV_HEADS = 8
HEAD_DIM = 64
LANES = 128

f32 = jnp.float32
bf16 = jnp.bfloat16
epsilon = 1e-06
neg_large = -1e30


def swap_with(value, axis, mask):
    if mask == 0:
        return value
    count = lax.axis_size(axis)
    return lax.ppermute(value, axis, [(i, i ^ mask) for i in range(count)])


def shifted(value, axis, steps):
    count = lax.axis_size(axis)
    leading, last = (max(0, -steps), min(count, count - steps))
    return lax.ppermute(value, axis, [(i, i + steps) for i in range(leading, last)])


def gather_seq(value):
    count = lax.axis_size("seq")
    me = lax.axis_index("seq")
    whole = jnp.zeros((count,) + value.shape, value.dtype)
    for k in range(count):
        piece = swap_with(value, "seq", k)
        whole = lax.dynamic_update_index_in_dim(whole, piece, me ^ k, 0)
    return whole


def after(value, *others):
    return lax.optimization_barrier((value,) + others)[0]


def gather_masks(groups):
    near = [0, 2, 4, 6]
    far = [4 * k + x for k in range(2, groups) for x in (0, 2)]
    return [m + c for half in (near, far) for c in (0, 1) for m in half]


def gather_rows(value):
    groups = lax.axis_size("blk") // 4
    near_z = swap_with(value, "blk", 4)
    far, last = [], value
    for k in range(2, groups):
        last = swap_with(after(value, last), "blk", 4 * k)
        far += [last, swap_with(last, "blk", 2)]
    near = jnp.concatenate(
        [value, swap_with(value, "blk", 2), near_z, swap_with(near_z, "blk", 2)], axis=0
    )
    far = jnp.concatenate(far, axis=0)
    return [near, swap_with(near, "blk", 1), far, swap_with(far, "blk", 1)]


def added(a, b):
    return (a.astype(f32) + b.astype(f32)).astype(a.dtype)


def scatter_core(keep, send):
    return added(keep, swap_with(send, "blk", 1))


def scatter_across(total):
    groups = lax.axis_size("blk") // 4
    parts = total.reshape(groups, 2, total.shape[0] // groups // 2, -1)
    return added(parts[:, 0], swap_with(parts[:, 1], "blk", 2))


def scatter_far(parts):
    return [swap_with(parts[k], "blk", 4 * k) for k in range(parts.shape[0] - 1, 0, -1)] + [parts[0]]


def call(body, out_shape, limit=16, flops=0, **options):
    many = isinstance(out_shape, (tuple, list))
    if "grid" not in options:
        space = pl.BlockSpec(memory_space=pltpu.VMEM)
        options.setdefault("out_specs", tuple(space for _ in out_shape) if many else space)
    sized = sum(math.prod(o.shape) * o.dtype.itemsize for o in (out_shape if many else [out_shape]))
    return pl.pallas_call(
        body,
        out_shape=out_shape,
        compiler_params=pltpu.CompilerParams(vmem_limit_bytes=limit * 1024 * 1024),
        cost_estimate=pl.CostEstimate(flops=flops, bytes_accessed=2 * sized, transcendentals=0),
        **options,
    )


def in_hbm(value):
    return pltpu.with_memory_space_constraint(value, pltpu.HBM)


def shape_of(dims, dtype):
    return jax.ShapeDtypeStruct(dims, dtype)


def lane_ids(shape):
    return lax.broadcasted_iota(jnp.int32, shape, len(shape) - 1)


def half_swap(tile):
    lanes = lane_ids(tile.shape)
    return jnp.where(lanes % 64 < 32, pltpu.roll(tile, 96, 1), pltpu.roll(tile, 32, 1))


def nt(a, b):
    return lax.dot_general(a, b, (((1,), (1,)), ((), ())), preferred_element_type=f32)


def tn(a, b):
    return lax.dot_general(a, b, (((0,), (0,)), ((), ())), preferred_element_type=f32)


def nn(a, b):
    return jnp.dot(a, b, preferred_element_type=f32)


def turned(tile, cos, sin, back=False):
    moved = half_swap(tile) * sin
    return tile * cos + (-moved if back else moved)


def key_tables(cos, sin):
    low = lane_ids(cos.shape) < HEAD_DIM
    return jnp.where(low, cos, 1.0), jnp.where(low, sin, 0.0)


def pack_body(seqs, dims, me_ref, *refs):
    q_cols, kv_cols, experts = dims
    sources, outs = refs[:7], refs[7 : 7 + seqs]
    held, sems = refs[7 + seqs : 14 + seqs], refs[14 + seqs]
    copies = [pltpu.make_async_copy(a, b, sems.at[i]) for i, (a, b) in enumerate(zip(sources, held))]
    for copy in copies:
        copy.start()
    for copy in copies:
        copy.wait()
    wq, wk, wv, wo, wr, gain_a, gain_m = held
    own_rows = wq.shape[0]
    lines = [wr[...].astype(f32), gain_a[...].astype(f32), gain_m[...].astype(f32)]
    lines.append(jnp.zeros((LANES - experts - 2, own_rows), f32))
    extra = jnp.concatenate(lines, axis=0).T.astype(bf16)
    half = kv_cols // 2
    for s in range(seqs):
        for k in range(seqs):

            @pl.when(me_ref[0] == s ^ k)
            def _(s=s, k=k):
                out = outs[k]
                out[:, :q_cols] = wq[:, s * q_cols : (s + 1) * q_cols]
                for g in range(half // HEAD_DIM):
                    span = slice(s * half + g * HEAD_DIM, s * half + (g + 1) * HEAD_DIM)
                    at = q_cols + 2 * g * HEAD_DIM
                    out[:, at : at + LANES] = jnp.concatenate([wk[:, span], wv[:, span]], axis=1)
                at = q_cols + kv_cols
                out[:, at : at + LANES] = extra
                out[:, at + LANES :] = wo[:, s * q_cols : (s + 1) * q_cols]


def restore_body(seqs, masks, experts, seq_ref, blk_ref, w0, w1, w2, w3, qkv_ref, router_ref, gain_ref):
    cols = qkv_ref.shape[1]
    blks = len(masks)
    unit = qkv_ref.shape[0] // blks
    own_rows = unit // seqs
    places = [(weight, r) for weight in (w0, w1, w2, w3) for r in range(0, weight.shape[0], unit)]
    for (weight, row), mask in zip(places, masks):
        for k in range(seqs):
            at = ((seq_ref[0] ^ k) * blks + (blk_ref[0] ^ mask)) * own_rows
            to = pl.ds(pl.multiple_of(at, own_rows), own_rows)
            span = slice(row + k * own_rows, row + (k + 1) * own_rows)
            qkv_ref[to, :] = weight[span, :cols]
            router_ref[to, :] = weight[span, cols:]
    pick = lax.broadcasted_iota(jnp.int32, (8, LANES), 0) + experts == lane_ids((8, LANES))
    gain_ref[...] = nt(pick.astype(bf16), router_ref[...])


def restore_out_body(seqs, blks, seq_ref, blk_ref, own, other, out_ref, sem):
    q_cols = out_ref.shape[1]
    own_rows = out_ref.shape[0] // blks // seqs
    copies = []
    for i in range(blks // 2):
        for c, weight in enumerate((own, other)):
            for k in range(seqs):
                blk = 2 * i + ((blk_ref[0] & 1) ^ c)
                at = ((seq_ref[0] ^ k) * blks + blk) * own_rows
                to = pl.ds(pl.multiple_of(at, own_rows), own_rows)
                part = weight.at[i, :, k * q_cols : (k + 1) * q_cols]
                copies.append(pltpu.make_async_copy(part, out_ref.at[to, :], sem.at[len(copies)]))
    for copy in copies:
        copy.start()
    for copy in copies:
        copy.wait()


def project_body(q_cols, kv_cols, gain_lane, x_ref, *refs):
    weights, (cos, sin, q_ref, kv_ref, normed_ref) = refs[:4], refs[4:]
    x = x_ref[...].astype(f32)
    inverse = lax.rsqrt(jnp.mean(x * x, axis=-1, keepdims=True) + epsilon)
    cols = q_cols + kv_cols
    pick = (lane_ids((8, LANES)) == gain_lane).astype(bf16)
    spans, at = [], 0
    for weight in weights:
        span = slice(at, at + weight.shape[0])
        gain = nt(pick, weight[:, cols : cols + LANES])[0:1, :]
        normed_ref[:, span] = (x[:, span] * inverse * gain).astype(bf16)
        spans.append(span)
        at += weight.shape[0]
    cos_q, sin_q = cos[...], sin[...]
    cos_k, sin_k = key_tables(cos_q, sin_q)
    wide = 2 * LANES if q_cols % (2 * LANES) == 0 and kv_cols % (2 * LANES) == 0 else LANES
    for first in range(0, cols, wide):
        both = None
        for span, weight in zip(spans, weights):
            term = nn(normed_ref[:, span], weight[:, first : first + wide])
            both = term if both is None else both + term
        for at in range(first, first + wide, LANES):
            tile = both[:, at - first : at - first + LANES]
            if at < q_cols:
                q_ref[:, at : at + LANES] = turned(tile, cos_q, sin_q).astype(bf16)
            else:
                kv_ref[:, at - q_cols : at - q_cols + LANES] = turned(tile, cos_k, sin_k).astype(bf16)


def visible_keys(meta_q, meta_k):
    mine = meta_q[...].T
    theirs = meta_k[...]
    return (theirs[1:2, :] <= mine[:, 1:2]) & (theirs[0:1, :] == mine[:, 0:1])


def attend_body(scale, q_ref, kv_ref, meta_q, meta_k, out_ref, lse_ref):
    visible = visible_keys(meta_q, meta_k)
    q = q_ref[...].astype(f32)
    kv = kv_ref[...]
    low = lane_ids(q.shape) < HEAD_DIM
    outs, lses = [], []
    for half in range(2):
        head = jnp.where(low, pltpu.roll(q, HEAD_DIM, 1) if half else q, 0.0).astype(bf16)
        scores = jnp.where(visible, nt(head, kv) * scale, neg_large)
        most = jnp.max(scores, axis=-1, keepdims=True)
        weights = jnp.exp(scores - most)
        total = jnp.sum(weights, axis=-1, keepdims=True)
        outs.append(nn(weights.astype(bf16), kv) / total)
        lses.append(most + jnp.log(total))
    out_ref[...] = jnp.where(low, pltpu.roll(outs[0], HEAD_DIM, 1), outs[1]).astype(bf16)
    lse_ref[...] = jnp.where(low, lses[0], lses[1])


def attend_back_body(
    scale, q_ref, kv_ref, mixed_ref, grad_ref, lse_ref, meta_q, meta_k, cos, sin, dq_ref, *outs
):
    outs, dkv_ref = outs[:-1], outs[-1]
    visible = visible_keys(meta_q, meta_k)
    q = q_ref[...].astype(f32)
    kv = kv_ref[...]
    grad = grad_ref[...].astype(f32)
    low = lane_ids(q.shape) < HEAD_DIM
    product = grad * mixed_ref[...].astype(f32)
    lse = lse_ref[...]
    dqs = []
    dkv = None
    for half in range(2):
        head = jnp.where(low, pltpu.roll(q, HEAD_DIM, 1) if half else q, 0.0).astype(bf16)
        grad_head = jnp.where(low, 0.0, grad if half else pltpu.roll(grad, HEAD_DIM, 1)).astype(bf16)
        delta = jnp.sum(jnp.where(low == (half == 0), product, 0.0), axis=-1, keepdims=True)
        lse_head = lse[:, HEAD_DIM * half : HEAD_DIM * half + 1]
        probs = jnp.where(visible, jnp.exp(nt(head, kv) * scale - lse_head), 0.0)
        grad_scores = (probs * (nt(grad_head, kv) - delta)).astype(bf16)
        dqs.append(nn(grad_scores, kv) * scale)
        term = tn(grad_scores, head) * scale + tn(probs.astype(bf16), grad_head)
        dkv = term if dkv is None else dkv + term
    dq = jnp.where(low, dqs[0], pltpu.roll(dqs[1], HEAD_DIM, 1)).astype(bf16).astype(f32)
    dq_ref[...] = turned(dq, cos[...], sin[...], back=True).astype(bf16)

    @pl.when(pl.program_id(1) == 0)
    def _():
        dkv_ref[...] = dkv

    @pl.when(pl.program_id(1) > 0)
    def _():
        dkv_ref[...] += dkv

    @pl.when(pl.program_id(1) == pl.num_programs(1) - 1)
    def _():
        at = 0
        for out in outs:
            out[...] = dkv_ref[at : at + out.shape[0], :].astype(out.dtype)
            at += out.shape[0]


def row_spans(width):
    near, far = 4, width // 2 - 4
    return ((0, near, 0, 0), (near, near, 1, 0), (2 * near, far, 0, near), (2 * near + far, far, 1, near))


def query_terms_body(blks, normed, gq, branch, mixed, pack, *outs):
    q_cols = gq.shape[1]
    unit = normed.shape[1] // blks
    for at, count, which, to in row_spans(blks):
        span, place = slice(at * unit, (at + count) * unit), slice(to * unit, (to + count) * unit)
        out = outs[which]
        out[place, :q_cols] = tn(normed[:, span], gq[...]).astype(bf16)
        out[place, q_cols : 2 * q_cols] = tn(branch[:, span], mixed[...]).astype(bf16)
        out[place, 2 * q_cols :] = pack[span, :]


def key_terms_body(blks, normed, gkv, *outs):
    unit = normed.shape[1] // blks
    for at, count, which, to in row_spans(blks):
        span, place = slice(at * unit, (at + count) * unit), slice(to * unit, (to + count) * unit)
        outs[which][place, :] = tn(normed[:, span], gkv[...]).astype(bf16)


def turn_back_body(count, seqs, *refs):
    own, others = refs[0], refs[1 : 1 + count]
    cos, sin, gq, weight = refs[1 + count : 5 + count]
    outs = refs[5 + count :]
    gkv_ref, parts = outs[0], outs[1:]
    cos_k, sin_k = key_tables(cos[...], sin[...])
    q_cols = gq.shape[1]
    for first in range(0, own.shape[1], LANES):
        span = slice(first, first + LANES)
        total = own[:, span]
        for other in others:
            total = total + other[:, span].astype(f32)
        gkv_ref[:, span] = turned(total.astype(bf16).astype(f32), cos_k, sin_k, back=True).astype(bf16)
    toks = parts[0].shape[0]
    for k in reversed(range(seqs)):
        span = slice(k * toks, (k + 1) * toks)
        grad = nt(gq[span, :], weight[:, :q_cols]) + nt(gkv_ref[span, :], weight[:, q_cols:])
        parts[k][...] = grad.astype(parts[k].dtype)


def to_row(column):
    count = column.shape[0]
    same = lax.broadcasted_iota(jnp.int32, (count, count), 0) == lane_ids((count, count))
    return jnp.sum(jnp.where(same, column, 0.0), axis=0, keepdims=True)


def finish_body(seqs, experts, me_ref, *refs):
    q_pieces, kv_pieces = refs[:seqs], refs[seqs : 2 * seqs]
    wq, wk, wv, gain = refs[2 * seqs : 2 * seqs + 4]
    query_ref, key_ref, value_ref, out_ref, router_ref, gain_one_ref, gain_two_ref = refs[2 * seqs + 4 :]
    q_cols = query_ref.shape[1] // seqs
    half = key_ref.shape[1] // seqs
    packed = None
    for k in range(seqs):
        part = q_pieces[k][:, 2 * q_cols :].astype(f32)
        packed = part if packed is None else packed + part
        for s in range(seqs):

            @pl.when(me_ref[0] == s ^ k)
            def _(s=s, k=k):
                span = slice(s * q_cols, (s + 1) * q_cols)
                query_ref[:, span] = q_pieces[k][:, :q_cols].astype(f32)
                out_ref[:, span] = q_pieces[k][:, q_cols : 2 * q_cols].astype(f32)
                for g in range(half // HEAD_DIM):
                    both = kv_pieces[k][:, 2 * g * HEAD_DIM : 2 * (g + 1) * HEAD_DIM].astype(f32)
                    span = slice(s * half + g * HEAD_DIM, s * half + (g + 1) * HEAD_DIM)
                    key_ref[:, span] = both[:, :HEAD_DIM]
                    value_ref[:, span] = both[:, HEAD_DIM:]

    router_ref[...] = packed.T[:experts, :]
    gain_two_ref[...] = to_row(packed[:, experts : experts + 1])
    weigh = lambda w, g: jnp.sum(w[...].astype(f32) * g[...], axis=1, keepdims=True)
    total = weigh(wq, query_ref) + weigh(wk, key_ref) + weigh(wv, value_ref)
    gain_one_ref[...] = to_row(total) / gain[...].astype(f32)


def middle_body(count, experts, *refs):
    parts = refs[:count]
    res, gains, router, routes, middle_ref, wide_ref, prob_ref = refs[count:]
    width = res.shape[1]
    middle = res[...].astype(f32)
    for part in parts:
        middle = middle + part[...].astype(f32)
    middle_ref[...] = middle
    inverse = lax.rsqrt(jnp.mean(middle * middle, axis=-1, keepdims=True) + epsilon)
    normed = (middle * inverse * gains[1:2, :]).astype(bf16)
    wide_ref[:, :width] = normed
    named = routes[...].astype(f32).T
    lanes = lane_ids((named.shape[0], LANES)).astype(f32)
    inside = lanes == named[:, 0:1]
    for i in range(1, named.shape[1]):
        inside = inside | (lanes == named[:, i : i + 1])
    logits = jnp.where(inside, nn(normed, router[...]), neg_large)
    raised = jnp.where(inside, jnp.exp(logits - jnp.max(logits, axis=-1, keepdims=True)), 0.0)
    prob = raised / jnp.sum(raised, axis=-1, keepdims=True)
    prob_ref[...] = prob
    high = prob.astype(bf16).astype(f32)
    rest = (prob - high).astype(bf16).astype(f32)
    wide_ref[:, width:] = (high + pltpu.roll(rest, experts, 1)).astype(bf16)


def expert_body(experts, k, seqs, me_ref, seq_ref, *refs):
    pieces, cot_all, packs = refs[:2], refs[2], refs[3 : 3 + 2 * seqs]
    outs, scratch = refs[-17:-10], refs[-10:]
    y_keep, y_send, x_all, hid_all, gg_all, geo_all, gi_ref = outs
    wide, cot_ref, y_ref, x_ref, hid_ref, gg_ref, geo_ref, wgu, wd, sems = scratch
    rows, width = cot_ref.shape[1], cot_ref.shape[2]
    high, low, cols = width // seqs, wd.shape[1] // seqs, wgu.shape[2] // 2
    me = me_ref[0]
    loads = [pltpu.make_async_copy(p, wide.at[i], sems.at[0, i]) for i, p in enumerate(pieces)]
    gates, downs = [], []
    for e in range(2):
        for j in range(seqs):
            at = pl.ds(pl.multiple_of((seq_ref[0] ^ j) * high, high), high)
            to = pl.ds(pl.multiple_of((seq_ref[0] ^ j) * low, low), low)
            pack = packs[e * seqs + j]
            gates.append(pltpu.make_async_copy(pack.at[:high, :], wgu.at[e, at, :], sems.at[1 + e, j]))
            downs.append(pltpu.make_async_copy(pack.at[high:, :], wd.at[e, to, :], sems.at[3 + e, j]))
    cots = [
        pltpu.make_async_copy(cot_all.at[(me ^ (4 * k + 2 * i)) // 2, :rows, :], cot_ref.at[i], sems.at[5, i])
        for i in range(2)
    ]
    for copies in (loads, gates[:seqs], downs[:seqs], cots, gates[seqs:], downs[seqs:]):
        for copy in copies:
            copy.start()
    for copy in loads:
        copy.wait()
    probs = [[], []]
    for i in range(2):
        x_ref[i * rows : (i + 1) * rows, :] = wide[i, :, :width]
        extra = wide[i, :, width:].astype(f32)
        lanes = lane_ids(extra.shape)
        for e in range(2):
            mine = (lanes == (me ^ e)) | (lanes == (me ^ e) + experts)
            probs[e].append(jnp.sum(jnp.where(mine, extra, 0.0), axis=-1, keepdims=True))
    x = x_ref[...]
    place = pl.ds(2 * k * rows, 2 * rows)
    stores = []

    def store(a, b, sem):
        stores.append(pltpu.make_async_copy(a, b, sem))
        stores[-1].start()

    store(x_ref, x_all.at[place, :], sems.at[8, 2])
    out, grad_in, marks, kept = None, None, [], []
    for e in range(2):
        prob = jnp.concatenate(probs[e], axis=0)
        for copy in gates[e * seqs : (e + 1) * seqs]:
            copy.wait()
        both = nn(x, wgu[e])
        gate, up = both[:, :cols], both[:, cols:]
        sigmoid = 1.0 / (1.0 + jnp.exp(-gate))
        active = gate * sigmoid
        hidden = (active * up).astype(bf16)
        hid_ref[e] = hidden
        store(hid_ref.at[e], hid_all.at[e, place, :], sems.at[6 + e, 0])
        for copy in downs[e * seqs : (e + 1) * seqs]:
            copy.wait()
        result = nn(hidden, wd[e]).astype(bf16).astype(f32)
        if e == 0:
            for copy in cots:
                copy.wait()
        final = jnp.concatenate([cot_ref[0], cot_ref[1]], axis=0).astype(f32)
        out = prob * result if out is None else out + prob * result
        marks.append(jnp.sum(result * final, axis=-1, keepdims=True))
        geo_ref[e] = (prob * final).astype(bf16)
        store(geo_ref.at[e], geo_all.at[e, place, :], sems.at[6 + e, 3])
        kept.append((gate, up, sigmoid, active))
    y_ref[...] = out.astype(bf16)
    store(y_ref.at[:rows, :], y_keep.at[k], sems.at[8, 0])
    store(y_ref.at[rows:, :], y_send.at[k], sems.at[8, 1])
    for e in range(2):
        gate, up, sigmoid, active = kept[e]
        grad_hidden = nt(geo_ref[e], wd[e])
        ggp = (grad_hidden * up * sigmoid * (1.0 + gate * (1.0 - sigmoid))).astype(bf16)
        gup = (grad_hidden * active).astype(bf16)
        gg_ref[e, :, :cols] = ggp
        gg_ref[e, :, cols:] = gup
        store(gg_ref.at[e], gg_all.at[e, place, :], sems.at[6 + e, 1])
        grad = nt(gg_ref[e], wgu[e])
        grad_in = grad if grad_in is None else grad_in + grad
    lanes = lane_ids((2 * rows, LANES))
    extra = jnp.zeros((2 * rows, LANES), f32)
    for e in range(2):
        mark = marks[e].astype(bf16).astype(f32)
        extra = extra + jnp.where(lanes == (me ^ e), mark, 0.0)
        extra = extra + jnp.where(lanes == (me ^ e) + experts, marks[e] - mark, 0.0)
    for i in range(2):
        span = slice(i * rows, (i + 1) * rows)
        gi_ref[i, :, :width] = grad_in[span, :].astype(bf16)
        gi_ref[i, :, width:] = extra[span, :].astype(bf16)
    for copy in stores:
        copy.wait()


def expert_grads_body(e, seqs, me_ref, *refs):
    sources, (x, gg, hid, geo, sems) = refs[:4], refs[-5:]
    outs = refs[4:-5]
    copies = [
        pltpu.make_async_copy(a if i == 0 else a.at[e], b, sems.at[i])
        for i, (a, b) in enumerate(zip(sources, (x, gg, hid, geo)))
    ]
    for copy in copies:
        copy.start()
    high, low = x.shape[1] // seqs, hid.shape[1] // seqs
    for i, (rows, a, b) in enumerate(((slice(0, high), x, gg), (slice(high, high + low), hid, geo))):
        for copy in copies[2 * i : 2 * i + 2]:
            copy.wait()
        size = rows.stop - rows.start
        for s in range(seqs):
            k = me_ref[0] ^ s
            part = tn(a[:, s * size : (s + 1) * size], b[...])
            if e == 1:
                outs[0][k, rows, :] = part.astype(bf16)
            else:
                part = part + outs[0][k, rows, :].astype(f32)

                @pl.when(k == 0)
                def _(part=part, i=i):
                    outs[1 + i][...] = part

                @pl.when(k != 0)
                def _(part=part, i=i):
                    outs[3 + i][k - 1] = part.astype(bf16)


def middle_back_body(count, experts, *refs):
    parts = refs[:count]
    middle_ref, prob_ref, cot, gains, router, grad_ref, branch_ref, pack_ref = refs[count:]
    width = cot.shape[1]
    gain = gains[1:2, :]
    total = parts[0][...].astype(f32)
    for part in parts[1:]:
        total = total + part[...].astype(f32)
    extra = total[:, width:]
    marks = extra + pltpu.roll(extra, LANES - experts, 1)
    prob = prob_ref[...]
    weighted = jnp.where(prob > 0, prob * marks, 0.0)
    spread = jnp.sum(weighted, axis=-1, keepdims=True)
    grad_logits = weighted - prob * spread
    high = grad_logits.astype(bf16)
    rest = (grad_logits - high.astype(f32)).astype(bf16)
    grad_normed = total[:, :width] + nt(high, router[...]) + nt(rest, router[...])
    middle = middle_ref[...]
    inverse = lax.rsqrt(jnp.mean(middle * middle, axis=-1, keepdims=True) + epsilon)
    unit = middle * inverse
    scaled = grad_normed * gain
    grad = cot[...].astype(f32) + inverse * (
        scaled - unit * jnp.mean(scaled * unit, axis=-1, keepdims=True)
    )
    grad_ref[...] = grad
    branch_ref[...] = grad.astype(bf16)
    normed = (unit * gain).astype(bf16)
    pack = tn(high, normed) + tn(rest, normed)
    gain_row = jnp.sum(grad_normed * unit, axis=0, keepdims=True)
    at_gain = lax.broadcasted_iota(jnp.int32, pack.shape, 0) == experts
    pack_ref[...] = jnp.where(at_gain, gain_row, pack).astype(bf16)


def input_back_body(count, *refs):
    parts = refs[:count]
    res, grad_middle, gains, out_ref = refs[count:]
    grad_normed = parts[0][...].astype(f32)
    for part in parts[1:]:
        grad_normed = grad_normed + part[...].astype(f32)
    x = res[...].astype(f32)
    inverse = lax.rsqrt(jnp.mean(x * x, axis=-1, keepdims=True) + epsilon)
    unit = x * inverse
    scaled = grad_normed * gains[0:1, :]
    out_ref[...] = grad_middle[...] + inverse * (
        scaled - unit * jnp.mean(scaled * unit, axis=-1, keepdims=True)
    )


def per_device(
    residual, segments, routes, w_query, w_key, w_value, w_out, w_router, attn_gain, moe_gain,
    w_gate, w_up, w_down, cotangent,
):
    seqs, blks = lax.axis_size("seq"), lax.axis_size("blk")
    seq_me, blk_me = lax.axis_index("seq"), lax.axis_index("blk")
    toks, width = residual.shape[1], residual.shape[2]
    rows = toks * seqs
    experts = blks
    own_rows = w_query.shape[0]
    kv_local = KV_HEADS // seqs
    q_cols, kv_cols = HEADS // seqs * HEAD_DIM, kv_local * 2 * HEAD_DIM
    cols = q_cols + kv_cols
    scale = HEAD_DIM ** (-0.5)
    tokens = segments.shape[0]
    doc_most = tokens // 8
    hops = min(blks - 1, -(-(doc_most - 1) // rows))
    behind = hops * rows
    keys = behind + rows
    groups = blks // 4
    masks = gather_masks(groups)
    res = residual[0]
    cot = cotangent[0]
    vmem = pl.BlockSpec(memory_space=pltpu.VMEM)
    smem = pl.BlockSpec(memory_space=pltpu.SMEM)
    seq_scalar = jnp.reshape(seq_me, (1,)).astype(jnp.int32)
    blk_scalar = jnp.reshape(blk_me, (1,)).astype(jnp.int32)
    hbm = pl.BlockSpec(memory_space=pltpu.HBM)
    gain_row = attn_gain[None, :]

    weight_dims = (own_rows, cols + LANES + q_cols)
    sources = (w_query, w_key, w_value, w_out.T, w_router.T, gain_row, moe_gain[None, :])
    weight_parts = call(
        functools.partial(pack_body, seqs, (q_cols, kv_cols, experts)),
        tuple(shape_of(weight_dims, bf16) for _ in range(seqs)),
        in_specs=[smem] + [hbm] * 7,
        scratch_shapes=[pltpu.VMEM(a.shape, a.dtype) for a in sources] + [pltpu.SemaphoreType.DMA((7,))],
    )(seq_scalar, *[in_hbm(a) for a in sources])
    weight_both = jnp.concatenate([swap_with(p, "seq", k) for k, p in enumerate(weight_parts)], axis=0)
    weight_own = weight_both[:, : cols + LANES]
    late_res = after(res, weight_both)
    res_parts = [res] + [swap_with(late_res, "seq", k) for k in range(1, seqs)]
    weight_rel = gather_rows(weight_own)
    same_core = [[2 * i + c for i in range(blks // 2)] for c in range(2)]
    joint = seqs * own_rows * q_cols // width
    out_own = weight_both[:, cols + LANES :].reshape(seqs, own_rows, q_cols)
    out_own = jnp.concatenate([out_own[k] for k in range(seqs)], axis=1).reshape(joint, width)
    both_all = lax.all_gather(
        jnp.concatenate([cot, out_own], axis=0), "blk", axis=0, axis_index_groups=same_core
    )
    gate, up, down, *_ = lax.optimization_barrier((w_gate[0], w_up[0], w_down[0], *res_parts))
    expert_pack = jnp.concatenate([jnp.concatenate([gate, up], axis=1), down], axis=0)
    packs = [swap_with(expert_pack, "seq", k) for k in range(seqs)]
    seq_me, blk_me = after(seq_me, weight_own), after(blk_me, weight_own)

    spot = np.arange(width)
    place, inner = spot // (seqs * own_rows), spot % (seqs * own_rows)
    mask_row = jnp.asarray(np.asarray(masks)[place], jnp.int32)
    seq_row = jnp.asarray(inner // own_rows, jnp.int32)
    source = ((seq_me ^ seq_row) * blks + (blk_me ^ mask_row)) * own_rows + (inner % own_rows)
    order = (lax.broadcasted_iota(jnp.int32, (width, width), 0) == source[None, :]).astype(bf16)

    turn = lambda i: (seq_me ^ (i // toks % seqs)) * toks + i % toks
    half_dim = HEAD_DIM // 2
    lanes = lane_ids((rows, LANES))
    inverse = jnp.exp((lanes % half_dim).astype(f32) * (-2.0 * math.log(10000.0) / HEAD_DIM))
    position = blk_me * rows + turn(lax.broadcasted_iota(jnp.int32, (rows, LANES), 0))
    angles = position.astype(f32) * inverse
    cos, sin = jnp.cos(angles), jnp.where(lanes % HEAD_DIM < half_dim, -1.0, 1.0) * jnp.sin(angles)
    key_ids = jnp.arange(keys, dtype=jnp.int32)
    key_places = key_ids // rows * rows - behind + turn(key_ids % rows)
    seg_padded = jnp.concatenate([jnp.full((behind,), -1, jnp.int32), segments])
    seg_near = lax.dynamic_slice_in_dim(seg_padded, blk_me * rows, keys).reshape(hops + 1, seqs, toks)
    seg_keys = jnp.stack(
        [lax.dynamic_index_in_dim(seg_near, seq_me ^ k, 1, keepdims=False) for k in range(seqs)], axis=1
    ).reshape(keys)
    meta = jnp.concatenate(
        [seg_keys.astype(f32)[None], key_places.astype(f32)[None], jnp.zeros((6, keys), f32)], axis=0
    )

    x_rel = jnp.concatenate([nn(part, order).astype(bf16) for part in res_parts], axis=0)
    q_all, kv_own, normed_rel = call(
        functools.partial(project_body, q_cols, kv_cols, experts),
        (shape_of((rows, q_cols), bf16), shape_of((rows, kv_cols), bf16), shape_of((rows, width), bf16)),
    )(x_rel, *weight_rel, cos, sin)
    if own_rows % 16 == 0:
        qkv_abs, router_abs, gains = call(
            functools.partial(restore_body, seqs, masks, experts),
            (shape_of((width, cols), bf16), shape_of((width, LANES), bf16), shape_of((8, width), f32)),
            in_specs=[smem, smem] + [vmem] * 4,
        )(seq_scalar, blk_scalar, *weight_rel)
    else:
        weight_abs = nn(order, jnp.concatenate(weight_rel, axis=0)).astype(bf16)
        qkv_abs, router_abs = weight_abs[:, :cols], weight_abs[:, cols:]
        gains = jnp.pad(router_abs[:, experts : experts + 2].astype(f32).T, ((0, 6), (0, 0)))

    kv_keys = jnp.concatenate([shifted(kv_own, "blk", n) for n in range(hops, 0, -1)] + [kv_own], axis=0)
    step = min(rows, 256)
    grid = (kv_local, rows // step)
    row_block = pl.BlockSpec((step, LANES), lambda g, i: (i, g))
    key_block = pl.BlockSpec((keys, LANES), lambda g, i: (0, g))
    meta_q_block = pl.BlockSpec((8, step), lambda g, i: (0, behind // step + i))
    meta_k_block = pl.BlockSpec((8, keys), lambda g, i: (0, 0))
    table_block = pl.BlockSpec((step, LANES), lambda g, i: (i, 0))
    attend_limit = 8 + step * keys * 40 // 1024 // 1024
    mixed, lse = call(
        functools.partial(attend_body, scale),
        (shape_of((rows, q_cols), bf16), shape_of((rows, q_cols), f32)),
        limit=attend_limit,
        grid=grid,
        in_specs=[row_block, key_block, meta_q_block, meta_k_block],
        out_specs=(row_block, row_block),
    )(q_all, kv_keys, meta, meta)

    packs += [swap_with(after(p, mixed), "blk", 1) for p in packs]

    out_same = after(both_all[:, toks:], mixed)
    out_pair = [out_same, swap_with(out_same, "blk", 1)]
    if own_rows % 16 == 0:
        out_abs = call(
            functools.partial(restore_out_body, seqs, blks),
            shape_of((width, q_cols), bf16),
            in_specs=[smem, smem, hbm, hbm],
            scratch_shapes=[pltpu.SemaphoreType.DMA((blks * seqs,))],
        )(seq_scalar, blk_scalar, *[in_hbm(a) for a in out_pair])
    else:
        odd = blk_me % 2 == 1
        pair = jnp.stack([jnp.where(odd, out_pair[1 - c], out_pair[c]) for c in range(2)], axis=1)
        out_parts = pair.reshape(blks, own_rows, seqs, q_cols).swapaxes(1, 2)
        out_abs = jnp.stack(
            [lax.dynamic_index_in_dim(out_parts, seq_me ^ k, 1, keepdims=False) for k in range(seqs)]
        ).reshape(width, q_cols)

    branch = nt(mixed, out_abs)
    branch_parts = [branch[:toks]] + [
        swap_with(branch[k * toks : (k + 1) * toks].astype(bf16), "seq", k) for k in range(1, seqs)
    ]
    middle, wide, prob = call(
        functools.partial(middle_body, seqs, experts),
        (shape_of((toks, width), f32), shape_of((toks, width + LANES), bf16), shape_of((toks, LANES), f32)),
    )(*branch_parts, res, gains, router_abs, routes[0].T)

    hidden_cols = w_gate.shape[2]
    held = 2 * toks * groups
    buffers = [
        (groups, toks, width), (groups, toks, width), (held, width), (2, held, hidden_cols), (2, held, 2 * hidden_cols),
        (2, held, width),
    ]

    def run_experts(k, pieces, before):
        operands = [*pieces, both_all, *packs, *before]
        fixed = len(operands) - len(before) + 2
        return call(
            functools.partial(expert_body, experts, k, seqs),
            tuple(pltpu.HBM(d, bf16) for d in buffers) + (shape_of((2, toks, width + LANES), bf16),),
            limit=24,
            flops=48 * toks * width * hidden_cols,
            in_specs=[smem, smem] + [hbm] * len(operands),
            out_specs=(hbm,) * len(buffers) + (vmem,),
            input_output_aliases={fixed + i: i for i in range(len(before))},
            scratch_shapes=[
                pltpu.VMEM((2, toks, width + LANES), bf16),
                pltpu.VMEM((2, toks, width), bf16),
                pltpu.VMEM((2 * toks, width), bf16),
                pltpu.VMEM((2 * toks, width), bf16),
                pltpu.VMEM((2, 2 * toks, hidden_cols), bf16),
                pltpu.VMEM((2, 2 * toks, 2 * hidden_cols), bf16),
                pltpu.VMEM((2, 2 * toks, width), bf16),
                pltpu.VMEM((2, width, 2 * hidden_cols), bf16),
                pltpu.VMEM((2, hidden_cols, width), bf16),
                pltpu.SemaphoreType.DMA((9, max(4, seqs))),
            ],
        )(blk_scalar, seq_scalar, *[in_hbm(a) for a in operands])

    turns = [1] + list(range(groups - 1, 1, -1)) + [0]
    far = {0: wide}
    last = wide
    for k in turns[:-1]:
        far[k] = swap_with(after(wide, last), "blk", 4 * k)
        last = far[k] if k > 1 else last
    across = {k: swap_with(far[k], "blk", 2) for k in far}
    grads, nears, before = {}, {}, []
    for i, k in enumerate(turns):
        holds = [prob]
        if i > 0:
            holds.append(grads[turns[i - 1]])
        if i > 1:
            n = turns[i - 2]
            nears[n] = added(grads[n][0], swap_with(grads[n][1], "blk", 2))
            holds.append(nears[n])
        *before, grads[k] = run_experts(k, [after(far[k], *holds), across[k]], before)
    for n in turns[-2:]:
        nears[n] = added(grads[n][0], swap_with(grads[n][1], "blk", 2))
    grad_parts = [swap_with(nears[k], "blk", 4 * k) for k in turns]
    y_keep, y_send, x_all, hid_all, gg_all, geo_all = before
    tdot = lambda a, b: lax.dot_general(a, b, (((0,), (0,)), ((), ())), preferred_element_type=f32)

    grad_middle, grad_branch, pack = call(
        functools.partial(middle_back_body, groups, experts),
        (shape_of((toks, width), f32), shape_of((toks, width), bf16), shape_of((LANES, width), bf16)),
    )(*grad_parts, middle, prob, cot, gains, router_abs)

    high, low = width // seqs, hidden_cols // seqs

    x_all = after(x_all, nears[turns[-1]])
    y_far = swap_with(after(y_send, grad_branch), "blk", 2)

    def expert_grads(e, outs, *others):
        operands = [in_hbm(a) for a in (x_all, gg_all, hid_all, geo_all)]
        return call(
            functools.partial(expert_grads_body, e, seqs),
            outs,
            limit=10 + 7 * held // 1024,
            flops=6 * held * width * hidden_cols,
            in_specs=[smem] + [hbm] * 4 + [vmem] * len(others),
            scratch_shapes=[
                pltpu.VMEM((held, width), bf16), pltpu.VMEM((held, 2 * hidden_cols), bf16),
                pltpu.VMEM((held, hidden_cols), bf16), pltpu.VMEM((held, width), bf16),
                pltpu.SemaphoreType.DMA((4,)),
            ],
        )(seq_scalar, *operands, *others)

    partner_terms = expert_grads(1, shape_of((seqs, high + low, width), bf16))
    branch_others = [swap_with(grad_branch, "seq", k) for k in range(1, seqs)]
    branch_all = after(jnp.concatenate([grad_branch] + branch_others, axis=0), partner_terms)
    grad_mixed = nn(branch_all, out_abs).astype(bf16)
    block_spec = pl.BlockSpec((rows, LANES), lambda g, i: (0, g))
    gq_pre, *grad_kv = call(
        functools.partial(attend_back_body, scale),
        (shape_of((rows, q_cols), bf16),)
        + (shape_of((rows, kv_cols), bf16),) * hops
        + (shape_of((rows, kv_cols), f32),),
        limit=attend_limit,
        grid=grid,
        flops=24 * rows * keys * q_cols,
        in_specs=[row_block, key_block, row_block, row_block, row_block, meta_q_block, meta_k_block,
                  table_block, table_block],
        out_specs=(row_block,) + (block_spec,) * (hops + 1),
        scratch_shapes=[pltpu.VMEM((keys, LANES), f32)],
    )(q_all, kv_keys, mixed, grad_mixed, lse, meta, meta, cos, sin)
    returned = [shifted(grad_kv[hops - n], "blk", -n) for n in range(1, hops + 1)]
    spare = max(1, seqs - 1)
    gg_own, down_own, gg_sends, down_sends = expert_grads(
        0,
        (shape_of((high, 2 * hidden_cols), f32), shape_of((low, width), f32),
         shape_of((spare, high, 2 * hidden_cols), bf16), shape_of((spare, low, width), bf16)),
        after(swap_with(partner_terms, "blk", 1), gq_pre),
    )
    down_from = [swap_with(down_sends[k - 1], "seq", k) for k in range(1, seqs)]
    y_near = added(y_keep, y_far)
    branch_rel = nn(branch_all, order).astype(bf16)
    pack_rel = tdot(order, pack.T).astype(bf16)
    unit = seqs * own_rows
    q_terms = call(
        functools.partial(query_terms_body, blks),
        (shape_of((width // 2, 2 * q_cols + LANES), bf16),) * 2,
    )(normed_rel, gq_pre, branch_rel, mixed, pack_rel)

    def for_this_row(terms):
        total = sum(t.astype(f32) for t in terms).astype(bf16)
        return [swap_with(total[k * own_rows : (k + 1) * own_rows], "seq", k) for k in range(seqs)]

    q_total = scatter_core(*q_terms)
    q_stage = scatter_across(after(q_total, gg_sends, *returned))
    own_kv = after(grad_kv[-1], q_total, gg_sends)

    gkv_pre, *normed_parts = call(
        functools.partial(turn_back_body, hops, seqs),
        (shape_of((rows, kv_cols), bf16),)
        + tuple(shape_of((toks, width), bf16 if k else f32) for k in range(seqs)),
    )(own_kv, *returned, cos, sin, gq_pre, qkv_abs)
    kv_terms = call(
        functools.partial(key_terms_body, blks), (shape_of((width // 2, kv_cols), bf16),) * 2
    )(normed_rel, gkv_pre)
    q_pieces = for_this_row(scatter_far(q_stage))
    gg_from = [swap_with(gg_sends[k - 1], "seq", k) for k in range(1, seqs)]
    kv_stage = scatter_across(scatter_core(*kv_terms))
    kv_pieces = for_this_row(scatter_far(kv_stage))
    shard_query, shard_key, shard_value, shard_out, shard_router, shard_gain_one, shard_gain_two = call(
        functools.partial(finish_body, seqs, experts),
        (shape_of(w_query.shape, f32), shape_of(w_key.shape, f32), shape_of(w_value.shape, f32),
         shape_of(w_out.shape[::-1], f32), shape_of(w_router.shape[::-1], f32),
         shape_of((1, own_rows), f32), shape_of((1, own_rows), f32)),
        in_specs=[smem] + [vmem] * (2 * seqs + 4),
    )(seq_scalar, *q_pieces, *kv_pieces, w_query, w_key, w_value, gain_row)
    normed_others = [swap_with(p, "seq", k) for k, p in enumerate(normed_parts) if k]
    grad_input = call(
        functools.partial(input_back_body, seqs), shape_of((toks, width), f32)
    )(normed_parts[0], *normed_others, res, grad_middle, gains)

    for k in range(1, seqs):
        gg_own = gg_own + gg_from[k - 1].astype(f32)
        down_own = down_own + down_from[k - 1].astype(f32)
    shard_gate, shard_up = gg_own[None, :, :hidden_cols], gg_own[None, :, hidden_cols:]
    shard_down = down_own[None]

    y_sum = middle + y_near[0].astype(f32)
    for k in range(1, groups):
        y_sum = y_sum + swap_with(after(y_near[k], *returned), "blk", 4 * k).astype(f32)
    block_out = y_sum.astype(bf16)[None]
    return (
        block_out, grad_input[None], shard_query, shard_key, shard_value, shard_out.T, shard_router.T,
        shard_gain_one[0], shard_gain_two[0], shard_gate, shard_up, shard_down,
    )


def solution(mesh):
    both = ("seq", "blk")
    tokens, rows, cols, line = P("blk", "seq", None), P(both, None), P(None, both), P(both)
    return jax.shard_map(
        per_device,
        mesh=mesh,
        in_specs=(
            tokens, P(), tokens, rows, rows, rows, cols, rows, line, line, tokens, tokens, tokens, tokens,
        ),
        out_specs=(
            tokens, tokens, rows, rows, rows, cols, rows, line, line, tokens, tokens, tokens,
        ),
        check_vma=False,
    )
```

```python
import functools
import math

import jax
import jax.numpy as jnp
import numpy as np
from jax import lax
from jax.experimental import pallas as pl
from jax.experimental.pallas import tpu as pltpu
from jax.sharding import PartitionSpec as P

HEADS = 16
KV_HEADS = 8
HEAD_DIM = 64
LANES = 128

f32 = jnp.float32
bf16 = jnp.bfloat16
epsilon = 1e-06
neg_large = -1e30


def swap_with(value, axis, mask):
    if mask == 0:
        return value
    count = lax.axis_size(axis)
    return lax.ppermute(value, axis, [(i, i ^ mask) for i in range(count)])


def shifted(value, axis, steps):
    count = lax.axis_size(axis)
    leading, last = (max(0, -steps), min(count, count - steps))
    return lax.ppermute(value, axis, [(i, i + steps) for i in range(leading, last)])


def gather_seq(value):
    count = lax.axis_size("seq")
    me = lax.axis_index("seq")
    whole = jnp.zeros((count,) + value.shape, value.dtype)
    for k in range(count):
        piece = swap_with(value, "seq", k)
        whole = lax.dynamic_update_index_in_dim(whole, piece, me ^ k, 0)
    return whole


def after(value, *others):
    return lax.optimization_barrier((value,) + others)[0]


def gather_masks(groups):
    near = [0, 2, 4, 6]
    far = [4 * k + x for k in range(2, groups) for x in (0, 2)]
    return [m + c for half in (near, far) for c in (0, 1) for m in half]


def gather_rows(value):
    groups = lax.axis_size("blk") // 4
    near_z = swap_with(value, "blk", 4)
    far, last = [], value
    for k in range(2, groups):
        last = swap_with(after(value, last), "blk", 4 * k)
        far += [last, swap_with(last, "blk", 2)]
    near = jnp.concatenate(
        [value, swap_with(value, "blk", 2), near_z, swap_with(near_z, "blk", 2)], axis=0
    )
    far = jnp.concatenate(far, axis=0)
    return [near, swap_with(near, "blk", 1), far, swap_with(far, "blk", 1)]


def added(a, b):
    return (a.astype(f32) + b.astype(f32)).astype(a.dtype)


def scatter_core(keep, send):
    return added(keep, swap_with(send, "blk", 1))


def scatter_across(total):
    groups = lax.axis_size("blk") // 4
    parts = total.reshape(groups, 2, total.shape[0] // groups // 2, -1)
    return added(parts[:, 0], swap_with(parts[:, 1], "blk", 2))


def scatter_far(parts):
    return [swap_with(parts[k], "blk", 4 * k) for k in range(parts.shape[0] - 1, 0, -1)] + [parts[0]]


def call(body, out_shape, limit=16, flops=0, **options):
    many = isinstance(out_shape, (tuple, list))
    if "grid" not in options:
        space = pl.BlockSpec(memory_space=pltpu.VMEM)
        options.setdefault("out_specs", tuple(space for _ in out_shape) if many else space)
    sized = sum(math.prod(o.shape) * o.dtype.itemsize for o in (out_shape if many else [out_shape]))
    return pl.pallas_call(
        body,
        out_shape=out_shape,
        compiler_params=pltpu.CompilerParams(vmem_limit_bytes=limit * 1024 * 1024),
        cost_estimate=pl.CostEstimate(flops=flops, bytes_accessed=2 * sized, transcendentals=0),
        **options,
    )


def in_hbm(value):
    return pltpu.with_memory_space_constraint(value, pltpu.HBM)


def shape_of(dims, dtype):
    return jax.ShapeDtypeStruct(dims, dtype)


def lane_ids(shape):
    return lax.broadcasted_iota(jnp.int32, shape, len(shape) - 1)


def half_swap(tile):
    lanes = lane_ids(tile.shape)
    return jnp.where(lanes % 64 < 32, pltpu.roll(tile, 96, 1), pltpu.roll(tile, 32, 1))


def nt(a, b):
    return lax.dot_general(a, b, (((1,), (1,)), ((), ())), preferred_element_type=f32)


def tn(a, b):
    return lax.dot_general(a, b, (((0,), (0,)), ((), ())), preferred_element_type=f32)


def nn(a, b):
    return jnp.dot(a, b, preferred_element_type=f32)


def turned(tile, cos, sin, back=False):
    moved = half_swap(tile) * sin
    return tile * cos + (-moved if back else moved)


def key_tables(cos, sin):
    low = lane_ids(cos.shape) < HEAD_DIM
    return jnp.where(low, cos, 1.0), jnp.where(low, sin, 0.0)


def pack_body(seqs, dims, me_ref, *refs):
    q_cols, kv_cols, experts = dims
    sources, outs = refs[:7], refs[7 : 7 + seqs]
    held, sems = refs[7 + seqs : 14 + seqs], refs[14 + seqs]
    copies = [pltpu.make_async_copy(a, b, sems.at[i]) for i, (a, b) in enumerate(zip(sources, held))]
    for copy in copies:
        copy.start()
    for copy in copies:
        copy.wait()
    wq, wk, wv, wo, wr, gain_a, gain_m = held
    own_rows = wq.shape[0]
    lines = [wr[...].astype(f32), gain_a[...].astype(f32), gain_m[...].astype(f32)]
    lines.append(jnp.zeros((LANES - experts - 2, own_rows), f32))
    extra = jnp.concatenate(lines, axis=0).T.astype(bf16)
    half = kv_cols // 2
    for s in range(seqs):
        for k in range(seqs):

            @pl.when(me_ref[0] == s ^ k)
            def _(s=s, k=k):
                out = outs[k]
                out[:, :q_cols] = wq[:, s * q_cols : (s + 1) * q_cols]
                for g in range(half // HEAD_DIM):
                    span = slice(s * half + g * HEAD_DIM, s * half + (g + 1) * HEAD_DIM)
                    at = q_cols + 2 * g * HEAD_DIM
                    out[:, at : at + LANES] = jnp.concatenate([wk[:, span], wv[:, span]], axis=1)
                at = q_cols + kv_cols
                out[:, at : at + LANES] = extra
                out[:, at + LANES :] = wo[:, s * q_cols : (s + 1) * q_cols]


def restore_body(seqs, masks, experts, seq_ref, blk_ref, w0, w1, w2, w3, qkv_ref, router_ref, gain_ref):
    cols = qkv_ref.shape[1]
    blks = len(masks)
    unit = qkv_ref.shape[0] // blks
    own_rows = unit // seqs
    places = [(weight, r) for weight in (w0, w1, w2, w3) for r in range(0, weight.shape[0], unit)]
    for (weight, row), mask in zip(places, masks):
        for k in range(seqs):
            at = ((seq_ref[0] ^ k) * blks + (blk_ref[0] ^ mask)) * own_rows
            to = pl.ds(pl.multiple_of(at, own_rows), own_rows)
            span = slice(row + k * own_rows, row + (k + 1) * own_rows)
            qkv_ref[to, :] = weight[span, :cols]
            router_ref[to, :] = weight[span, cols:]
    pick = lax.broadcasted_iota(jnp.int32, (8, LANES), 0) + experts == lane_ids((8, LANES))
    gain_ref[...] = nt(pick.astype(bf16), router_ref[...])


def restore_out_body(seqs, blks, seq_ref, blk_ref, own, other, out_ref, sem):
    q_cols = out_ref.shape[1]
    own_rows = out_ref.shape[0] // blks // seqs
    copies = []
    for i in range(blks // 2):
        for c, weight in enumerate((own, other)):
            for k in range(seqs):
                blk = 2 * i + ((blk_ref[0] & 1) ^ c)
                at = ((seq_ref[0] ^ k) * blks + blk) * own_rows
                to = pl.ds(pl.multiple_of(at, own_rows), own_rows)
                part = weight.at[i, :, k * q_cols : (k + 1) * q_cols]
                copies.append(pltpu.make_async_copy(part, out_ref.at[to, :], sem.at[len(copies)]))
    for copy in copies:
        copy.start()
    for copy in copies:
        copy.wait()


def project_body(q_cols, kv_cols, gain_lane, x_ref, *refs):
    weights, (cos, sin, q_ref, kv_ref, normed_ref) = refs[:4], refs[4:]
    x = x_ref[...].astype(f32)
    inverse = lax.rsqrt(jnp.mean(x * x, axis=-1, keepdims=True) + epsilon)
    cols = q_cols + kv_cols
    pick = (lane_ids((8, LANES)) == gain_lane).astype(bf16)
    spans, at = [], 0
    for weight in weights:
        span = slice(at, at + weight.shape[0])
        gain = nt(pick, weight[:, cols : cols + LANES])[0:1, :]
        normed_ref[:, span] = (x[:, span] * inverse * gain).astype(bf16)
        spans.append(span)
        at += weight.shape[0]
    cos_q, sin_q = cos[...], sin[...]
    cos_k, sin_k = key_tables(cos_q, sin_q)
    wide = 2 * LANES if q_cols % (2 * LANES) == 0 and kv_cols % (2 * LANES) == 0 else LANES
    for first in range(0, cols, wide):
        both = None
        for span, weight in zip(spans, weights):
            term = nn(normed_ref[:, span], weight[:, first : first + wide])
            both = term if both is None else both + term
        for at in range(first, first + wide, LANES):
            tile = both[:, at - first : at - first + LANES]
            if at < q_cols:
                q_ref[:, at : at + LANES] = turned(tile, cos_q, sin_q).astype(bf16)
            else:
                kv_ref[:, at - q_cols : at - q_cols + LANES] = turned(tile, cos_k, sin_k).astype(bf16)


def hide_keys(meta_q, meta_k, bias_ref):
    @pl.when((pl.program_id(0) == 0) | (pl.num_programs(1) > 1))
    def _():
        mine = meta_q[...].T
        theirs = meta_k[...]
        visible = (theirs[1:2, :] <= mine[:, 1:2]) & (theirs[0:1, :] == mine[:, 0:1])
        bias_ref[...] = jnp.where(visible, 0.0, neg_large)


def attend_body(scale, q_ref, kv_ref, meta_q, meta_k, out_ref, lse_ref, bias_ref):
    hide_keys(meta_q, meta_k, bias_ref)
    q = q_ref[...].astype(f32) * scale
    kv = kv_ref[...]
    low = lane_ids(q.shape) < HEAD_DIM
    outs, lses = [], []
    for half in range(2):
        head = jnp.where(low, pltpu.roll(q, HEAD_DIM, 1) if half else q, 0.0).astype(bf16)
        scores = nt(head, kv) + bias_ref[...]
        most = jnp.max(scores, axis=-1, keepdims=True)
        weights = jnp.exp(scores - most)
        total = jnp.sum(weights, axis=-1, keepdims=True)
        outs.append(nn(weights.astype(bf16), kv) / total)
        lses.append(most + jnp.log(total))
    out_ref[...] = jnp.where(low, pltpu.roll(outs[0], HEAD_DIM, 1), outs[1]).astype(bf16)
    lse_ref[...] = jnp.where(low, lses[0], lses[1])


def attend_back_body(
    scale, q_ref, kv_ref, mixed_ref, grad_ref, lse_ref, meta_q, meta_k, cos, sin, dq_ref, *outs
):
    outs, dkv_ref, bias_ref = outs[:-2], outs[-2], outs[-1]
    hide_keys(meta_q, meta_k, bias_ref)
    q = q_ref[...].astype(f32) * scale
    kv = kv_ref[...]
    grad = grad_ref[...].astype(f32)
    low = lane_ids(q.shape) < HEAD_DIM
    product = grad * mixed_ref[...].astype(f32)
    lse = lse_ref[...]
    dqs = []
    dkv = None
    for half in range(2):
        head = jnp.where(low, pltpu.roll(q, HEAD_DIM, 1) if half else q, 0.0).astype(bf16)
        grad_head = jnp.where(low, 0.0, grad if half else pltpu.roll(grad, HEAD_DIM, 1)).astype(bf16)
        delta = jnp.sum(jnp.where(low == (half == 0), product, 0.0), axis=-1, keepdims=True)
        lse_head = lse[:, HEAD_DIM * half : HEAD_DIM * half + 1]
        probs = jnp.exp(nt(head, kv) + (bias_ref[...] - lse_head))
        grad_scores = (probs * (nt(grad_head, kv) - delta)).astype(bf16)
        dqs.append(nn(grad_scores, kv) * scale)
        term = tn(grad_scores, head) + tn(probs.astype(bf16), grad_head)
        dkv = term if dkv is None else dkv + term
    dq = jnp.where(low, dqs[0], pltpu.roll(dqs[1], HEAD_DIM, 1)).astype(bf16).astype(f32)
    dq_ref[...] = turned(dq, cos[...], sin[...], back=True).astype(bf16)

    @pl.when(pl.program_id(1) == 0)
    def _():
        dkv_ref[...] = dkv

    @pl.when(pl.program_id(1) > 0)
    def _():
        dkv_ref[...] += dkv

    @pl.when(pl.program_id(1) == pl.num_programs(1) - 1)
    def _():
        at = 0
        for out in outs:
            out[...] = dkv_ref[at : at + out.shape[0], :].astype(out.dtype)
            at += out.shape[0]


def row_spans(width):
    near, far = 4, width // 2 - 4
    return ((0, near, 0, 0), (near, near, 1, 0), (2 * near, far, 0, near), (2 * near + far, far, 1, near))


def query_terms_body(blks, normed, gq, branch, mixed, pack, *outs):
    q_cols = gq.shape[1]
    unit = normed.shape[1] // blks
    for at, count, which, to in row_spans(blks):
        span, place = slice(at * unit, (at + count) * unit), slice(to * unit, (to + count) * unit)
        out = outs[which]
        out[place, :q_cols] = tn(normed[:, span], gq[...]).astype(bf16)
        out[place, q_cols : 2 * q_cols] = tn(branch[:, span], mixed[...]).astype(bf16)
        out[place, 2 * q_cols :] = pack[span, :]


def key_terms_body(blks, normed, gkv, *outs):
    unit = normed.shape[1] // blks
    for at, count, which, to in row_spans(blks):
        span, place = slice(at * unit, (at + count) * unit), slice(to * unit, (to + count) * unit)
        outs[which][place, :] = tn(normed[:, span], gkv[...]).astype(bf16)


def turn_back_body(count, seqs, *refs):
    own, others = refs[0], refs[1 : 1 + count]
    cos, sin, gq, weight = refs[1 + count : 5 + count]
    outs = refs[5 + count :]
    gkv_ref, parts = outs[0], outs[1:]
    cos_k, sin_k = key_tables(cos[...], sin[...])
    q_cols = gq.shape[1]
    for first in range(0, own.shape[1], LANES):
        span = slice(first, first + LANES)
        total = own[:, span]
        for other in others:
            total = total + other[:, span].astype(f32)
        gkv_ref[:, span] = turned(total.astype(bf16).astype(f32), cos_k, sin_k, back=True).astype(bf16)
    toks = parts[0].shape[0]
    for k in reversed(range(seqs)):
        span = slice(k * toks, (k + 1) * toks)
        grad = nt(gq[span, :], weight[:, :q_cols]) + nt(gkv_ref[span, :], weight[:, q_cols:])
        parts[k][...] = grad.astype(parts[k].dtype)


def to_row(column):
    count = column.shape[0]
    same = lax.broadcasted_iota(jnp.int32, (count, count), 0) == lane_ids((count, count))
    return jnp.sum(jnp.where(same, column, 0.0), axis=0, keepdims=True)


def finish_body(seqs, experts, me_ref, *refs):
    q_pieces, kv_pieces = refs[:seqs], refs[seqs : 2 * seqs]
    wq, wk, wv, gain = refs[2 * seqs : 2 * seqs + 4]
    query_ref, key_ref, value_ref, out_ref, router_ref, gain_one_ref, gain_two_ref = refs[2 * seqs + 4 :]
    q_cols = query_ref.shape[1] // seqs
    half = key_ref.shape[1] // seqs
    packed = None
    for k in range(seqs):
        part = q_pieces[k][:, 2 * q_cols :].astype(f32)
        packed = part if packed is None else packed + part
        for s in range(seqs):

            @pl.when(me_ref[0] == s ^ k)
            def _(s=s, k=k):
                span = slice(s * q_cols, (s + 1) * q_cols)
                query_ref[:, span] = q_pieces[k][:, :q_cols].astype(f32)
                out_ref[:, span] = q_pieces[k][:, q_cols : 2 * q_cols].astype(f32)
                for g in range(half // HEAD_DIM):
                    both = kv_pieces[k][:, 2 * g * HEAD_DIM : 2 * (g + 1) * HEAD_DIM].astype(f32)
                    span = slice(s * half + g * HEAD_DIM, s * half + (g + 1) * HEAD_DIM)
                    key_ref[:, span] = both[:, :HEAD_DIM]
                    value_ref[:, span] = both[:, HEAD_DIM:]

    router_ref[...] = packed.T[:experts, :]
    gain_two_ref[...] = to_row(packed[:, experts : experts + 1])
    weigh = lambda w, g: jnp.sum(w[...].astype(f32) * g[...], axis=1, keepdims=True)
    total = weigh(wq, query_ref) + weigh(wk, key_ref) + weigh(wv, value_ref)
    gain_one_ref[...] = to_row(total) / gain[...].astype(f32)


def middle_body(count, experts, *refs):
    parts = refs[:count]
    res, gains, router, routes, middle_ref, wide_ref, prob_ref = refs[count:]
    width = res.shape[1]
    middle = res[...].astype(f32)
    for part in parts:
        middle = middle + part[...].astype(f32)
    middle_ref[...] = middle
    inverse = lax.rsqrt(jnp.mean(middle * middle, axis=-1, keepdims=True) + epsilon)
    normed = (middle * inverse * gains[1:2, :]).astype(bf16)
    wide_ref[:, :width] = normed
    named = routes[...].astype(f32).T
    lanes = lane_ids((named.shape[0], LANES)).astype(f32)
    inside = lanes == named[:, 0:1]
    for i in range(1, named.shape[1]):
        inside = inside | (lanes == named[:, i : i + 1])
    logits = jnp.where(inside, nn(normed, router[...]), neg_large)
    raised = jnp.where(inside, jnp.exp(logits - jnp.max(logits, axis=-1, keepdims=True)), 0.0)
    prob = raised / jnp.sum(raised, axis=-1, keepdims=True)
    prob_ref[...] = prob
    high = prob.astype(bf16).astype(f32)
    rest = (prob - high).astype(bf16).astype(f32)
    wide_ref[:, width:] = (high + pltpu.roll(rest, experts, 1)).astype(bf16)


def expert_body(experts, k, seqs, me_ref, seq_ref, *refs):
    pieces, cot_all, packs = refs[:2], refs[2], refs[3 : 3 + 2 * seqs]
    outs, scratch = refs[-17:-10], refs[-10:]
    y_keep, y_send, x_all, hid_all, gg_all, geo_all, gi_ref = outs
    wide, cot_ref, y_ref, x_ref, hid_ref, gg_ref, geo_ref, wgu, wd, sems = scratch
    rows, width = cot_ref.shape[1], cot_ref.shape[2]
    high, low, cols = width // seqs, wd.shape[1] // seqs, wgu.shape[2] // 2
    me = me_ref[0]
    loads = [pltpu.make_async_copy(p, wide.at[i], sems.at[0, i]) for i, p in enumerate(pieces)]
    gates, downs = [], []
    for e in range(2):
        for j in range(seqs):
            at = pl.ds(pl.multiple_of((seq_ref[0] ^ j) * high, high), high)
            to = pl.ds(pl.multiple_of((seq_ref[0] ^ j) * low, low), low)
            pack = packs[e * seqs + j]
            gates.append(pltpu.make_async_copy(pack.at[:high, :], wgu.at[e, at, :], sems.at[1 + e, j]))
            downs.append(pltpu.make_async_copy(pack.at[high:, :], wd.at[e, to, :], sems.at[3 + e, j]))
    cots = [
        pltpu.make_async_copy(cot_all.at[(me ^ (4 * k + 2 * i)) // 2, :rows, :], cot_ref.at[i], sems.at[5, i])
        for i in range(2)
    ]
    for copies in (loads, gates[:seqs], downs[:seqs], cots, gates[seqs:], downs[seqs:]):
        for copy in copies:
            copy.start()
    for copy in loads:
        copy.wait()
    probs = [[], []]
    for i in range(2):
        x_ref[i * rows : (i + 1) * rows, :] = wide[i, :, :width]
        extra = wide[i, :, width:].astype(f32)
        lanes = lane_ids(extra.shape)
        for e in range(2):
            mine = (lanes == (me ^ e)) | (lanes == (me ^ e) + experts)
            probs[e].append(jnp.sum(jnp.where(mine, extra, 0.0), axis=-1, keepdims=True))
    x = x_ref[...]
    place = pl.ds(2 * k * rows, 2 * rows)
    stores = []

    def store(a, b, sem):
        stores.append(pltpu.make_async_copy(a, b, sem))
        stores[-1].start()

    store(x_ref, x_all.at[place, :], sems.at[8, 2])
    out, grad_in, marks, kept = None, None, [], []
    for e in range(2):
        prob = jnp.concatenate(probs[e], axis=0)
        for copy in gates[e * seqs : (e + 1) * seqs]:
            copy.wait()
        both = nn(x, wgu[e])
        gate, up = both[:, :cols], both[:, cols:]
        sigmoid = 1.0 / (1.0 + jnp.exp(-gate))
        active = gate * sigmoid
        hidden = (active * up).astype(bf16)
        hid_ref[e] = hidden
        store(hid_ref.at[e], hid_all.at[e, place, :], sems.at[6 + e, 0])
        for copy in downs[e * seqs : (e + 1) * seqs]:
            copy.wait()
        result = nn(hidden, wd[e]).astype(bf16).astype(f32)
        if e == 0:
            for copy in cots:
                copy.wait()
        final = jnp.concatenate([cot_ref[0], cot_ref[1]], axis=0).astype(f32)
        out = prob * result if out is None else out + prob * result
        marks.append(jnp.sum(result * final, axis=-1, keepdims=True))
        geo_ref[e] = (prob * final).astype(bf16)
        store(geo_ref.at[e], geo_all.at[e, place, :], sems.at[6 + e, 3])
        kept.append((gate, up, sigmoid, active))
    y_ref[...] = out.astype(bf16)
    store(y_ref.at[:rows, :], y_keep.at[k], sems.at[8, 0])
    store(y_ref.at[rows:, :], y_send.at[k], sems.at[8, 1])
    for e in range(2):
        gate, up, sigmoid, active = kept[e]
        grad_hidden = nt(geo_ref[e], wd[e])
        ggp = (grad_hidden * up * sigmoid * (1.0 + gate * (1.0 - sigmoid))).astype(bf16)
        gup = (grad_hidden * active).astype(bf16)
        gg_ref[e, :, :cols] = ggp
        gg_ref[e, :, cols:] = gup
        store(gg_ref.at[e], gg_all.at[e, place, :], sems.at[6 + e, 1])
        grad = nt(gg_ref[e], wgu[e])
        grad_in = grad if grad_in is None else grad_in + grad
    lanes = lane_ids((2 * rows, LANES))
    extra = jnp.zeros((2 * rows, LANES), f32)
    for e in range(2):
        mark = marks[e].astype(bf16).astype(f32)
        extra = extra + jnp.where(lanes == (me ^ e), mark, 0.0)
        extra = extra + jnp.where(lanes == (me ^ e) + experts, marks[e] - mark, 0.0)
    for i in range(2):
        span = slice(i * rows, (i + 1) * rows)
        gi_ref[i, :, :width] = grad_in[span, :].astype(bf16)
        gi_ref[i, :, width:] = extra[span, :].astype(bf16)
    for copy in stores:
        copy.wait()


def expert_grads_body(e, seqs, me_ref, *refs):
    sources, (x, gg, hid, geo, sems) = refs[:4], refs[-5:]
    outs = refs[4:-5]
    copies = [
        pltpu.make_async_copy(a if i == 0 else a.at[e], b, sems.at[i])
        for i, (a, b) in enumerate(zip(sources, (x, gg, hid, geo)))
    ]
    for copy in copies:
        copy.start()
    high, low = x.shape[1] // seqs, hid.shape[1] // seqs
    for i, (rows, a, b) in enumerate(((slice(0, high), x, gg), (slice(high, high + low), hid, geo))):
        for copy in copies[2 * i : 2 * i + 2]:
            copy.wait()
        size = rows.stop - rows.start
        for s in range(seqs):
            k = me_ref[0] ^ s
            part = tn(a[:, s * size : (s + 1) * size], b[...])
            if e == 1:
                outs[0][k, rows, :] = part.astype(bf16)
            else:
                part = part + outs[0][k, rows, :].astype(f32)

                @pl.when(k == 0)
                def _(part=part, i=i):
                    outs[1 + i][...] = part

                @pl.when(k != 0)
                def _(part=part, i=i):
                    outs[3 + i][k - 1] = part.astype(bf16)


def middle_back_body(count, experts, *refs):
    parts = refs[:count]
    middle_ref, prob_ref, cot, gains, router, grad_ref, branch_ref, pack_ref = refs[count:]
    width = cot.shape[1]
    gain = gains[1:2, :]
    total = parts[0][...].astype(f32)
    for part in parts[1:]:
        total = total + part[...].astype(f32)
    extra = total[:, width:]
    marks = extra + pltpu.roll(extra, LANES - experts, 1)
    prob = prob_ref[...]
    weighted = jnp.where(prob > 0, prob * marks, 0.0)
    spread = jnp.sum(weighted, axis=-1, keepdims=True)
    grad_logits = weighted - prob * spread
    high = grad_logits.astype(bf16)
    rest = (grad_logits - high.astype(f32)).astype(bf16)
    grad_normed = total[:, :width] + nt(high, router[...]) + nt(rest, router[...])
    middle = middle_ref[...]
    inverse = lax.rsqrt(jnp.mean(middle * middle, axis=-1, keepdims=True) + epsilon)
    unit = middle * inverse
    scaled = grad_normed * gain
    grad = cot[...].astype(f32) + inverse * (
        scaled - unit * jnp.mean(scaled * unit, axis=-1, keepdims=True)
    )
    grad_ref[...] = grad
    branch_ref[...] = grad.astype(bf16)
    normed = (unit * gain).astype(bf16)
    pack = tn(high, normed) + tn(rest, normed)
    gain_row = jnp.sum(grad_normed * unit, axis=0, keepdims=True)
    at_gain = lax.broadcasted_iota(jnp.int32, pack.shape, 0) == experts
    pack_ref[...] = jnp.where(at_gain, gain_row, pack).astype(bf16)


def input_back_body(count, *refs):
    parts = refs[:count]
    res, grad_middle, gains, out_ref = refs[count:]
    grad_normed = parts[0][...].astype(f32)
    for part in parts[1:]:
        grad_normed = grad_normed + part[...].astype(f32)
    x = res[...].astype(f32)
    inverse = lax.rsqrt(jnp.mean(x * x, axis=-1, keepdims=True) + epsilon)
    unit = x * inverse
    scaled = grad_normed * gains[0:1, :]
    out_ref[...] = grad_middle[...] + inverse * (
        scaled - unit * jnp.mean(scaled * unit, axis=-1, keepdims=True)
    )


def per_device(
    residual, segments, routes, w_query, w_key, w_value, w_out, w_router, attn_gain, moe_gain,
    w_gate, w_up, w_down, cotangent,
):
    seqs, blks = lax.axis_size("seq"), lax.axis_size("blk")
    seq_me, blk_me = lax.axis_index("seq"), lax.axis_index("blk")
    toks, width = residual.shape[1], residual.shape[2]
    rows = toks * seqs
    experts = blks
    own_rows = w_query.shape[0]
    kv_local = KV_HEADS // seqs
    q_cols, kv_cols = HEADS // seqs * HEAD_DIM, kv_local * 2 * HEAD_DIM
    cols = q_cols + kv_cols
    scale = HEAD_DIM ** (-0.5)
    tokens = segments.shape[0]
    doc_most = tokens // 8
    hops = min(blks - 1, -(-(doc_most - 1) // rows))
    behind = hops * rows
    keys = behind + rows
    groups = blks // 4
    masks = gather_masks(groups)
    res = residual[0]
    cot = cotangent[0]
    vmem = pl.BlockSpec(memory_space=pltpu.VMEM)
    smem = pl.BlockSpec(memory_space=pltpu.SMEM)
    seq_scalar = jnp.reshape(seq_me, (1,)).astype(jnp.int32)
    blk_scalar = jnp.reshape(blk_me, (1,)).astype(jnp.int32)
    hbm = pl.BlockSpec(memory_space=pltpu.HBM)
    gain_row = attn_gain[None, :]

    weight_dims = (own_rows, cols + LANES + q_cols)
    sources = (w_query, w_key, w_value, w_out.T, w_router.T, gain_row, moe_gain[None, :])
    weight_parts = call(
        functools.partial(pack_body, seqs, (q_cols, kv_cols, experts)),
        tuple(shape_of(weight_dims, bf16) for _ in range(seqs)),
        in_specs=[smem] + [hbm] * 7,
        scratch_shapes=[pltpu.VMEM(a.shape, a.dtype) for a in sources] + [pltpu.SemaphoreType.DMA((7,))],
    )(seq_scalar, *[in_hbm(a) for a in sources])
    weight_both = jnp.concatenate([swap_with(p, "seq", k) for k, p in enumerate(weight_parts)], axis=0)
    weight_own = weight_both[:, : cols + LANES]
    late_res = after(res, weight_both)
    res_parts = [res] + [swap_with(late_res, "seq", k) for k in range(1, seqs)]
    weight_rel = gather_rows(weight_own)
    same_core = [[2 * i + c for i in range(blks // 2)] for c in range(2)]
    joint = seqs * own_rows * q_cols // width
    out_own = weight_both[:, cols + LANES :].reshape(seqs, own_rows, q_cols)
    out_own = jnp.concatenate([out_own[k] for k in range(seqs)], axis=1).reshape(joint, width)
    both_all = lax.all_gather(
        jnp.concatenate([cot, out_own], axis=0), "blk", axis=0, axis_index_groups=same_core
    )
    gate, up, down, *_ = lax.optimization_barrier((w_gate[0], w_up[0], w_down[0], *res_parts))
    expert_pack = jnp.concatenate([jnp.concatenate([gate, up], axis=1), down], axis=0)
    packs = [swap_with(expert_pack, "seq", k) for k in range(seqs)]
    seq_me, blk_me = after(seq_me, weight_own), after(blk_me, weight_own)

    spot = np.arange(width)
    place, inner = spot // (seqs * own_rows), spot % (seqs * own_rows)
    mask_row = jnp.asarray(np.asarray(masks)[place], jnp.int32)
    seq_row = jnp.asarray(inner // own_rows, jnp.int32)
    source = ((seq_me ^ seq_row) * blks + (blk_me ^ mask_row)) * own_rows + (inner % own_rows)
    order = (lax.broadcasted_iota(jnp.int32, (width, width), 0) == source[None, :]).astype(bf16)

    turn = lambda i: (seq_me ^ (i // toks % seqs)) * toks + i % toks
    half_dim = HEAD_DIM // 2
    lanes = lane_ids((rows, LANES))
    inverse = jnp.exp((lanes % half_dim).astype(f32) * (-2.0 * math.log(10000.0) / HEAD_DIM))
    position = blk_me * rows + turn(lax.broadcasted_iota(jnp.int32, (rows, LANES), 0))
    angles = position.astype(f32) * inverse
    cos, sin = jnp.cos(angles), jnp.where(lanes % HEAD_DIM < half_dim, -1.0, 1.0) * jnp.sin(angles)
    key_ids = jnp.arange(keys, dtype=jnp.int32)
    key_places = key_ids // rows * rows - behind + turn(key_ids % rows)
    seg_padded = jnp.concatenate([jnp.full((behind,), -1, jnp.int32), segments])
    seg_near = lax.dynamic_slice_in_dim(seg_padded, blk_me * rows, keys).reshape(hops + 1, seqs, toks)
    seg_keys = jnp.stack(
        [lax.dynamic_index_in_dim(seg_near, seq_me ^ k, 1, keepdims=False) for k in range(seqs)], axis=1
    ).reshape(keys)
    meta = jnp.concatenate(
        [seg_keys.astype(f32)[None], key_places.astype(f32)[None], jnp.zeros((6, keys), f32)], axis=0
    )

    x_rel = jnp.concatenate([nn(part, order).astype(bf16) for part in res_parts], axis=0)
    q_all, kv_own, normed_rel = call(
        functools.partial(project_body, q_cols, kv_cols, experts),
        (shape_of((rows, q_cols), bf16), shape_of((rows, kv_cols), bf16), shape_of((rows, width), bf16)),
    )(x_rel, *weight_rel, cos, sin)
    if own_rows % 16 == 0:
        qkv_abs, router_abs, gains = call(
            functools.partial(restore_body, seqs, masks, experts),
            (shape_of((width, cols), bf16), shape_of((width, LANES), bf16), shape_of((8, width), f32)),
            in_specs=[smem, smem] + [vmem] * 4,
        )(seq_scalar, blk_scalar, *weight_rel)
    else:
        weight_abs = nn(order, jnp.concatenate(weight_rel, axis=0)).astype(bf16)
        qkv_abs, router_abs = weight_abs[:, :cols], weight_abs[:, cols:]
        gains = jnp.pad(router_abs[:, experts : experts + 2].astype(f32).T, ((0, 6), (0, 0)))

    kv_keys = jnp.concatenate([shifted(kv_own, "blk", n) for n in range(hops, 0, -1)] + [kv_own], axis=0)
    step = min(rows, 256)
    grid = (kv_local, rows // step)
    row_block = pl.BlockSpec((step, LANES), lambda g, i: (i, g))
    key_block = pl.BlockSpec((keys, LANES), lambda g, i: (0, g))
    meta_q_block = pl.BlockSpec((8, step), lambda g, i: (0, behind // step + i))
    meta_k_block = pl.BlockSpec((8, keys), lambda g, i: (0, 0))
    table_block = pl.BlockSpec((step, LANES), lambda g, i: (i, 0))
    attend_limit = 8 + step * keys * 40 // 1024 // 1024
    mixed, lse = call(
        functools.partial(attend_body, scale),
        (shape_of((rows, q_cols), bf16), shape_of((rows, q_cols), f32)),
        limit=attend_limit,
        grid=grid,
        in_specs=[row_block, key_block, meta_q_block, meta_k_block],
        out_specs=(row_block, row_block),
        scratch_shapes=[pltpu.VMEM((step, keys), f32)],
    )(q_all, kv_keys, meta, meta)

    packs += [swap_with(after(p, mixed), "blk", 1) for p in packs]

    out_same = after(both_all[:, toks:], mixed)
    out_pair = [out_same, swap_with(out_same, "blk", 1)]
    if own_rows % 16 == 0:
        out_abs = call(
            functools.partial(restore_out_body, seqs, blks),
            shape_of((width, q_cols), bf16),
            in_specs=[smem, smem, hbm, hbm],
            scratch_shapes=[pltpu.SemaphoreType.DMA((blks * seqs,))],
        )(seq_scalar, blk_scalar, *[in_hbm(a) for a in out_pair])
    else:
        odd = blk_me % 2 == 1
        pair = jnp.stack([jnp.where(odd, out_pair[1 - c], out_pair[c]) for c in range(2)], axis=1)
        out_parts = pair.reshape(blks, own_rows, seqs, q_cols).swapaxes(1, 2)
        out_abs = jnp.stack(
            [lax.dynamic_index_in_dim(out_parts, seq_me ^ k, 1, keepdims=False) for k in range(seqs)]
        ).reshape(width, q_cols)

    branch = nt(mixed, out_abs)
    branch_parts = [branch[:toks]] + [
        swap_with(branch[k * toks : (k + 1) * toks].astype(bf16), "seq", k) for k in range(1, seqs)
    ]
    middle, wide, prob = call(
        functools.partial(middle_body, seqs, experts),
        (shape_of((toks, width), f32), shape_of((toks, width + LANES), bf16), shape_of((toks, LANES), f32)),
    )(*branch_parts, res, gains, router_abs, routes[0].T)

    hidden_cols = w_gate.shape[2]
    held = 2 * toks * groups
    buffers = [
        (groups, toks, width), (groups, toks, width), (held, width), (2, held, hidden_cols), (2, held, 2 * hidden_cols),
        (2, held, width),
    ]

    def run_experts(k, pieces, before):
        operands = [*pieces, both_all, *packs, *before]
        fixed = len(operands) - len(before) + 2
        return call(
            functools.partial(expert_body, experts, k, seqs),
            tuple(pltpu.HBM(d, bf16) for d in buffers) + (shape_of((2, toks, width + LANES), bf16),),
            limit=24,
            flops=48 * toks * width * hidden_cols,
            in_specs=[smem, smem] + [hbm] * len(operands),
            out_specs=(hbm,) * len(buffers) + (vmem,),
            input_output_aliases={fixed + i: i for i in range(len(before))},
            scratch_shapes=[
                pltpu.VMEM((2, toks, width + LANES), bf16),
                pltpu.VMEM((2, toks, width), bf16),
                pltpu.VMEM((2 * toks, width), bf16),
                pltpu.VMEM((2 * toks, width), bf16),
                pltpu.VMEM((2, 2 * toks, hidden_cols), bf16),
                pltpu.VMEM((2, 2 * toks, 2 * hidden_cols), bf16),
                pltpu.VMEM((2, 2 * toks, width), bf16),
                pltpu.VMEM((2, width, 2 * hidden_cols), bf16),
                pltpu.VMEM((2, hidden_cols, width), bf16),
                pltpu.SemaphoreType.DMA((9, max(4, seqs))),
            ],
        )(blk_scalar, seq_scalar, *[in_hbm(a) for a in operands])

    turns = [1] + list(range(groups - 1, 1, -1)) + [0]
    far = {0: wide}
    last = wide
    for k in turns[:-1]:
        far[k] = swap_with(after(wide, last), "blk", 4 * k)
        last = far[k] if k > 1 else last
    across = {k: swap_with(far[k], "blk", 2) for k in far}
    grads, nears, before = {}, {}, []
    for i, k in enumerate(turns):
        holds = [prob]
        if i > 0:
            holds.append(grads[turns[i - 1]])
        if i > 1:
            n = turns[i - 2]
            nears[n] = added(grads[n][0], swap_with(grads[n][1], "blk", 2))
            holds.append(nears[n])
        *before, grads[k] = run_experts(k, [after(far[k], *holds), across[k]], before)
    for n in turns[-2:]:
        nears[n] = added(grads[n][0], swap_with(grads[n][1], "blk", 2))
    grad_parts = [swap_with(nears[k], "blk", 4 * k) for k in turns]
    y_keep, y_send, x_all, hid_all, gg_all, geo_all = before
    tdot = lambda a, b: lax.dot_general(a, b, (((0,), (0,)), ((), ())), preferred_element_type=f32)

    grad_middle, grad_branch, pack = call(
        functools.partial(middle_back_body, groups, experts),
        (shape_of((toks, width), f32), shape_of((toks, width), bf16), shape_of((LANES, width), bf16)),
    )(*grad_parts, middle, prob, cot, gains, router_abs)

    high, low = width // seqs, hidden_cols // seqs

    x_all = after(x_all, nears[turns[-1]])
    y_far = swap_with(after(y_send, grad_branch), "blk", 2)

    def expert_grads(e, outs, *others):
        operands = [in_hbm(a) for a in (x_all, gg_all, hid_all, geo_all)]
        return call(
            functools.partial(expert_grads_body, e, seqs),
            outs,
            limit=10 + 7 * held // 1024,
            flops=6 * held * width * hidden_cols,
            in_specs=[smem] + [hbm] * 4 + [vmem] * len(others),
            scratch_shapes=[
                pltpu.VMEM((held, width), bf16), pltpu.VMEM((held, 2 * hidden_cols), bf16),
                pltpu.VMEM((held, hidden_cols), bf16), pltpu.VMEM((held, width), bf16),
                pltpu.SemaphoreType.DMA((4,)),
            ],
        )(seq_scalar, *operands, *others)

    partner_terms = expert_grads(1, shape_of((seqs, high + low, width), bf16))
    branch_others = [swap_with(grad_branch, "seq", k) for k in range(1, seqs)]
    branch_all = after(jnp.concatenate([grad_branch] + branch_others, axis=0), partner_terms)
    grad_mixed = nn(branch_all, out_abs).astype(bf16)
    block_spec = pl.BlockSpec((rows, LANES), lambda g, i: (0, g))
    gq_pre, *grad_kv = call(
        functools.partial(attend_back_body, scale),
        (shape_of((rows, q_cols), bf16),)
        + (shape_of((rows, kv_cols), bf16),) * hops
        + (shape_of((rows, kv_cols), f32),),
        limit=attend_limit,
        grid=grid,
        flops=24 * rows * keys * q_cols,
        in_specs=[row_block, key_block, row_block, row_block, row_block, meta_q_block, meta_k_block,
                  table_block, table_block],
        out_specs=(row_block,) + (block_spec,) * (hops + 1),
        scratch_shapes=[pltpu.VMEM((keys, LANES), f32), pltpu.VMEM((step, keys), f32)],
    )(q_all, kv_keys, mixed, grad_mixed, lse, meta, meta, cos, sin)
    returned = [shifted(grad_kv[hops - n], "blk", -n) for n in range(1, hops + 1)]
    spare = max(1, seqs - 1)
    gg_own, down_own, gg_sends, down_sends = expert_grads(
        0,
        (shape_of((high, 2 * hidden_cols), f32), shape_of((low, width), f32),
         shape_of((spare, high, 2 * hidden_cols), bf16), shape_of((spare, low, width), bf16)),
        after(swap_with(partner_terms, "blk", 1), gq_pre),
    )
    down_from = [swap_with(down_sends[k - 1], "seq", k) for k in range(1, seqs)]
    y_near = added(y_keep, y_far)
    branch_rel = nn(branch_all, order).astype(bf16)
    pack_rel = tdot(order, pack.T).astype(bf16)
    unit = seqs * own_rows
    q_terms = call(
        functools.partial(query_terms_body, blks),
        (shape_of((width // 2, 2 * q_cols + LANES), bf16),) * 2,
    )(normed_rel, gq_pre, branch_rel, mixed, pack_rel)

    def for_this_row(terms):
        total = sum(t.astype(f32) for t in terms).astype(bf16)
        return [swap_with(total[k * own_rows : (k + 1) * own_rows], "seq", k) for k in range(seqs)]

    q_total = scatter_core(*q_terms)
    q_stage = scatter_across(after(q_total, gg_sends, *returned))
    own_kv = after(grad_kv[-1], q_total, gg_sends)

    gkv_pre, *normed_parts = call(
        functools.partial(turn_back_body, hops, seqs),
        (shape_of((rows, kv_cols), bf16),)
        + tuple(shape_of((toks, width), bf16 if k else f32) for k in range(seqs)),
    )(own_kv, *returned, cos, sin, gq_pre, qkv_abs)
    kv_terms = call(
        functools.partial(key_terms_body, blks), (shape_of((width // 2, kv_cols), bf16),) * 2
    )(normed_rel, gkv_pre)
    q_pieces = for_this_row(scatter_far(q_stage))
    gg_from = [swap_with(gg_sends[k - 1], "seq", k) for k in range(1, seqs)]
    kv_stage = scatter_across(scatter_core(*kv_terms))
    kv_pieces = for_this_row(scatter_far(kv_stage))
    shard_query, shard_key, shard_value, shard_out, shard_router, shard_gain_one, shard_gain_two = call(
        functools.partial(finish_body, seqs, experts),
        (shape_of(w_query.shape, f32), shape_of(w_key.shape, f32), shape_of(w_value.shape, f32),
         shape_of(w_out.shape[::-1], f32), shape_of(w_router.shape[::-1], f32),
         shape_of((1, own_rows), f32), shape_of((1, own_rows), f32)),
        in_specs=[smem] + [vmem] * (2 * seqs + 4),
    )(seq_scalar, *q_pieces, *kv_pieces, w_query, w_key, w_value, gain_row)
    normed_others = [swap_with(p, "seq", k) for k, p in enumerate(normed_parts) if k]
    grad_input = call(
        functools.partial(input_back_body, seqs), shape_of((toks, width), f32)
    )(normed_parts[0], *normed_others, res, grad_middle, gains)

    for k in range(1, seqs):
        gg_own = gg_own + gg_from[k - 1].astype(f32)
        down_own = down_own + down_from[k - 1].astype(f32)
    shard_gate, shard_up = gg_own[None, :, :hidden_cols], gg_own[None, :, hidden_cols:]
    shard_down = down_own[None]

    y_sum = middle + y_near[0].astype(f32)
    for k in range(1, groups):
        y_sum = y_sum + swap_with(y_near[k], "blk", 4 * k).astype(f32)
    block_out = y_sum.astype(bf16)[None]
    return (
        block_out, grad_input[None], shard_query, shard_key, shard_value, shard_out.T, shard_router.T,
        shard_gain_one[0], shard_gain_two[0], shard_gate, shard_up, shard_down,
    )


def solution(mesh):
    both = ("seq", "blk")
    tokens, rows, cols, line = P("blk", "seq", None), P(both, None), P(None, both), P(both)
    return jax.shard_map(
        per_device,
        mesh=mesh,
        in_specs=(
            tokens, P(), tokens, rows, rows, rows, cols, rows, line, line, tokens, tokens, tokens, tokens,
        ),
        out_specs=(
            tokens, tokens, rows, rows, rows, cols, rows, line, line, tokens, tokens, tokens,
        ),
        check_vma=False,
    )
```

```python
import functools
import math

import jax
import jax.numpy as jnp
import numpy as np
from jax import lax
from jax.experimental import pallas as pl
from jax.experimental.pallas import tpu as pltpu
from jax.sharding import PartitionSpec as P

HEADS = 16
KV_HEADS = 8
HEAD_DIM = 64
LANES = 128

f32 = jnp.float32
bf16 = jnp.bfloat16
epsilon = 1e-06
neg_large = -1e30


def swap_with(value, axis, mask):
    if mask == 0:
        return value
    count = lax.axis_size(axis)
    return lax.ppermute(value, axis, [(i, i ^ mask) for i in range(count)])


def shifted(value, axis, steps):
    count = lax.axis_size(axis)
    leading, last = (max(0, -steps), min(count, count - steps))
    return lax.ppermute(value, axis, [(i, i + steps) for i in range(leading, last)])


def gather_seq(value):
    count = lax.axis_size("seq")
    me = lax.axis_index("seq")
    whole = jnp.zeros((count,) + value.shape, value.dtype)
    for k in range(count):
        piece = swap_with(value, "seq", k)
        whole = lax.dynamic_update_index_in_dim(whole, piece, me ^ k, 0)
    return whole


def after(value, *others):
    return lax.optimization_barrier((value,) + others)[0]


def gather_masks(groups):
    near = [0, 2, 4, 6]
    far = [4 * k + x for k in range(2, groups) for x in (0, 2)]
    return [m + c for half in (near, far) for c in (0, 1) for m in half]


def gather_rows(value):
    groups = lax.axis_size("blk") // 4
    near_z = swap_with(value, "blk", 4)
    far, last = [], value
    for k in range(2, groups):
        last = swap_with(after(value, last), "blk", 4 * k)
        far += [last, swap_with(last, "blk", 2)]
    near = jnp.concatenate(
        [value, swap_with(value, "blk", 2), near_z, swap_with(near_z, "blk", 2)], axis=0
    )
    far = jnp.concatenate(far, axis=0)
    return [near, swap_with(near, "blk", 1), far, swap_with(far, "blk", 1)]


def added(a, b):
    return (a.astype(f32) + b.astype(f32)).astype(a.dtype)


def scatter_core(keep, send):
    return added(keep, swap_with(send, "blk", 1))


def scatter_across(total):
    groups = lax.axis_size("blk") // 4
    parts = total.reshape(groups, 2, total.shape[0] // groups // 2, -1)
    return added(parts[:, 0], swap_with(parts[:, 1], "blk", 2))


def scatter_far(parts):
    return [swap_with(parts[k], "blk", 4 * k) for k in range(parts.shape[0] - 1, 0, -1)] + [parts[0]]


def call(body, out_shape, limit=16, flops=0, **options):
    many = isinstance(out_shape, (tuple, list))
    if "grid" not in options:
        space = pl.BlockSpec(memory_space=pltpu.VMEM)
        options.setdefault("out_specs", tuple(space for _ in out_shape) if many else space)
    sized = sum(math.prod(o.shape) * o.dtype.itemsize for o in (out_shape if many else [out_shape]))
    return pl.pallas_call(
        body,
        out_shape=out_shape,
        compiler_params=pltpu.CompilerParams(vmem_limit_bytes=limit * 1024 * 1024),
        cost_estimate=pl.CostEstimate(flops=flops, bytes_accessed=2 * sized, transcendentals=0),
        **options,
    )


def in_hbm(value):
    return pltpu.with_memory_space_constraint(value, pltpu.HBM)


def shape_of(dims, dtype):
    return jax.ShapeDtypeStruct(dims, dtype)


def lane_ids(shape):
    return lax.broadcasted_iota(jnp.int32, shape, len(shape) - 1)


def half_swap(tile):
    lanes = lane_ids(tile.shape)
    return jnp.where(lanes % 64 < 32, pltpu.roll(tile, 96, 1), pltpu.roll(tile, 32, 1))


def nt(a, b):
    return lax.dot_general(a, b, (((1,), (1,)), ((), ())), preferred_element_type=f32)


def tn(a, b):
    return lax.dot_general(a, b, (((0,), (0,)), ((), ())), preferred_element_type=f32)


def nn(a, b):
    return jnp.dot(a, b, preferred_element_type=f32)


def turned(tile, cos, sin, back=False):
    moved = half_swap(tile) * sin
    return tile * cos + (-moved if back else moved)


def key_tables(cos, sin):
    low = lane_ids(cos.shape) < HEAD_DIM
    return jnp.where(low, cos, 1.0), jnp.where(low, sin, 0.0)


def pack_body(seqs, dims, me_ref, *refs):
    q_cols, kv_cols, experts = dims
    sources, outs = refs[:7], refs[7 : 7 + seqs]
    held, sems = refs[7 + seqs : 14 + seqs], refs[14 + seqs]
    copies = [pltpu.make_async_copy(a, b, sems.at[i]) for i, (a, b) in enumerate(zip(sources, held))]
    for copy in copies:
        copy.start()
    for copy in copies:
        copy.wait()
    wq, wk, wv, wo, wr, gain_a, gain_m = held
    own_rows = wq.shape[0]
    lines = [wr[...].astype(f32), gain_a[...].astype(f32), gain_m[...].astype(f32)]
    lines.append(jnp.zeros((LANES - experts - 2, own_rows), f32))
    extra = jnp.concatenate(lines, axis=0).T.astype(bf16)
    half = kv_cols // 2
    for s in range(seqs):
        for k in range(seqs):

            @pl.when(me_ref[0] == s ^ k)
            def _(s=s, k=k):
                out = outs[k]
                out[:, :q_cols] = wq[:, s * q_cols : (s + 1) * q_cols]
                for g in range(half // HEAD_DIM):
                    span = slice(s * half + g * HEAD_DIM, s * half + (g + 1) * HEAD_DIM)
                    at = q_cols + 2 * g * HEAD_DIM
                    out[:, at : at + LANES] = jnp.concatenate([wk[:, span], wv[:, span]], axis=1)
                at = q_cols + kv_cols
                out[:, at : at + LANES] = extra
                out[:, at + LANES :] = wo[:, s * q_cols : (s + 1) * q_cols]


def restore_body(seqs, masks, experts, seq_ref, blk_ref, w0, w1, w2, w3, qkv_ref, router_ref, gain_ref):
    cols = qkv_ref.shape[1]
    blks = len(masks)
    unit = qkv_ref.shape[0] // blks
    own_rows = unit // seqs
    places = [(weight, r) for weight in (w0, w1, w2, w3) for r in range(0, weight.shape[0], unit)]
    for (weight, row), mask in zip(places, masks):
        for k in range(seqs):
            at = ((seq_ref[0] ^ k) * blks + (blk_ref[0] ^ mask)) * own_rows
            to = pl.ds(pl.multiple_of(at, own_rows), own_rows)
            span = slice(row + k * own_rows, row + (k + 1) * own_rows)
            qkv_ref[to, :] = weight[span, :cols]
            router_ref[to, :] = weight[span, cols:]
    pick = lax.broadcasted_iota(jnp.int32, (8, LANES), 0) + experts == lane_ids((8, LANES))
    gain_ref[...] = nt(pick.astype(bf16), router_ref[...])


def restore_out_body(seqs, blks, seq_ref, blk_ref, own, other, out_ref, sem):
    q_cols = out_ref.shape[1]
    own_rows = out_ref.shape[0] // blks // seqs
    copies = []
    for i in range(blks // 2):
        for c, weight in enumerate((own, other)):
            for k in range(seqs):
                blk = 2 * i + ((blk_ref[0] & 1) ^ c)
                at = ((seq_ref[0] ^ k) * blks + blk) * own_rows
                to = pl.ds(pl.multiple_of(at, own_rows), own_rows)
                part = weight.at[i, :, k * q_cols : (k + 1) * q_cols]
                copies.append(pltpu.make_async_copy(part, out_ref.at[to, :], sem.at[len(copies)]))
    for copy in copies:
        copy.start()
    for copy in copies:
        copy.wait()


def project_body(q_cols, kv_cols, gain_lane, x_ref, *refs):
    weights, (cos, sin, q_ref, kv_ref, normed_ref) = refs[:4], refs[4:]
    x = x_ref[...].astype(f32)
    inverse = lax.rsqrt(jnp.mean(x * x, axis=-1, keepdims=True) + epsilon)
    cols = q_cols + kv_cols
    pick = (lane_ids((8, LANES)) == gain_lane).astype(bf16)
    spans, at = [], 0
    for weight in weights:
        span = slice(at, at + weight.shape[0])
        gain = nt(pick, weight[:, cols : cols + LANES])[0:1, :]
        normed_ref[:, span] = (x[:, span] * inverse * gain).astype(bf16)
        spans.append(span)
        at += weight.shape[0]
    cos_q, sin_q = cos[...], sin[...]
    cos_k, sin_k = key_tables(cos_q, sin_q)
    wide = 2 * LANES if q_cols % (2 * LANES) == 0 and kv_cols % (2 * LANES) == 0 else LANES
    for first in range(0, cols, wide):
        both = None
        for span, weight in zip(spans, weights):
            term = nn(normed_ref[:, span], weight[:, first : first + wide])
            both = term if both is None else both + term
        for at in range(first, first + wide, LANES):
            tile = both[:, at - first : at - first + LANES]
            if at < q_cols:
                q_ref[:, at : at + LANES] = turned(tile, cos_q, sin_q).astype(bf16)
            else:
                kv_ref[:, at - q_cols : at - q_cols + LANES] = turned(tile, cos_k, sin_k).astype(bf16)


def hide_keys(meta_q, meta_k, bias_ref):
    @pl.when((pl.program_id(0) == 0) | (pl.num_programs(1) > 1))
    def _():
        mine = meta_q[...].T
        theirs = meta_k[...]
        visible = (theirs[1:2, :] <= mine[:, 1:2]) & (theirs[0:1, :] == mine[:, 0:1])
        bias_ref[...] = jnp.where(visible, 0.0, neg_large)


def attend_body(scale, q_ref, kv_ref, meta_q, meta_k, out_ref, lse_ref, bias_ref):
    hide_keys(meta_q, meta_k, bias_ref)
    q = q_ref[...].astype(f32) * scale
    kv = kv_ref[...]
    low = lane_ids(q.shape) < HEAD_DIM
    outs, lses = [], []
    for half in range(2):
        head = jnp.where(low, pltpu.roll(q, HEAD_DIM, 1) if half else q, 0.0).astype(bf16)
        scores = nt(head, kv) + bias_ref[...]
        most = jnp.max(scores, axis=-1, keepdims=True)
        weights = jnp.exp(scores - most)
        total = jnp.sum(weights, axis=-1, keepdims=True)
        outs.append(nn(weights.astype(bf16), kv) / total)
        lses.append(most + jnp.log(total))
    out_ref[...] = jnp.where(low, pltpu.roll(outs[0], HEAD_DIM, 1), outs[1]).astype(bf16)
    lse_ref[...] = jnp.where(low, lses[0], lses[1])


def attend_back_body(
    scale, q_ref, kv_ref, mixed_ref, grad_ref, lse_ref, meta_q, meta_k, cos, sin, dq_ref, *outs
):
    outs, dkv_ref, bias_ref = outs[:-2], outs[-2], outs[-1]
    hide_keys(meta_q, meta_k, bias_ref)
    q = q_ref[...].astype(f32) * scale
    kv = kv_ref[...]
    grad = grad_ref[...].astype(f32)
    low = lane_ids(q.shape) < HEAD_DIM
    product = grad * mixed_ref[...].astype(f32)
    lse = lse_ref[...]
    dqs = []
    dkv = None
    for half in range(2):
        head = jnp.where(low, pltpu.roll(q, HEAD_DIM, 1) if half else q, 0.0).astype(bf16)
        grad_head = jnp.where(low, 0.0, grad if half else pltpu.roll(grad, HEAD_DIM, 1)).astype(bf16)
        delta = jnp.sum(jnp.where(low == (half == 0), product, 0.0), axis=-1, keepdims=True)
        lse_head = lse[:, HEAD_DIM * half : HEAD_DIM * half + 1]
        probs = jnp.exp(nt(head, kv) + (bias_ref[...] - lse_head))
        grad_scores = (probs * (nt(grad_head, kv) - delta)).astype(bf16)
        dqs.append(nn(grad_scores, kv) * scale)
        term = tn(grad_scores, head) + tn(probs.astype(bf16), grad_head)
        dkv = term if dkv is None else dkv + term
    dq = jnp.where(low, dqs[0], pltpu.roll(dqs[1], HEAD_DIM, 1)).astype(bf16).astype(f32)
    dq_ref[...] = turned(dq, cos[...], sin[...], back=True).astype(bf16)

    @pl.when(pl.program_id(1) == 0)
    def _():
        dkv_ref[...] = dkv

    @pl.when(pl.program_id(1) > 0)
    def _():
        dkv_ref[...] += dkv

    @pl.when(pl.program_id(1) == pl.num_programs(1) - 1)
    def _():
        at = 0
        for out in outs:
            out[...] = dkv_ref[at : at + out.shape[0], :].astype(out.dtype)
            at += out.shape[0]


def row_spans(width):
    near, far = 4, width // 2 - 4
    return ((0, near, 0, 0), (near, near, 1, 0), (2 * near, far, 0, near), (2 * near + far, far, 1, near))


def query_terms_body(blks, normed, gq, branch, mixed, pack, *outs):
    q_cols = gq.shape[1]
    unit = normed.shape[1] // blks
    for at, count, which, to in row_spans(blks):
        span, place = slice(at * unit, (at + count) * unit), slice(to * unit, (to + count) * unit)
        out = outs[which]
        out[place, :q_cols] = tn(normed[:, span], gq[...]).astype(bf16)
        out[place, q_cols : 2 * q_cols] = tn(branch[:, span], mixed[...]).astype(bf16)
        out[place, 2 * q_cols :] = pack[span, :]


def key_terms_body(blks, normed, gkv, *outs):
    unit = normed.shape[1] // blks
    for at, count, which, to in row_spans(blks):
        span, place = slice(at * unit, (at + count) * unit), slice(to * unit, (to + count) * unit)
        outs[which][place, :] = tn(normed[:, span], gkv[...]).astype(bf16)


def turn_back_body(count, seqs, *refs):
    own, others = refs[0], refs[1 : 1 + count]
    cos, sin, gq, weight = refs[1 + count : 5 + count]
    outs = refs[5 + count :]
    gkv_ref, parts = outs[0], outs[1:]
    cos_k, sin_k = key_tables(cos[...], sin[...])
    q_cols = gq.shape[1]
    for first in range(0, own.shape[1], LANES):
        span = slice(first, first + LANES)
        total = own[:, span]
        for other in others:
            total = total + other[:, span].astype(f32)
        gkv_ref[:, span] = turned(total.astype(bf16).astype(f32), cos_k, sin_k, back=True).astype(bf16)
    toks = parts[0].shape[0]
    for k in reversed(range(seqs)):
        span = slice(k * toks, (k + 1) * toks)
        grad = nt(gq[span, :], weight[:, :q_cols]) + nt(gkv_ref[span, :], weight[:, q_cols:])
        parts[k][...] = grad.astype(parts[k].dtype)


def to_row(column):
    count = column.shape[0]
    same = lax.broadcasted_iota(jnp.int32, (count, count), 0) == lane_ids((count, count))
    return jnp.sum(jnp.where(same, column, 0.0), axis=0, keepdims=True)


def finish_body(seqs, experts, me_ref, *refs):
    q_pieces, kv_pieces = refs[:seqs], refs[seqs : 2 * seqs]
    wq, wk, wv, gain = refs[2 * seqs : 2 * seqs + 4]
    query_ref, key_ref, value_ref, out_ref, router_ref, gain_one_ref, gain_two_ref = refs[2 * seqs + 4 :]
    q_cols = query_ref.shape[1] // seqs
    half = key_ref.shape[1] // seqs
    packed = None
    for k in range(seqs):
        part = q_pieces[k][:, 2 * q_cols :].astype(f32)
        packed = part if packed is None else packed + part
        for s in range(seqs):

            @pl.when(me_ref[0] == s ^ k)
            def _(s=s, k=k):
                span = slice(s * q_cols, (s + 1) * q_cols)
                query_ref[:, span] = q_pieces[k][:, :q_cols].astype(f32)
                out_ref[:, span] = q_pieces[k][:, q_cols : 2 * q_cols].astype(f32)
                for g in range(half // HEAD_DIM):
                    both = kv_pieces[k][:, 2 * g * HEAD_DIM : 2 * (g + 1) * HEAD_DIM].astype(f32)
                    span = slice(s * half + g * HEAD_DIM, s * half + (g + 1) * HEAD_DIM)
                    key_ref[:, span] = both[:, :HEAD_DIM]
                    value_ref[:, span] = both[:, HEAD_DIM:]

    router_ref[...] = packed.T[:experts, :]
    gain_two_ref[...] = to_row(packed[:, experts : experts + 1])
    weigh = lambda w, g: jnp.sum(w[...].astype(f32) * g[...], axis=1, keepdims=True)
    total = weigh(wq, query_ref) + weigh(wk, key_ref) + weigh(wv, value_ref)
    gain_one_ref[...] = to_row(total) / gain[...].astype(f32)


def middle_body(count, experts, *refs):
    parts = refs[:count]
    res, gains, router, routes, middle_ref, wide_ref, prob_ref = refs[count:]
    width = res.shape[1]
    middle = res[...].astype(f32)
    for part in parts:
        middle = middle + part[...].astype(f32)
    middle_ref[...] = middle
    inverse = lax.rsqrt(jnp.mean(middle * middle, axis=-1, keepdims=True) + epsilon)
    normed = (middle * inverse * gains[1:2, :]).astype(bf16)
    wide_ref[:, :width] = normed
    named = routes[...].astype(f32).T
    lanes = lane_ids((named.shape[0], LANES)).astype(f32)
    inside = lanes == named[:, 0:1]
    for i in range(1, named.shape[1]):
        inside = inside | (lanes == named[:, i : i + 1])
    logits = jnp.where(inside, nn(normed, router[...]), neg_large)
    raised = jnp.where(inside, jnp.exp(logits - jnp.max(logits, axis=-1, keepdims=True)), 0.0)
    prob = raised / jnp.sum(raised, axis=-1, keepdims=True)
    prob_ref[...] = prob
    high = prob.astype(bf16).astype(f32)
    rest = (prob - high).astype(bf16).astype(f32)
    wide_ref[:, width:] = (high + pltpu.roll(rest, experts, 1)).astype(bf16)


def expert_body(experts, k, seqs, me_ref, seq_ref, *refs):
    pieces, cot_all, packs = refs[:2], refs[2], refs[3 : 3 + 2 * seqs]
    outs, scratch = refs[-17:-10], refs[-10:]
    y_keep, y_send, x_all, hid_all, gg_all, geo_all, gi_ref = outs
    wide, cot_ref, y_ref, x_ref, hid_ref, gg_ref, geo_ref, wgu, wd, sems = scratch
    rows, width = cot_ref.shape[1], cot_ref.shape[2]
    high, low, cols = width // seqs, wd.shape[1] // seqs, wgu.shape[2] // 2
    me = me_ref[0]
    loads = [pltpu.make_async_copy(p, wide.at[i], sems.at[0, i]) for i, p in enumerate(pieces)]
    gates, downs = [], []
    for e in range(2):
        for j in range(seqs):
            at = pl.ds(pl.multiple_of((seq_ref[0] ^ j) * high, high), high)
            to = pl.ds(pl.multiple_of((seq_ref[0] ^ j) * low, low), low)
            pack = packs[e * seqs + j]
            gates.append(pltpu.make_async_copy(pack.at[:high, :], wgu.at[e, at, :], sems.at[1 + e, j]))
            downs.append(pltpu.make_async_copy(pack.at[high:, :], wd.at[e, to, :], sems.at[3 + e, j]))
    cots = [
        pltpu.make_async_copy(cot_all.at[(me ^ (4 * k + 2 * i)) // 2, :rows, :], cot_ref.at[i], sems.at[5, i])
        for i in range(2)
    ]
    for copies in (loads, gates[:seqs], downs[:seqs], cots, gates[seqs:], downs[seqs:]):
        for copy in copies:
            copy.start()
    for copy in loads:
        copy.wait()
    probs = [[], []]
    for i in range(2):
        x_ref[i * rows : (i + 1) * rows, :] = wide[i, :, :width]
        extra = wide[i, :, width:].astype(f32)
        lanes = lane_ids(extra.shape)
        for e in range(2):
            mine = (lanes == (me ^ e)) | (lanes == (me ^ e) + experts)
            probs[e].append(jnp.sum(jnp.where(mine, extra, 0.0), axis=-1, keepdims=True))
    x = x_ref[...]
    place = pl.ds(2 * k * rows, 2 * rows)
    stores = []

    def store(a, b, sem):
        stores.append(pltpu.make_async_copy(a, b, sem))
        stores[-1].start()

    store(x_ref, x_all.at[place, :], sems.at[8, 2])
    out, grad_in, marks, kept = None, None, [], []
    for e in range(2):
        prob = jnp.concatenate(probs[e], axis=0)
        for copy in gates[e * seqs : (e + 1) * seqs]:
            copy.wait()
        both = nn(x, wgu[e])
        gate, up = both[:, :cols], both[:, cols:]
        sigmoid = 1.0 / (1.0 + jnp.exp(-gate))
        active = gate * sigmoid
        hidden = (active * up).astype(bf16)
        hid_ref[e] = hidden
        store(hid_ref.at[e], hid_all.at[e, place, :], sems.at[6 + e, 0])
        for copy in downs[e * seqs : (e + 1) * seqs]:
            copy.wait()
        result = nn(hidden, wd[e]).astype(bf16).astype(f32)
        if e == 0:
            for copy in cots:
                copy.wait()
        final = jnp.concatenate([cot_ref[0], cot_ref[1]], axis=0).astype(f32)
        out = prob * result if out is None else out + prob * result
        marks.append(jnp.sum(result * final, axis=-1, keepdims=True))
        geo_ref[e] = (prob * final).astype(bf16)
        store(geo_ref.at[e], geo_all.at[e, place, :], sems.at[6 + e, 3])
        kept.append((gate, up, sigmoid, active))
    y_ref[...] = out.astype(bf16)
    store(y_ref.at[:rows, :], y_keep.at[k], sems.at[8, 0])
    store(y_ref.at[rows:, :], y_send.at[k], sems.at[8, 1])
    for e in range(2):
        gate, up, sigmoid, active = kept[e]
        grad_hidden = nt(geo_ref[e], wd[e])
        ggp = (grad_hidden * up * sigmoid * (1.0 + gate * (1.0 - sigmoid))).astype(bf16)
        gup = (grad_hidden * active).astype(bf16)
        gg_ref[e, :, :cols] = ggp
        gg_ref[e, :, cols:] = gup
        store(gg_ref.at[e], gg_all.at[e, place, :], sems.at[6 + e, 1])
        grad = nt(gg_ref[e], wgu[e])
        grad_in = grad if grad_in is None else grad_in + grad
    lanes = lane_ids((2 * rows, LANES))
    extra = jnp.zeros((2 * rows, LANES), f32)
    for e in range(2):
        mark = marks[e].astype(bf16).astype(f32)
        extra = extra + jnp.where(lanes == (me ^ e), mark, 0.0)
        extra = extra + jnp.where(lanes == (me ^ e) + experts, marks[e] - mark, 0.0)
    for i in range(2):
        span = slice(i * rows, (i + 1) * rows)
        gi_ref[i, :, :width] = grad_in[span, :].astype(bf16)
        gi_ref[i, :, width:] = extra[span, :].astype(bf16)
    for copy in stores:
        copy.wait()


def expert_grads_body(e, seqs, me_ref, *refs):
    sources, (x, gg, hid, geo, sems) = refs[:4], refs[-5:]
    outs = refs[4:-5]
    copies = [
        pltpu.make_async_copy(a if i == 0 else a.at[e], b, sems.at[i])
        for i, (a, b) in enumerate(zip(sources, (x, gg, hid, geo)))
    ]
    for copy in copies:
        copy.start()
    high, low = x.shape[1] // seqs, hid.shape[1] // seqs
    for i, (rows, a, b) in enumerate(((slice(0, high), x, gg), (slice(high, high + low), hid, geo))):
        for copy in copies[2 * i : 2 * i + 2]:
            copy.wait()
        size = rows.stop - rows.start
        for s in range(seqs):
            k = me_ref[0] ^ s
            part = tn(a[:, s * size : (s + 1) * size], b[...])
            if e == 1:
                outs[0][k, rows, :] = part.astype(bf16)
            else:
                part = part + outs[0][k, rows, :].astype(f32)

                @pl.when(k == 0)
                def _(part=part, i=i):
                    outs[1 + i][...] = part

                @pl.when(k != 0)
                def _(part=part, i=i):
                    outs[3 + i][k - 1] = part.astype(bf16)


def middle_back_body(count, experts, *refs):
    parts = refs[:count]
    middle_ref, prob_ref, cot, gains, router, grad_ref, branch_ref, pack_ref = refs[count:]
    width = cot.shape[1]
    gain = gains[1:2, :]
    total = parts[0][...].astype(f32)
    for part in parts[1:]:
        total = total + part[...].astype(f32)
    extra = total[:, width:]
    marks = extra + pltpu.roll(extra, LANES - experts, 1)
    prob = prob_ref[...]
    weighted = jnp.where(prob > 0, prob * marks, 0.0)
    spread = jnp.sum(weighted, axis=-1, keepdims=True)
    grad_logits = weighted - prob * spread
    high = grad_logits.astype(bf16)
    rest = (grad_logits - high.astype(f32)).astype(bf16)
    grad_normed = total[:, :width] + nt(high, router[...]) + nt(rest, router[...])
    middle = middle_ref[...]
    inverse = lax.rsqrt(jnp.mean(middle * middle, axis=-1, keepdims=True) + epsilon)
    unit = middle * inverse
    scaled = grad_normed * gain
    grad = cot[...].astype(f32) + inverse * (
        scaled - unit * jnp.mean(scaled * unit, axis=-1, keepdims=True)
    )
    grad_ref[...] = grad
    branch_ref[...] = grad.astype(bf16)
    normed = (unit * gain).astype(bf16)
    pack = tn(high, normed) + tn(rest, normed)
    gain_row = jnp.sum(grad_normed * unit, axis=0, keepdims=True)
    at_gain = lax.broadcasted_iota(jnp.int32, pack.shape, 0) == experts
    pack_ref[...] = jnp.where(at_gain, gain_row, pack).astype(bf16)


def input_back_body(count, *refs):
    parts = refs[:count]
    res, grad_middle, gains, out_ref = refs[count:]
    grad_normed = parts[0][...].astype(f32)
    for part in parts[1:]:
        grad_normed = grad_normed + part[...].astype(f32)
    x = res[...].astype(f32)
    inverse = lax.rsqrt(jnp.mean(x * x, axis=-1, keepdims=True) + epsilon)
    unit = x * inverse
    scaled = grad_normed * gains[0:1, :]
    out_ref[...] = grad_middle[...] + inverse * (
        scaled - unit * jnp.mean(scaled * unit, axis=-1, keepdims=True)
    )


def per_device(
    residual, segments, routes, w_query, w_key, w_value, w_out, w_router, attn_gain, moe_gain,
    w_gate, w_up, w_down, cotangent,
):
    seqs, blks = lax.axis_size("seq"), lax.axis_size("blk")
    seq_me, blk_me = lax.axis_index("seq"), lax.axis_index("blk")
    toks, width = residual.shape[1], residual.shape[2]
    rows = toks * seqs
    experts = blks
    own_rows = w_query.shape[0]
    kv_local = KV_HEADS // seqs
    q_cols, kv_cols = HEADS // seqs * HEAD_DIM, kv_local * 2 * HEAD_DIM
    cols = q_cols + kv_cols
    scale = HEAD_DIM ** (-0.5)
    tokens = segments.shape[0]
    doc_most = tokens // 8
    hops = min(blks - 1, -(-(doc_most - 1) // rows))
    behind = hops * rows
    keys = behind + rows
    groups = blks // 4
    masks = gather_masks(groups)
    res = residual[0]
    cot = cotangent[0]
    vmem = pl.BlockSpec(memory_space=pltpu.VMEM)
    smem = pl.BlockSpec(memory_space=pltpu.SMEM)
    seq_scalar = jnp.reshape(seq_me, (1,)).astype(jnp.int32)
    blk_scalar = jnp.reshape(blk_me, (1,)).astype(jnp.int32)
    hbm = pl.BlockSpec(memory_space=pltpu.HBM)
    gain_row = attn_gain[None, :]

    weight_dims = (own_rows, cols + LANES + q_cols)
    sources = (w_query, w_key, w_value, w_out.T, w_router.T, gain_row, moe_gain[None, :])
    weight_parts = call(
        functools.partial(pack_body, seqs, (q_cols, kv_cols, experts)),
        tuple(shape_of(weight_dims, bf16) for _ in range(seqs)),
        in_specs=[smem] + [hbm] * 7,
        scratch_shapes=[pltpu.VMEM(a.shape, a.dtype) for a in sources] + [pltpu.SemaphoreType.DMA((7,))],
    )(seq_scalar, *[in_hbm(a) for a in sources])
    weight_both = jnp.concatenate([swap_with(p, "seq", k) for k, p in enumerate(weight_parts)], axis=0)
    weight_own = weight_both[:, : cols + LANES]
    late_res = after(res, weight_both)
    res_parts = [res] + [swap_with(late_res, "seq", k) for k in range(1, seqs)]
    weight_rel = gather_rows(weight_own)
    same_core = [[2 * i + c for i in range(blks // 2)] for c in range(2)]
    joint = seqs * own_rows * q_cols // width
    out_own = weight_both[:, cols + LANES :].reshape(seqs, own_rows, q_cols)
    out_own = jnp.concatenate([out_own[k] for k in range(seqs)], axis=1).reshape(joint, width)
    both_all = lax.all_gather(
        jnp.concatenate([cot, out_own], axis=0), "blk", axis=0, axis_index_groups=same_core
    )
    gate, up, down, *_ = lax.optimization_barrier((w_gate[0], w_up[0], w_down[0], *res_parts))
    expert_pack = jnp.concatenate([jnp.concatenate([gate, up], axis=1), down], axis=0)
    packs = [swap_with(expert_pack, "seq", k) for k in range(seqs)]
    seq_me, blk_me = after(seq_me, weight_own), after(blk_me, weight_own)

    spot = np.arange(width)
    place, inner = spot // (seqs * own_rows), spot % (seqs * own_rows)
    mask_row = jnp.asarray(np.asarray(masks)[place], jnp.int32)
    seq_row = jnp.asarray(inner // own_rows, jnp.int32)
    source = ((seq_me ^ seq_row) * blks + (blk_me ^ mask_row)) * own_rows + (inner % own_rows)
    order = (lax.broadcasted_iota(jnp.int32, (width, width), 0) == source[None, :]).astype(bf16)

    turn = lambda i: (seq_me ^ (i // toks % seqs)) * toks + i % toks
    half_dim = HEAD_DIM // 2
    lanes = lane_ids((rows, LANES))
    inverse = jnp.exp((lanes % half_dim).astype(f32) * (-2.0 * math.log(10000.0) / HEAD_DIM))
    position = blk_me * rows + turn(lax.broadcasted_iota(jnp.int32, (rows, LANES), 0))
    angles = position.astype(f32) * inverse
    cos, sin = jnp.cos(angles), jnp.where(lanes % HEAD_DIM < half_dim, -1.0, 1.0) * jnp.sin(angles)
    key_ids = jnp.arange(keys, dtype=jnp.int32)
    key_places = key_ids // rows * rows - behind + turn(key_ids % rows)
    seg_padded = jnp.concatenate([jnp.full((behind,), -1, jnp.int32), segments])
    seg_near = lax.dynamic_slice_in_dim(seg_padded, blk_me * rows, keys).reshape(hops + 1, seqs, toks)
    seg_keys = jnp.stack(
        [lax.dynamic_index_in_dim(seg_near, seq_me ^ k, 1, keepdims=False) for k in range(seqs)], axis=1
    ).reshape(keys)
    meta = jnp.concatenate(
        [seg_keys.astype(f32)[None], key_places.astype(f32)[None], jnp.zeros((6, keys), f32)], axis=0
    )

    x_rel = jnp.concatenate([nn(part, order).astype(bf16) for part in res_parts], axis=0)
    q_all, kv_own, normed_rel = call(
        functools.partial(project_body, q_cols, kv_cols, experts),
        (shape_of((rows, q_cols), bf16), shape_of((rows, kv_cols), bf16), shape_of((rows, width), bf16)),
    )(x_rel, *weight_rel, cos, sin)
    if own_rows % 16 == 0:
        qkv_abs, router_abs, gains = call(
            functools.partial(restore_body, seqs, masks, experts),
            (shape_of((width, cols), bf16), shape_of((width, LANES), bf16), shape_of((8, width), f32)),
            in_specs=[smem, smem] + [vmem] * 4,
        )(seq_scalar, blk_scalar, *weight_rel)
    else:
        weight_abs = nn(order, jnp.concatenate(weight_rel, axis=0)).astype(bf16)
        qkv_abs, router_abs = weight_abs[:, :cols], weight_abs[:, cols:]
        gains = jnp.pad(router_abs[:, experts : experts + 2].astype(f32).T, ((0, 6), (0, 0)))

    kv_keys = jnp.concatenate([shifted(kv_own, "blk", n) for n in range(hops, 0, -1)] + [kv_own], axis=0)
    step = min(rows, 256)
    grid = (kv_local, rows // step)
    row_block = pl.BlockSpec((step, LANES), lambda g, i: (i, g))
    key_block = pl.BlockSpec((keys, LANES), lambda g, i: (0, g))
    meta_q_block = pl.BlockSpec((8, step), lambda g, i: (0, behind // step + i))
    meta_k_block = pl.BlockSpec((8, keys), lambda g, i: (0, 0))
    table_block = pl.BlockSpec((step, LANES), lambda g, i: (i, 0))
    attend_limit = 8 + step * keys * 40 // 1024 // 1024
    mixed, lse = call(
        functools.partial(attend_body, scale),
        (shape_of((rows, q_cols), bf16), shape_of((rows, q_cols), f32)),
        limit=attend_limit,
        grid=grid,
        in_specs=[row_block, key_block, meta_q_block, meta_k_block],
        out_specs=(row_block, row_block),
        scratch_shapes=[pltpu.VMEM((step, keys), f32)],
    )(q_all, kv_keys, meta, meta)

    packs += [swap_with(after(p, mixed), "blk", 1) for p in packs]

    out_same = after(both_all[:, toks:], mixed)
    out_pair = [out_same, swap_with(out_same, "blk", 1)]
    if own_rows % 16 == 0:
        out_abs = call(
            functools.partial(restore_out_body, seqs, blks),
            shape_of((width, q_cols), bf16),
            in_specs=[smem, smem, hbm, hbm],
            scratch_shapes=[pltpu.SemaphoreType.DMA((blks * seqs,))],
        )(seq_scalar, blk_scalar, *[in_hbm(a) for a in out_pair])
    else:
        odd = blk_me % 2 == 1
        pair = jnp.stack([jnp.where(odd, out_pair[1 - c], out_pair[c]) for c in range(2)], axis=1)
        out_parts = pair.reshape(blks, own_rows, seqs, q_cols).swapaxes(1, 2)
        out_abs = jnp.stack(
            [lax.dynamic_index_in_dim(out_parts, seq_me ^ k, 1, keepdims=False) for k in range(seqs)]
        ).reshape(width, q_cols)

    branch = nt(mixed, out_abs)
    branch_parts = [branch[:toks]] + [
        swap_with(branch[k * toks : (k + 1) * toks].astype(bf16), "seq", k) for k in range(1, seqs)
    ]
    middle, wide, prob = call(
        functools.partial(middle_body, seqs, experts),
        (shape_of((toks, width), f32), shape_of((toks, width + LANES), bf16), shape_of((toks, LANES), f32)),
    )(*branch_parts, res, gains, router_abs, routes[0].T)

    hidden_cols = w_gate.shape[2]
    held = 2 * toks * groups
    buffers = [
        (groups, toks, width), (groups, toks, width), (held, width), (2, held, hidden_cols), (2, held, 2 * hidden_cols),
        (2, held, width),
    ]

    def run_experts(k, pieces, before):
        operands = [*pieces, both_all, *packs, *before]
        fixed = len(operands) - len(before) + 2
        return call(
            functools.partial(expert_body, experts, k, seqs),
            tuple(pltpu.HBM(d, bf16) for d in buffers) + (shape_of((2, toks, width + LANES), bf16),),
            limit=24,
            flops=48 * toks * width * hidden_cols,
            in_specs=[smem, smem] + [hbm] * len(operands),
            out_specs=(hbm,) * len(buffers) + (vmem,),
            input_output_aliases={fixed + i: i for i in range(len(before))},
            scratch_shapes=[
                pltpu.VMEM((2, toks, width + LANES), bf16),
                pltpu.VMEM((2, toks, width), bf16),
                pltpu.VMEM((2 * toks, width), bf16),
                pltpu.VMEM((2 * toks, width), bf16),
                pltpu.VMEM((2, 2 * toks, hidden_cols), bf16),
                pltpu.VMEM((2, 2 * toks, 2 * hidden_cols), bf16),
                pltpu.VMEM((2, 2 * toks, width), bf16),
                pltpu.VMEM((2, width, 2 * hidden_cols), bf16),
                pltpu.VMEM((2, hidden_cols, width), bf16),
                pltpu.SemaphoreType.DMA((9, max(4, seqs))),
            ],
        )(blk_scalar, seq_scalar, *[in_hbm(a) for a in operands])

    turns = [1, 3, 0] + [k for k in range(2, groups) if k != 3]
    far = {0: wide}
    last = wide
    for k in [t for t in turns if t]:
        far[k] = swap_with(after(wide, last), "blk", 4 * k)
        last = far[k] if k > 1 else last
    across = {k: swap_with(far[k], "blk", 2) for k in far}
    grads, nears, before = {}, {}, []
    for i, k in enumerate(turns):
        holds = [prob]
        if i > 0:
            holds.append(grads[turns[i - 1]])
        if i > 1:
            n = turns[i - 2]
            nears[n] = added(grads[n][0], swap_with(grads[n][1], "blk", 2))
            holds.append(nears[n])
        *before, grads[k] = run_experts(k, [after(far[k], *holds), across[k]], before)
    for n in turns[-2:]:
        nears[n] = added(grads[n][0], swap_with(grads[n][1], "blk", 2))
    grad_parts = [swap_with(nears[k], "blk", 4 * k) for k in turns]
    y_keep, y_send, x_all, hid_all, gg_all, geo_all = before
    tdot = lambda a, b: lax.dot_general(a, b, (((0,), (0,)), ((), ())), preferred_element_type=f32)

    grad_middle, grad_branch, pack = call(
        functools.partial(middle_back_body, groups, experts),
        (shape_of((toks, width), f32), shape_of((toks, width), bf16), shape_of((LANES, width), bf16)),
    )(*grad_parts, middle, prob, cot, gains, router_abs)

    high, low = width // seqs, hidden_cols // seqs

    x_all = after(x_all, nears[turns[-1]])
    y_far = swap_with(after(y_send, grad_branch), "blk", 2)

    def expert_grads(e, outs, *others):
        operands = [in_hbm(a) for a in (x_all, gg_all, hid_all, geo_all)]
        return call(
            functools.partial(expert_grads_body, e, seqs),
            outs,
            limit=10 + 7 * held // 1024,
            flops=6 * held * width * hidden_cols,
            in_specs=[smem] + [hbm] * 4 + [vmem] * len(others),
            scratch_shapes=[
                pltpu.VMEM((held, width), bf16), pltpu.VMEM((held, 2 * hidden_cols), bf16),
                pltpu.VMEM((held, hidden_cols), bf16), pltpu.VMEM((held, width), bf16),
                pltpu.SemaphoreType.DMA((4,)),
            ],
        )(seq_scalar, *operands, *others)

    partner_terms = expert_grads(1, shape_of((seqs, high + low, width), bf16))
    branch_others = [swap_with(grad_branch, "seq", k) for k in range(1, seqs)]
    branch_all = after(jnp.concatenate([grad_branch] + branch_others, axis=0), partner_terms)
    grad_mixed = nn(branch_all, out_abs).astype(bf16)
    block_spec = pl.BlockSpec((rows, LANES), lambda g, i: (0, g))
    gq_pre, *grad_kv = call(
        functools.partial(attend_back_body, scale),
        (shape_of((rows, q_cols), bf16),)
        + (shape_of((rows, kv_cols), bf16),) * hops
        + (shape_of((rows, kv_cols), f32),),
        limit=attend_limit,
        grid=grid,
        flops=24 * rows * keys * q_cols,
        in_specs=[row_block, key_block, row_block, row_block, row_block, meta_q_block, meta_k_block,
                  table_block, table_block],
        out_specs=(row_block,) + (block_spec,) * (hops + 1),
        scratch_shapes=[pltpu.VMEM((keys, LANES), f32), pltpu.VMEM((step, keys), f32)],
    )(q_all, kv_keys, mixed, grad_mixed, lse, meta, meta, cos, sin)
    returned = [shifted(grad_kv[hops - n], "blk", -n) for n in range(1, hops + 1)]
    spare = max(1, seqs - 1)
    gg_own, down_own, gg_sends, down_sends = expert_grads(
        0,
        (shape_of((high, 2 * hidden_cols), f32), shape_of((low, width), f32),
         shape_of((spare, high, 2 * hidden_cols), bf16), shape_of((spare, low, width), bf16)),
        after(swap_with(partner_terms, "blk", 1), gq_pre),
    )
    down_from = [swap_with(down_sends[k - 1], "seq", k) for k in range(1, seqs)]
    y_near = added(y_keep, y_far)
    branch_rel = nn(branch_all, order).astype(bf16)
    pack_rel = tdot(order, pack.T).astype(bf16)
    unit = seqs * own_rows
    q_terms = call(
        functools.partial(query_terms_body, blks),
        (shape_of((width // 2, 2 * q_cols + LANES), bf16),) * 2,
    )(normed_rel, gq_pre, branch_rel, mixed, pack_rel)

    def for_this_row(terms):
        total = sum(t.astype(f32) for t in terms).astype(bf16)
        return [swap_with(total[k * own_rows : (k + 1) * own_rows], "seq", k) for k in range(seqs)]

    q_total = scatter_core(*q_terms)
    q_stage = scatter_across(after(q_total, gg_sends, *returned))
    own_kv = after(grad_kv[-1], q_total, gg_sends)

    gkv_pre, *normed_parts = call(
        functools.partial(turn_back_body, hops, seqs),
        (shape_of((rows, kv_cols), bf16),)
        + tuple(shape_of((toks, width), bf16 if k else f32) for k in range(seqs)),
    )(own_kv, *returned, cos, sin, gq_pre, qkv_abs)
    kv_terms = call(
        functools.partial(key_terms_body, blks), (shape_of((width // 2, kv_cols), bf16),) * 2
    )(normed_rel, gkv_pre)
    q_pieces = for_this_row(scatter_far(q_stage))
    gg_from = [swap_with(gg_sends[k - 1], "seq", k) for k in range(1, seqs)]
    kv_stage = scatter_across(scatter_core(*kv_terms))
    kv_pieces = for_this_row(scatter_far(kv_stage))
    shard_query, shard_key, shard_value, shard_out, shard_router, shard_gain_one, shard_gain_two = call(
        functools.partial(finish_body, seqs, experts),
        (shape_of(w_query.shape, f32), shape_of(w_key.shape, f32), shape_of(w_value.shape, f32),
         shape_of(w_out.shape[::-1], f32), shape_of(w_router.shape[::-1], f32),
         shape_of((1, own_rows), f32), shape_of((1, own_rows), f32)),
        in_specs=[smem] + [vmem] * (2 * seqs + 4),
    )(seq_scalar, *q_pieces, *kv_pieces, w_query, w_key, w_value, gain_row)
    normed_others = [swap_with(p, "seq", k) for k, p in enumerate(normed_parts) if k]
    grad_input = call(
        functools.partial(input_back_body, seqs), shape_of((toks, width), f32)
    )(normed_parts[0], *normed_others, res, grad_middle, gains)

    for k in range(1, seqs):
        gg_own = gg_own + gg_from[k - 1].astype(f32)
        down_own = down_own + down_from[k - 1].astype(f32)
    shard_gate, shard_up = gg_own[None, :, :hidden_cols], gg_own[None, :, hidden_cols:]
    shard_down = down_own[None]

    y_sum = middle + y_near[0].astype(f32)
    for k in range(1, groups):
        y_sum = y_sum + swap_with(y_near[k], "blk", 4 * k).astype(f32)
    block_out = y_sum.astype(bf16)[None]
    return (
        block_out, grad_input[None], shard_query, shard_key, shard_value, shard_out.T, shard_router.T,
        shard_gain_one[0], shard_gain_two[0], shard_gate, shard_up, shard_down,
    )


def solution(mesh):
    both = ("seq", "blk")
    tokens, rows, cols, line = P("blk", "seq", None), P(both, None), P(None, both), P(both)
    return jax.shard_map(
        per_device,
        mesh=mesh,
        in_specs=(
            tokens, P(), tokens, rows, rows, rows, cols, rows, line, line, tokens, tokens, tokens, tokens,
        ),
        out_specs=(
            tokens, tokens, rows, rows, rows, cols, rows, line, line, tokens, tokens, tokens,
        ),
        check_vma=False,
    )
```
